32 devices in a mesh: parts: 2 (over y), gx: 4 (over z), gy: 4 (over x, core).
Axes of the slice: x: 2, y: 2, z: 4, core: 2. Of those that a mesh axis runs over, the one named last changes fastest.
Arguments:
- base_cond: float32 [3, 4, 32, 512], P(None, None, 'gx', 'gy'), may hold values from 0.5 to 2
- base_mass: float32 [4, 32, 512], P(None, 'gx', 'gy'), may hold values from 0.05 to 0.5
- fine_residual: float32 [8, 32, 512], P('parts', 'gx', 'gy'), parts along dimension 0, may hold values from -6 to 6
- point_index: int32 [2], P('parts'), parts along dimension 0, may hold values from 0 to 1048575
- gen_vector: int32 [32], replicated, may hold values from 1 to 1048575
- z_offset: int32 [1], replicated, may hold values from 0 to 508
Outputs:
- coarse_stencil: float32 [27, 4, 16, 256], P(None, 'parts', 'gx', 'gy'), parts along dimension 1
- coarse_solution: float32 [4, 16, 256], P('parts', 'gx', 'gy'), parts along dimension 0
The draws below stay inside these ranges and needn't reach their ends.
There are 2 independent parts, one for each index of `parts`. The reference program is written for one: setup_inputs(seed, part) draws one part's arguments, and reference() takes and returns one part's arrays. A program takes and returns all parts, laid end to end along the dimension named above; an argument that names none is the same for every part. Nothing has to cross between parts.
All inputs are finite; a program needn't handle non-finite values.
Results may differ from the reference program's by a relative error of at most 0.0003.
Values sent between devices are 32-bit elements; how exact they have to be, the bound alone decides.
No kernel may reach another device: no remote copies, remote signals or barrier semaphores. Data moves between devices by JAX's collectives and lax.ppermute only.
A program may use at most 128 MiB of HBM per device.

```python
import math
import jax
import jax.numpy as jnp
from jax import lax

FZ = 4
NZG = 512
MODES = 32
QMCN = 1048576
SWEEPS = 4
NX = 32
NY = 512
CZ = 2
CNX = 16
CNY = 256


def set_ends(result, key, low, top_value):
    shape = result.shape
    index_at = [jax.random.randint(jax.random.fold_in(key, axis), (), 0, shape[axis]) for axis in range(len(shape))]
    result = result.at[tuple(index_at)].set(low)
    longest = shape.index(max(shape))
    index_at[longest] = (index_at[longest] + 1) % shape[longest]
    return result.at[tuple(index_at)].set(top_value)


def shard_levels(own_key, extent, split, smallest, largest):
    def one(position, shards_of):
        draws = jax.random.uniform(jax.random.fold_in(jax.random.fold_in(own_key, 6), position), (shards_of,), jnp.float32, smallest / len(split), largest / len(split))
        return jnp.repeat(jnp.exp(draws), extent[position] // shards_of).reshape((-1,) + (1,) * (len(extent) - position - 1))

    gain = one(*split[0])
    for cut in split[1:]:
        gain = gain * one(*cut)
    return gain


def normal_values(rng, extent, scale, reach, cuts=(), kind=jnp.bfloat16):
    values = jax.random.normal(rng, extent, jnp.float32) * scale
    if len(cuts) > 0:
        values = shard_levels(rng, extent, cuts, -0.22, 0.18) * values
    return jnp.clip(values, min=-reach, max=reach).astype(kind)


def setup_inputs(seed: int = 0, part: int = 0) -> dict:
    keys = jax.random.split(jax.random.key(seed), 7)
    part_keys = jax.random.split(jax.random.fold_in(keys[6], part), 7)
    return {
        "base_cond": jnp.clip(jnp.exp(math.log(2.0) - 1.3862944 * jax.random.uniform(keys[0], (3, FZ, NX, NY), jnp.float32) ** shard_levels(keys[0], (3, FZ, NX, NY), ((2, 4), (3, 4)), -0.2, 0.2)), 0.5, 2.0),
        "base_mass": jnp.clip(jnp.exp(math.log(0.5) - 2.3025851 * jax.random.uniform(keys[1], (FZ, NX, NY), jnp.float32) ** shard_levels(keys[1], (FZ, NX, NY), ((1, 4), (2, 4)), -0.2, 0.2)), 0.05, 0.5),
        "fine_residual": normal_values(part_keys[2], (FZ, NX, NY), 1.0, 6.0, ((1, 4), (2, 4)), jnp.float32),
        "point_index": jax.random.randint(part_keys[3], (1,), 0, QMCN).astype(jnp.int32),
        "gen_vector": set_ends(jax.random.randint(keys[4], (MODES,), 1, QMCN), jax.random.fold_in(keys[4], 1), 1, QMCN - 1).astype(jnp.int32),
        "z_offset": jax.random.randint(keys[5], (1,), 0, NZG - FZ + 1).astype(jnp.int32),
    }


omega_value = 0.6


def lattice_shift(point_index, gen_vector):
    product = point_index[0] * gen_vector
    return jnp.remainder(product, QMCN).astype(jnp.float32) / QMCN - 0.5


def field_log(qmc_shift, x_glob, y_glob, z_glob, nx_total, ny_total):
    x_angle = (x_glob.astype(jnp.float32) + 0.5) * (math.pi / nx_total)
    y_angle = (y_glob.astype(jnp.float32) + 0.5) * (math.pi / ny_total)
    z_angle = (z_glob.astype(jnp.float32) + 0.5) * (math.pi / NZG)
    summed = jnp.zeros((z_glob.shape[0], x_glob.shape[0], y_glob.shape[0]), jnp.float32)
    for mode_index in range(qmc_shift.shape[0]):
        amplitude = 1.2 / (1.0 + 0.5 * mode_index)
        angle_sum = (z_angle * (mode_index % 5))[:, None, None] + (x_angle * (1 + mode_index % 4))[None, :, None]
        angle_sum = angle_sum + (y_angle * (1 + (mode_index // 4) % 4))[None, None, :] + 0.7 * mode_index
        summed = summed + (qmc_shift[mode_index] * amplitude) * jnp.cos(angle_sum)
    return summed


def effective(base_cond, base_mass, qmc_shift, x_glob, y_glob, z_local, z_base, nx_total, ny_total):
    z_glob = z_local + z_base
    log_here = field_log(qmc_shift, x_glob, y_glob, z_glob, nx_total, ny_total)
    log_east = field_log(qmc_shift, x_glob + 1, y_glob, z_glob, nx_total, ny_total)
    log_north = field_log(qmc_shift, x_glob, y_glob + 1, z_glob, nx_total, ny_total)
    log_upper = field_log(qmc_shift, x_glob, y_glob, z_glob + 1, nx_total, ny_total)
    open_x = (x_glob + 1 < nx_total)[None, :, None]
    open_y = (y_glob + 1 < ny_total)[None, None, :]
    open_z = (z_local + 1 < z_local.shape[0])[:, None, None]
    cond_x = jnp.where(open_x, base_cond[0] * jnp.exp(0.5 * (log_here + log_east)), 0.0)
    cond_y = jnp.where(open_y, base_cond[1] * jnp.exp(0.5 * (log_here + log_north)), 0.0)
    cond_z = jnp.where(open_z, base_cond[2] * jnp.exp(0.5 * (log_here + log_upper)), 0.0)
    mass_term = base_mass * jnp.exp(log_here)
    return jnp.stack([cond_x, cond_y, cond_z, mass_term]).astype(jnp.float32)


def pad_plane(values):
    return jnp.pad(values, [(0, 0)] * (values.ndim - 2) + [(1, 1), (1, 1)])


def couple(padded, cond_wide):
    cond_east = cond_wide[0, :, 1:-1, 1:-1]
    cond_west = cond_wide[0, :, :-2, 1:-1]
    cond_north = cond_wide[1, :, 1:-1, 1:-1]
    cond_south = cond_wide[1, :, 1:-1, :-2]
    cond_upper = cond_wide[2, :, 1:-1, 1:-1]
    cond_lower = jnp.pad(cond_upper, ((1, 0), (0, 0), (0, 0)))[:-1]
    middle = padded[..., 1:-1, 1:-1]
    lead = [(0, 0)] * (middle.ndim - 3)
    below = jnp.pad(middle, lead + [(1, 0), (0, 0), (0, 0)])[..., :-1, :, :]
    above = jnp.pad(middle, lead + [(0, 1), (0, 0), (0, 0)])[..., 1:, :, :]
    summed = cond_west * padded[..., :-2, 1:-1] + cond_east * padded[..., 2:, 1:-1]
    summed = summed + cond_south * padded[..., 1:-1, :-2] + cond_north * padded[..., 1:-1, 2:]
    return summed + cond_lower * below + cond_upper * above


def weights(cond_wide, x_glob, y_glob, z_local, nx_total, ny_total):
    cond_east = cond_wide[0, :, 1:-1, 1:-1]
    cond_west = cond_wide[0, :, :-2, 1:-1]
    cond_north = cond_wide[1, :, 1:-1, 1:-1]
    cond_south = cond_wide[1, :, 1:-1, :-2]
    cond_upper = cond_wide[2, :, 1:-1, 1:-1]
    cond_lower = jnp.pad(cond_upper, ((1, 0), (0, 0), (0, 0)))[:-1]
    mass_term = cond_wide[3, :, 1:-1, 1:-1]
    odd_x = (x_glob % 2 == 1)[None, :, None]
    odd_y = (y_glob % 2 == 1)[None, None, :]
    odd_z = (z_local % 2 == 1)[:, None, None]
    inside = ((x_glob >= 0) & (x_glob < nx_total))[None, :, None] & ((y_glob >= 0) & (y_glob < ny_total))[None, None, :]
    pair_x = cond_east + cond_west
    pair_y = cond_north + cond_south
    pair_z = cond_upper + cond_lower
    denominator = mass_term + jnp.where(odd_x, pair_x, 0.0) + jnp.where(odd_y, pair_y, 0.0) + jnp.where(odd_z, pair_z, 0.0)
    reciprocal = jnp.where(inside, 1.0 / jnp.where(inside, denominator, 1.0), 0.0)
    odd_count = odd_x.astype(jnp.int32) + odd_y.astype(jnp.int32) + odd_z.astype(jnp.int32)
    weight_one = jnp.where(odd_count == 1, reciprocal, 0.0)
    weight_two = jnp.where(odd_count == 2, reciprocal, 0.0)
    weight_three = jnp.where(odd_count == 3, reciprocal, 0.0)
    diagonal = mass_term + pair_x + pair_y + pair_z
    return weight_one, weight_two, weight_three, diagonal


def prolong_apply(seed_wide, cond_wide, weight_one, weight_two, weight_three, diagonal, spread):
    level_zero = seed_wide[..., 1:-1, 1:-1]
    level_one = level_zero + weight_one * couple(seed_wide, cond_wide)
    level_two = level_one + weight_two * couple(spread(level_one), cond_wide)
    level_three = level_two + weight_three * couple(spread(level_two), cond_wide)
    return diagonal * level_three - couple(spread(level_three), cond_wide)


def restrict(applied, cond_wide, weight_one, weight_two, weight_three, spread):
    applied = applied + couple(spread(weight_three * applied), cond_wide)
    applied = applied + couple(spread(weight_two * applied), cond_wide)
    return applied + couple(spread(weight_one * applied), cond_wide)


def colour_table(coords, upper_limit):
    usable = (coords % 2 == 0) & (coords >= 0) & (coords < upper_limit)
    colour_of = (coords // 2) % 3
    return jnp.stack([jnp.where(usable & (colour_of == colour), 1.0, 0.0) for colour in range(3)]).astype(jnp.float32)


def offset_table(coords):
    return jnp.stack([jnp.stack([jnp.where((coords + offset - 1) % 3 == colour, 1.0, 0.0) for colour in range(3)]) for offset in range(3)]).astype(jnp.float32)


def select_offsets(probes, q_z, q_x, q_y):
    table_z = offset_table(q_z)
    table_x = offset_table(q_x)
    table_y = offset_table(q_y)
    plane_count, size_x, size_y = probes.shape[1:]
    grouped = probes.reshape(3, 3, 3, plane_count, size_x, size_y)
    section_one = jnp.sum(table_z[:, :, None, None, :, None, None] * grouped[None], axis=1)
    section_two = jnp.sum(table_x[None, :, :, None, None, :, None] * section_one[:, None], axis=2)
    section_three = jnp.sum(table_y[None, None, :, :, None, None, :] * section_two[:, :, None], axis=3)
    return section_three.reshape(27, plane_count, size_x, size_y)


def apply_coarse(stencil, padded):
    plane_count, size_x, size_y = stencil.shape[1:]
    deep_pad = jnp.pad(padded, ((1, 1), (0, 0), (0, 0)))
    summed = jnp.zeros((plane_count, size_x, size_y), jnp.float32)
    for offset_z in range(3):
        for offset_x in range(3):
            for offset_y in range(3):
                summed = summed + stencil[9 * offset_z + 3 * offset_x + offset_y] * deep_pad[offset_z:offset_z + plane_count, offset_x:offset_x + size_x, offset_y:offset_y + size_y]
    return summed


def jacobi(stencil, coarse_rhs, diag_safe, spread):
    solution = omega_value * coarse_rhs / diag_safe
    for sweep_index in range(SWEEPS - 1):
        solution = solution + omega_value * (coarse_rhs - apply_coarse(stencil, spread(solution))) / diag_safe
    return solution


def reference(base_cond, base_mass, fine_residual, point_index, gen_vector, z_offset):
    qmc_shift = lattice_shift(point_index, gen_vector)
    x_glob = jnp.arange(NX, dtype=jnp.int32)
    y_glob = jnp.arange(NY, dtype=jnp.int32)
    z_local = jnp.arange(FZ, dtype=jnp.int32)
    coeffs = effective(base_cond, base_mass, qmc_shift, x_glob, y_glob, z_local, z_offset[0], NX, NY)
    cond_wide = pad_plane(coeffs)
    weight_one, weight_two, weight_three, diagonal = weights(cond_wide, x_glob, y_glob, z_local, NX, NY)
    table_z = colour_table(z_local, FZ)
    table_x = colour_table(jnp.arange(-1, NX + 1, dtype=jnp.int32), NX)
    table_y = colour_table(jnp.arange(-1, NY + 1, dtype=jnp.int32), NY)

    def one_probe(colour_index):
        seed_wide = table_z[colour_index // 9][:, None, None] * table_x[(colour_index // 3) % 3][None, :, None] * table_y[colour_index % 3][None, None, :]
        applied = prolong_apply(seed_wide, cond_wide, weight_one, weight_two, weight_three, diagonal, pad_plane)
        restricted = restrict(applied, cond_wide, weight_one, weight_two, weight_three, pad_plane)
        return restricted[::2, ::2, ::2]

    probes = lax.map(one_probe, jnp.arange(27, dtype=jnp.int32))
    coarse_rhs = restrict(fine_residual, cond_wide, weight_one, weight_two, weight_three, pad_plane)[::2, ::2, ::2]
    stencil = select_offsets(probes, jnp.arange(CZ, dtype=jnp.int32), jnp.arange(CNX, dtype=jnp.int32), jnp.arange(CNY, dtype=jnp.int32))
    solution = jacobi(stencil, coarse_rhs, stencil[13], pad_plane)
    return stencil, solution
```

```python
import math

import jax
import jax.numpy as jnp
from jax import lax
from jax.experimental import pallas as pl
from jax.experimental.pallas import tpu as pltpu
from jax.sharding import PartitionSpec as P

NZG = 512
QMCN = 1048576
SWEEPS = 4
OMEGA = 0.6
ROWS = 16
LANES = 128
HALO = 8
F32 = jnp.float32
BF16 = jnp.bfloat16


def iota(shape, dim):
    return lax.broadcasted_iota(jnp.int32, shape, dim)


def strips_body(cond_ref, mass_ref, resid_ref, low_ref, high_ref):
    width = cond_ref.shape[-1]
    row, lane = iota((HALO, width), 0), iota((HALO, width), 1)
    coeffs = jnp.concatenate([cond_ref[...].reshape(-1, width), mass_ref[...].reshape(-1, width)], 0)
    resid = resid_ref[...].reshape(-1, width)
    for out_ref, first in ((low_ref, 0), (high_ref, width - HALO)):
        pick = jnp.where(lane == row + first, 1.0, 0.0)
        for start, rows in ((0, coeffs), (HALO, resid)):
            taken = lax.dot_general(
                pick, rows, (((1,), (1,)), ((), ())), precision=lax.Precision.HIGHEST, preferred_element_type=F32
            )
            if rows.shape[0] < LANES:
                taken = jnp.concatenate([taken, jnp.zeros((HALO, LANES - rows.shape[0]), F32)], 1)
            out_ref[start : start + HALO, :] = taken


def field_body(nx_total, ny_total, width_x, width_y, point_ref, offset_ref, gen_ref, out_ref):
    modes = gen_ref.shape[1]
    x_first = lax.axis_index("gx") * width_x
    y_first = lax.axis_index("gy") * width_y
    half_x, half_y = width_x // 2, width_y // 2
    product = point_ref[0] * gen_ref[...]
    shift = (product & (QMCN - 1)).astype(F32) / QMCN - 0.5
    mode_row = iota((modes, modes), 0)
    mode_col = jnp.sum(jnp.where(mode_row == iota((modes, modes), 1), shift, 0.0), axis=1, keepdims=True)
    k = iota((modes, LANES), 0)
    lane = iota((modes, LANES), 1)
    k_f = k.astype(F32)
    amplitude = 1.2 / (1.0 + 0.5 * k_f) * mode_col
    z_local = lane // (2 * ROWS)
    px = (lane // ROWS) % 2
    r = lane % ROWS
    coarse_x = jnp.where(r < 8, r, r - ROWS)
    x = x_first + 2 * coarse_x + px
    x_angle = (x.astype(F32) + 0.5) * (math.pi / nx_total)
    z_angle = ((z_local + offset_ref[0]).astype(F32) + 0.5) * (math.pi / NZG)
    phase = z_angle * (k % 5).astype(F32) + x_angle * (1 + k % 4).astype(F32) + 0.7 * k_f
    x_ok = (r < 8) | (r >= 12)
    ones = jnp.where(x_ok & (x >= 0) & (x < nx_total), 1.0, 0.0)
    left = jnp.concatenate([amplitude * jnp.cos(phase), -amplitude * jnp.sin(phase)], 0)
    inside_x = lax.dot_general(ones, jnp.ones((modes, LANES), F32), (((0,), (0,)), ((), ())), preferred_element_type=F32)
    y_mode = (1 + (k // 4) % 4).astype(F32)
    for py in range(2):
        coarse_y = jnp.where(lane < half_y + 4, lane, lane - LANES)
        y = y_first + 2 * coarse_y + py
        y_angle = (y.astype(F32) + 0.5) * (math.pi / ny_total) * y_mode
        right = jnp.concatenate([jnp.cos(y_angle), jnp.sin(y_angle)], 0)
        log_kappa = lax.dot_general(
            left, right, (((0,), (0,)), ((), ())), precision=lax.Precision.HIGHEST, preferred_element_type=F32
        )
        y_full = y[0:1, :]
        lane_full = lane[0:1, :]
        y_ok = (lane_full < half_y + 4) | (lane_full >= LANES - 4)
        y_ok = y_ok & (y_full >= 0) & (y_full < ny_total)
        value = jnp.where((inside_x > 0.5) & y_ok, jnp.exp(0.5 * log_kappa), 0.0)
        for group in range(8):
            out_ref[group // 2, group % 2, py] = value[group * ROWS : (group + 1) * ROWS]


def select_columns(width):
    half = width // 2
    column = iota((width, 2 * LANES), 1)
    own = iota((width, 2 * LANES), 0)
    parity, k = column // LANES, column % LANES
    pick_own = jnp.where((k < half) & (own == 2 * k + parity), 1.0, 0.0).astype(BF16)
    strip = iota((2 * HALO, 2 * LANES), 0)
    column = iota((2 * HALO, 2 * LANES), 1)
    parity, k = column // LANES, column % LANES
    k = jnp.where(k >= LANES - 4, k - LANES, k)
    fine = jnp.where(strip < HALO, strip - HALO, strip - HALO + width)
    wanted = ((k < 0) | (k >= half)) & (k < half + 4)
    pick_strip = jnp.where(wanted & (fine == 2 * k + parity), 1.0, 0.0).astype(BF16)
    return pick_own, pick_strip


def exact_pick(values, pick, dims):
    total = None
    rest = values
    for _ in range(3):
        part = rest.astype(BF16)
        rest = rest - part.astype(F32)
        term = lax.dot_general(part, pick, (dims, ((), ())), preferred_element_type=F32)
        total = term if total is None else total + term
    return total


class Lazy:
    def __init__(self, rule):
        self.rule, self.known = rule, {}

    def __call__(self, *key):
        if key not in self.known:
            self.known[key] = self.rule(*key)
        return self.known[key]


def plus(*terms):
    total = None
    for term in terms:
        if term is not None:
            total = term if total is None else total + term
    return total


def times(left, right):
    return None if left is None or right is None else left * right


def minus(left, right):
    if right is None:
        return left
    return -right if left is None else left - right


def shift_x(value, steps):
    return None if value is None else pltpu.roll(value, (-steps) % ROWS, 0)


def shift_y(value, steps):
    return None if value is None else pltpu.roll(value, (-steps) % LANES, 1)


def main_body(field_ref, own_ref, near_ref, far_ref, stencil_ref, solution_ref, wide_ref):
    width_y = own_ref.shape[1]
    n_rows = own_ref.shape[0] - 4 * HALO
    groups = n_rows // HALO
    pick_own, pick_strip = select_columns(width_y)
    even_block = lax.axis_index("gx") % 2 == 0
    near, far = near_ref[...], far_ref[...]
    blocks = (own_ref[...], jnp.where(even_block, near, far), jnp.where(even_block, far, near))
    for g in range(groups):
        for py in range(2):
            wide_ref[g, py, 16:24, :] = jnp.zeros((8, LANES), F32)
    for block, place in zip(blocks, (0, 8, 24)):
        spread = exact_pick(block[:n_rows], pick_own, ((1,), (0,)))
        strips = jnp.concatenate([block[n_rows : n_rows + HALO], block[n_rows + 2 * HALO : n_rows + 3 * HALO]], 0)
        rest = jnp.concatenate([block[n_rows + HALO : n_rows + 2 * HALO], block[n_rows + 3 * HALO :]], 0)
        border = jnp.concatenate(
            [exact_pick(strips, pick_strip, ((0,), (0,))), exact_pick(rest, pick_strip, ((0,), (0,)))[: n_rows - LANES]], 0
        )
        spread = spread + border
        for g in range(groups):
            for py in range(2):
                wide_ref[g, py, place : place + 8, :] = spread[8 * g : 8 * g + 8, LANES * py : LANES * (py + 1)]

    planes = 2

    def base(kind, z, px, py):
        return wide_ref[4 * kind + z, py, pl.ds(px, ROWS, stride=2), :]

    s = Lazy(lambda z, px, py: field_ref[z, px, py])

    def face(axis, z, px, py):
        here = s(z, px, py)
        if axis == "x":
            there = s(z, 1, py) if px == 0 else shift_x(s(z, 0, py), 1)
            return base(0, z, px, py) * (here * there)
        if axis == "y":
            there = s(z, px, 1) if py == 0 else shift_y(s(z, px, 0), 1)
            return base(1, z, px, py) * (here * there)
        if z < 0 or z + 1 >= 2 * planes:
            return None
        return base(2, z, px, py) * (here * s(z + 1, px, py))

    face = Lazy(face)
    mass = Lazy(lambda z, px, py: base(3, z, px, py) * (s(z, px, py) * s(z, px, py)))

    def pair(axis, z, px, py):
        if axis == "x":
            lower = face("x", z, 0, py) if px else shift_x(face("x", z, 1, py), -1)
        elif axis == "y":
            lower = face("y", z, px, 0) if py else shift_y(face("y", z, px, 1), -1)
        else:
            lower = face("z", z - 1, px, py)
        return plus(face(axis, z, px, py), lower)

    pair = Lazy(pair)

    def inverse(z, px, py):
        total = mass(z, px, py)
        for axis, odd in (("x", px), ("y", py), ("z", z % 2)):
            if odd:
                total = total + pair(axis, z, px, py)
        return 1.0 / jnp.where(s(z, px, py) > 0.0, total, 1.0)

    inverse = Lazy(inverse)

    def w_x(i, a):
        return None if not 0 <= i < planes else inverse(2 * i, 1, 0) * face("x", 2 * i, a, 0)

    def w_y(i, b):
        return None if not 0 <= i < planes else inverse(2 * i, 0, 1) * face("y", 2 * i, 0, b)

    def w_z(i, c):
        return times(inverse(2 * i + 1, 0, 0), face("z", 2 * i + c, 0, 0))

    w_x, w_y, w_z = Lazy(w_x), Lazy(w_y), Lazy(w_z)
    w_x_up = Lazy(lambda i, a: shift_y(w_x(i, a), 1))
    w_y_up = Lazy(lambda i, b: shift_x(w_y(i, b), 1))
    w_z_upx = Lazy(lambda i, c: shift_x(w_z(i, c), 1))
    w_z_upy = Lazy(lambda i, c: shift_y(w_z(i, c), 1))

    def w_xy(i, a, b):
        if not 0 <= i < planes:
            return None
        z = 2 * i
        return inverse(z, 1, 1) * (
            face("x", z, a, 1) * (w_y_up(i, b) if a else w_y(i, b)) + face("y", z, 1, b) * (w_x_up(i, a) if b else w_x(i, a))
        )

    def w_xz(i, a, c):
        z = 2 * i + 1
        return times(
            inverse(z, 1, 0),
            plus(times(face("x", z, a, 0), w_z_upx(i, c) if a else w_z(i, c)), times(face("z", 2 * i + c, 1, 0), w_x(i + c, a))),
        )

    def w_yz(i, b, c):
        z = 2 * i + 1
        return times(
            inverse(z, 0, 1),
            plus(times(face("y", z, 0, b), w_z_upy(i, c) if b else w_z(i, c)), times(face("z", 2 * i + c, 0, 1), w_y(i + c, b))),
        )

    w_xy, w_xz, w_yz = Lazy(w_xy), Lazy(w_xz), Lazy(w_yz)
    w_yz_up = Lazy(lambda i, b, c: shift_x(w_yz(i, b, c), 1))
    w_xz_up = Lazy(lambda i, a, c: shift_y(w_xz(i, a, c), 1))

    def w_xyz(i, a, b, c):
        z = 2 * i + 1
        if not 0 <= i < planes or not 0 <= i + c < planes:
            return None
        return inverse(z, 1, 1) * (
            face("x", z, a, 1) * (w_yz_up(i, b, c) if a else w_yz(i, b, c))
            + face("y", z, 1, b) * (w_xz_up(i, a, c) if b else w_xz(i, a, c))
            + face("z", 2 * i + c, 1, 1) * w_xy(i + c, a, b)
        )

    w_xyz = Lazy(w_xyz)

    low_x = Lazy(lambda i, b, c, a: shift_x(times(face("x", 2 * i + 1, 1, 1), w_xyz(i, a, b, c)), -1))
    low_y = Lazy(lambda i, a, c, b: shift_y(times(face("y", 2 * i + 1, 1, 1), w_xyz(i, a, b, c)), -1))

    def t_xy(i, a, b, dz):
        z = 2 * i
        row = None
        if dz == 0:
            row = times(pair("z", z, 1, 1), w_xy(i, a, b))
        if dz >= 0:
            row = minus(row, times(face("z", z, 1, 1), w_xyz(i, a, b, dz)))
        if dz <= 0:
            row = minus(row, times(face("z", z - 1, 1, 1), w_xyz(i - 1, a, b, dz + 1)))
        return minus(w_xy(i, a, b) if dz == 0 else None, times(inverse(z, 1, 1), row))

    def t_xz(i, a, c, dy):
        z = 2 * i + 1
        if not 0 <= i < planes or not 0 <= i + c < planes:
            return None
        row = None
        if dy == 0:
            row = times(pair("y", z, 1, 0), w_xz(i, a, c))
        if dy >= 0:
            row = minus(row, times(face("y", z, 1, 0), w_xyz(i, a, dy, c)))
        if dy <= 0:
            row = minus(row, low_y(i, a, c, dy + 1))
        return minus(w_xz(i, a, c) if dy == 0 else None, times(inverse(z, 1, 0), row))

    def t_yz(i, b, c, dx):
        z = 2 * i + 1
        if not 0 <= i < planes or not 0 <= i + c < planes:
            return None
        row = None
        if dx == 0:
            row = times(pair("x", z, 0, 1), w_yz(i, b, c))
        if dx >= 0:
            row = minus(row, times(face("x", z, 0, 1), w_xyz(i, dx, b, c)))
        if dx <= 0:
            row = minus(row, low_x(i, b, c, dx + 1))
        return minus(w_yz(i, b, c) if dx == 0 else None, times(inverse(z, 0, 1), row))

    t_xy, t_xz, t_yz = Lazy(t_xy), Lazy(t_xz), Lazy(t_yz)

    def t_x(i, a, dy, dz):
        z = 2 * i
        row = None
        if dy == 0 and dz == 0:
            row = plus(pair("y", z, 1, 0), pair("z", z, 1, 0)) * w_x(i, a)
        if dy >= 0:
            row = minus(row, times(face("y", z, 1, 0), t_xy(i, a, dy, dz)))
        if dy <= 0:
            row = minus(row, shift_y(times(face("y", z, 1, 1), t_xy(i, a, dy + 1, dz)), -1))
        if dz >= 0:
            row = minus(row, times(face("z", z, 1, 0), t_xz(i, a, dz, dy)))
        if dz <= 0:
            row = minus(row, times(face("z", z - 1, 1, 0), t_xz(i - 1, a, dz + 1, dy)))
        return minus(w_x(i, a) if dy == 0 and dz == 0 else None, times(inverse(z, 1, 0), row))

    def t_y(i, b, dx, dz):
        z = 2 * i
        row = None
        if dx == 0 and dz == 0:
            row = plus(pair("x", z, 0, 1), pair("z", z, 0, 1)) * w_y(i, b)
        if dx >= 0:
            row = minus(row, times(face("x", z, 0, 1), t_xy(i, dx, b, dz)))
        if dx <= 0:
            row = minus(row, shift_x(times(face("x", z, 1, 1), t_xy(i, dx + 1, b, dz)), -1))
        if dz >= 0:
            row = minus(row, times(face("z", z, 0, 1), t_yz(i, b, dz, dx)))
        if dz <= 0:
            row = minus(row, times(face("z", z - 1, 0, 1), t_yz(i - 1, b, dz + 1, dx)))
        return minus(w_y(i, b) if dx == 0 and dz == 0 else None, times(inverse(z, 0, 1), row))

    def t_z(i, c, dx, dy):
        z = 2 * i + 1
        if not 0 <= i < planes or not 0 <= i + c < planes:
            return None
        row = None
        if dx == 0 and dy == 0:
            row = plus(pair("x", z, 0, 0), pair("y", z, 0, 0)) * w_z(i, c)
        if dx >= 0:
            row = minus(row, times(face("x", z, 0, 0), t_xz(i, dx, c, dy)))
        if dx <= 0:
            row = minus(row, shift_x(times(face("x", z, 1, 0), t_xz(i, dx + 1, c, dy)), -1))
        if dy >= 0:
            row = minus(row, times(face("y", z, 0, 0), t_yz(i, dy, c, dx)))
        if dy <= 0:
            row = minus(row, shift_y(times(face("y", z, 0, 1), t_yz(i, dy + 1, c, dx)), -1))
        return minus(w_z(i, c) if dx == 0 and dy == 0 else None, times(inverse(z, 0, 0), row))

    t_x, t_y, t_z = Lazy(t_x), Lazy(t_y), Lazy(t_z)

    def direct(i, dz, dx, dy):
        z = 2 * i
        row = None
        if dx == 0 and dy == 0 and dz == 0:
            row = plus(mass(z, 0, 0), pair("x", z, 0, 0), pair("y", z, 0, 0), pair("z", z, 0, 0))
        if dx >= 0:
            row = minus(row, times(face("x", z, 0, 0), t_x(i, dx, dy, dz)))
        if dx <= 0:
            row = minus(row, shift_x(times(face("x", z, 1, 0), t_x(i, dx + 1, dy, dz)), -1))
        if dy >= 0:
            row = minus(row, times(face("y", z, 0, 0), t_y(i, dy, dx, dz)))
        if dy <= 0:
            row = minus(row, shift_y(times(face("y", z, 0, 1), t_y(i, dy + 1, dx, dz)), -1))
        if dz >= 0:
            row = minus(row, times(face("z", z, 0, 0), t_z(i, dz, dx, dy)))
        if dz <= 0:
            row = minus(row, times(face("z", z - 1, 0, 0), t_z(i - 1, dz + 1, dx, dy)))
        return row

    def coarse(i, dz, dx, dy):
        if not 0 <= i + dz < planes:
            return None
        if (dz, dx, dy) >= (0, 0, 0):
            return direct(i, dz, dx, dy)
        return shift_y(shift_x(coarse(i + dz, -dz, -dx, -dy), dx), dy)

    coarse = Lazy(coarse)

    resid = Lazy(lambda z, px, py: base(4, z, px, py))
    odd_z = range(planes)
    q_xyz = [inverse(2 * i + 1, 1, 1) * resid(2 * i + 1, 1, 1) for i in odd_z] + [None]
    q_xy, q_xz, q_yz, q_x, q_y, q_z, rhs = [], [], [], [], [], [], []

    def side_x(z, py, value):
        return plus(times(face("x", z, 0, py), value), shift_x(times(face("x", z, 1, py), value), -1))

    def side_y(z, px, value):
        return plus(times(face("y", z, px, 0), value), shift_y(times(face("y", z, px, 1), value), -1))

    def side_z(z, px, py, values):
        i = z // 2
        return plus(times(face("z", z, px, py), values[i]), times(face("z", z - 1, px, py), values[i - 1] if i else None))

    for i in range(planes):
        z = 2 * i
        q_xy.append(inverse(z, 1, 1) * plus(resid(z, 1, 1), side_z(z, 1, 1, q_xyz)))
        q_xz.append(inverse(z + 1, 1, 0) * plus(resid(z + 1, 1, 0), side_y(z + 1, 1, q_xyz[i])))
        q_yz.append(inverse(z + 1, 0, 1) * plus(resid(z + 1, 0, 1), side_x(z + 1, 1, q_xyz[i])))
    for i in range(planes):
        z = 2 * i
        q_x.append(inverse(z, 1, 0) * plus(resid(z, 1, 0), side_y(z, 1, q_xy[i]), side_z(z, 1, 0, q_xz)))
        q_y.append(inverse(z, 0, 1) * plus(resid(z, 0, 1), side_x(z, 1, q_xy[i]), side_z(z, 0, 1, q_yz)))
        q_z.append(
            inverse(z + 1, 0, 0) * plus(resid(z + 1, 0, 0), side_x(z + 1, 0, q_xz[i]), side_y(z + 1, 0, q_yz[i]))
        )
    for i in range(planes):
        z = 2 * i
        rhs.append(plus(resid(z, 0, 0), side_x(z, 0, q_x[i]), side_y(z, 0, q_y[i]), side_z(z, 0, 0, q_z)))

    keep_x, keep_y = stencil_ref.shape[2:]
    for i in range(planes):
        for dz in (-1, 0, 1):
            for dx in (-1, 0, 1):
                for dy in (-1, 0, 1):
                    value = coarse(i, dz, dx, dy)
                    number = 9 * (dz + 1) + 3 * (dx + 1) + dy + 1
                    if value is None:
                        stencil_ref[number, i] = jnp.zeros((keep_x, keep_y), F32)
                    else:
                        stencil_ref[number, i] = value[:keep_x, :keep_y]

    scaled = []
    for i in range(planes):
        inside = s(2 * i, 0, 0) > 0.0
        scaled.append(jnp.where(inside, OMEGA / jnp.where(inside, coarse(i, 0, 0, 0), 1.0), 0.0))
    u = [scaled[i] * rhs[i] for i in range(planes)]
    for _ in range(SWEEPS - 1):
        moved = {}
        for i in range(planes):
            for dx in (-1, 0, 1):
                row = shift_x(u[i], dx) if dx else u[i]
                for dy in (-1, 0, 1):
                    moved[i, dx, dy] = shift_y(row, dy) if dy else row
        new = []
        for i in range(planes):
            total = None
            for dz in (-1, 0, 1):
                for dx in (-1, 0, 1):
                    for dy in (-1, 0, 1):
                        total = plus(total, times(coarse(i, dz, dx, dy), moved.get((i + dz, dx, dy))))
            new.append(u[i] + scaled[i] * (rhs[i] - total))
        u = new
    for i in range(planes):
        solution_ref[i] = u[i][:keep_x, :keep_y]


def ring(value, axis, steps):
    count = lax.axis_size(axis)
    return lax.ppermute(value, axis, [(i, (i + steps) % count) for i in range(count)])


def swap(value, axis, first):
    count = lax.axis_size(axis)
    partner = list(range(count))
    for i in range(first, count - 1, 2):
        partner[i], partner[i + 1] = i + 1, i
    return lax.ppermute(value, axis, list(enumerate(partner)))


def on_device(base_cond, base_mass, fine_residual, point_index, gen_vector, z_offset):
    plane_count, width_x, width_y = base_mass.shape
    nx_total = width_x * lax.axis_size("gx")
    ny_total = width_y * lax.axis_size("gy")
    strip = jax.ShapeDtypeStruct((2 * HALO, LANES), F32)
    low, high = pl.pallas_call(strips_body, out_shape=(strip, strip), name="strips")(base_cond, base_mass, fine_residual)
    from_below = ring(high, "gy", 1)
    from_above = ring(low, "gy", -1)
    smem = pl.BlockSpec(memory_space=pltpu.SMEM)
    vmem = pl.BlockSpec(memory_space=pltpu.VMEM)
    field = pl.pallas_call(
        lambda *refs: field_body(nx_total, ny_total, width_x, width_y, *refs),
        out_shape=jax.ShapeDtypeStruct((plane_count, 2, 2, ROWS, LANES), F32),
        in_specs=[smem, smem, vmem],
        out_specs=vmem,
        name="field",
    )(point_index, z_offset, gen_vector.reshape(1, -1))
    own = jnp.concatenate(
        [
            base_cond.reshape(-1, width_y),
            base_mass.reshape(-1, width_y),
            fine_residual.reshape(-1, width_y),
            from_below,
            from_above,
        ],
        0,
    )
    far = swap(own, "gx", 1)
    near = swap(own, "gx", 0)
    groups = 5 * plane_count
    return pl.pallas_call(
        main_body,
        out_shape=(
            jax.ShapeDtypeStruct((27, plane_count // 2, width_x // 2, width_y // 2), F32),
            jax.ShapeDtypeStruct((plane_count // 2, width_x // 2, width_y // 2), F32),
        ),
        scratch_shapes=[pltpu.VMEM((groups, 2, 2 * ROWS, LANES), F32)],
        name="galerkin",
    )(field, own, near, far)


def solution(mesh):
    return jax.shard_map(
        on_device,
        mesh=mesh,
        in_specs=(
            P(None, None, "gx", "gy"),
            P(None, "gx", "gy"),
            P("parts", "gx", "gy"),
            P("parts"),
            P(),
            P(),
        ),
        out_specs=(P(None, "parts", "gx", "gy"), P("parts", "gx", "gy")),
        check_vma=False,
    )
```

```python
import math

import jax
import jax.numpy as jnp
from jax import lax
from jax.experimental import pallas as pl
from jax.experimental.pallas import tpu as pltpu
from jax.sharding import PartitionSpec as P

NZG = 512
QMCN = 1048576
SWEEPS = 4
OMEGA = 0.6
ROWS = 16
LANES = 128
HALO = 8
F32 = jnp.float32
BF16 = jnp.bfloat16


def iota(shape, dim):
    return lax.broadcasted_iota(jnp.int32, shape, dim)


def strips_body(cond_hbm, mass_hbm, resid_hbm, own_ref, near_ref, far_ref, sems):
    width = own_ref.shape[-1]
    planes = mass_hbm.shape[0]
    sources = [cond_hbm.at[axis] for axis in range(3)] + [mass_hbm, resid_hbm]
    copies = [
        pltpu.make_async_copy(source, own_ref.at[number * planes : (number + 1) * planes], sems.at[number])
        for number, source in enumerate(sources)
    ]
    for copy in copies:
        copy.start()
    even = lax.axis_index("gy") % 2 == 0
    row, lane = iota((HALO, width), 0), iota((HALO, width), 1)
    last = width - HALO
    picks = [jnp.where(lane == row + first, 1.0, 0.0) for first in (jnp.where(even, last, 0), jnp.where(even, 0, last))]
    for copy in copies:
        copy.wait()
    groups = LANES // HALO
    coeffs = own_ref[:groups].reshape(LANES, width)
    resid = own_ref[groups : 5 * planes].reshape(-1, width)
    for out_ref, pick in ((near_ref, picks[0]), (far_ref, picks[1])):
        for start, rows in ((0, coeffs), (1, resid)):
            taken = lax.dot_general(
                pick, rows, (((1,), (1,)), ((), ())), precision=lax.Precision.HIGHEST, preferred_element_type=F32
            )
            if rows.shape[0] < LANES:
                taken = jnp.concatenate([taken, jnp.zeros((HALO, LANES - rows.shape[0]), F32)], 1)
            out_ref[start] = taken


def field_body(nx_total, ny_total, width_x, width_y, point_ref, offset_ref, gen_ref, out_ref):
    modes = gen_ref.shape[1]
    x_first = lax.axis_index("gx") * width_x
    y_first = lax.axis_index("gy") * width_y
    half_x, half_y = width_x // 2, width_y // 2
    product = point_ref[0] * gen_ref[...]
    shift = (product & (QMCN - 1)).astype(F32) / QMCN - 0.5
    mode_row = iota((modes, modes), 0)
    mode_col = jnp.sum(jnp.where(mode_row == iota((modes, modes), 1), shift, 0.0), axis=1, keepdims=True)
    k = iota((modes, LANES), 0)
    lane = iota((modes, LANES), 1)
    k_f = k.astype(F32)
    amplitude = 1.2 / (1.0 + 0.5 * k_f) * mode_col
    z_local = lane // (2 * ROWS)
    px = (lane // ROWS) % 2
    r = lane % ROWS
    coarse_x = jnp.where(r < 8, r, r - ROWS)
    x = x_first + 2 * coarse_x + px
    x_angle = (x.astype(F32) + 0.5) * (math.pi / nx_total)
    z_angle = ((z_local + offset_ref[0]).astype(F32) + 0.5) * (math.pi / NZG)
    phase = z_angle * (k % 5).astype(F32) + x_angle * (1 + k % 4).astype(F32) + 0.7 * k_f
    x_ok = (r < 8) | (r >= 12)
    ones = jnp.where(x_ok & (x >= 0) & (x < nx_total), 1.0, 0.0)
    left = jnp.concatenate([amplitude * jnp.cos(phase), -amplitude * jnp.sin(phase)], 0)
    inside_x = lax.dot_general(ones, jnp.ones((modes, LANES), F32), (((0,), (0,)), ((), ())), preferred_element_type=F32)
    y_mode = (1 + (k // 4) % 4).astype(F32)
    for py in range(2):
        coarse_y = jnp.where(lane < half_y + 4, lane, lane - LANES)
        y = y_first + 2 * coarse_y + py
        y_angle = (y.astype(F32) + 0.5) * (math.pi / ny_total) * y_mode
        right = jnp.concatenate([jnp.cos(y_angle), jnp.sin(y_angle)], 0)
        log_kappa = lax.dot_general(
            left, right, (((0,), (0,)), ((), ())), precision=lax.Precision.HIGHEST, preferred_element_type=F32
        )
        y_full = y[0:1, :]
        lane_full = lane[0:1, :]
        y_ok = (lane_full < half_y + 4) | (lane_full >= LANES - 4)
        y_ok = y_ok & (y_full >= 0) & (y_full < ny_total)
        value = jnp.where((inside_x > 0.5) & y_ok, jnp.exp(0.5 * log_kappa), 0.0)
        for group in range(8):
            out_ref[group // 2, group % 2, py] = value[group * ROWS : (group + 1) * ROWS]


def select_columns(width):
    half = width // 2
    column = iota((width, 2 * LANES), 1)
    own = iota((width, 2 * LANES), 0)
    parity, k = column // LANES, column % LANES
    pick_own = jnp.where((k < half) & (own == 2 * k + parity), 1.0, 0.0).astype(BF16)
    strip = iota((2 * HALO, 2 * LANES), 0)
    column = iota((2 * HALO, 2 * LANES), 1)
    parity, k = column // LANES, column % LANES
    k = jnp.where(k >= LANES - 4, k - LANES, k)
    even = lax.axis_index("gy") % 2 == 0
    below = strip % HALO - HALO
    fine = jnp.where((strip < HALO) == even, below + HALO + width, below)
    wanted = ((k < 0) | (k >= half)) & (k < half + 4)
    pick_strip = jnp.where(wanted & (fine == 2 * k + parity), 1.0, 0.0).astype(BF16)
    return pick_own, pick_strip


def exact_pick(values, pick, dims):
    total = None
    rest = values
    for _ in range(3):
        part = rest.astype(BF16)
        rest = rest - part.astype(F32)
        term = lax.dot_general(part, pick, (dims, ((), ())), preferred_element_type=F32)
        total = term if total is None else total + term
    return total


class Lazy:
    def __init__(self, rule):
        self.rule, self.known = rule, {}

    def __call__(self, *key):
        if key not in self.known:
            self.known[key] = self.rule(*key)
        return self.known[key]


def plus(*terms):
    total = None
    for term in terms:
        if term is not None:
            total = term if total is None else total + term
    return total


def times(left, right):
    return None if left is None or right is None else left * right


def minus(left, right):
    if right is None:
        return left
    return -right if left is None else left - right


def shift_x(value, steps):
    return None if value is None else pltpu.roll(value, (-steps) % ROWS, 0)


def shift_y(value, steps):
    return None if value is None else pltpu.roll(value, (-steps) % LANES, 1)


def main_body(field_ref, own_ref, far_ref, near_ref, stencil_hbm, solution_ref, wide_ref, stencil_ref, sem):
    width_y = own_ref.shape[-1]
    groups = own_ref.shape[0] - 4
    n_rows = groups * HALO
    pick_own, pick_strip = select_columns(width_y)
    even_block = lax.axis_index("gx") % 2 == 0
    for g in range(groups):
        for py in range(2):
            wide_ref[g, py, 16:24, :] = jnp.zeros((8, LANES), F32)

    def spread_block(ref, place):
        block = ref[...].reshape(-1, width_y)
        spread = exact_pick(block[:n_rows], pick_own, ((1,), (0,)))
        strips = jnp.concatenate([block[n_rows : n_rows + HALO], block[n_rows + 2 * HALO : n_rows + 3 * HALO]], 0)
        rest = jnp.concatenate([block[n_rows + HALO : n_rows + 2 * HALO], block[n_rows + 3 * HALO :]], 0)
        border = jnp.concatenate(
            [exact_pick(strips, pick_strip, ((0,), (0,))), exact_pick(rest, pick_strip, ((0,), (0,)))[: n_rows - LANES]], 0
        )
        spread = spread + border
        for g in range(groups):
            for py in range(2):
                wide_ref[g, py, pl.ds(place, 8), :] = spread[8 * g : 8 * g + 8, LANES * py : LANES * (py + 1)]

    spread_block(own_ref, 0)
    spread_block(near_ref, pl.multiple_of(jnp.where(even_block, 8, 24), 8))
    spread_block(far_ref, pl.multiple_of(jnp.where(even_block, 24, 8), 8))

    planes = 2

    def base(kind, z, px, py):
        return wide_ref[4 * kind + z, py, pl.ds(px, ROWS, stride=2), :]

    s = Lazy(lambda z, px, py: field_ref[z, px, py])

    def face(axis, z, px, py):
        here = s(z, px, py)
        if axis == "x":
            there = s(z, 1, py) if px == 0 else shift_x(s(z, 0, py), 1)
            return base(0, z, px, py) * (here * there)
        if axis == "y":
            there = s(z, px, 1) if py == 0 else shift_y(s(z, px, 0), 1)
            return base(1, z, px, py) * (here * there)
        if z < 0 or z + 1 >= 2 * planes:
            return None
        return base(2, z, px, py) * (here * s(z + 1, px, py))

    face = Lazy(face)
    mass = Lazy(lambda z, px, py: base(3, z, px, py) * (s(z, px, py) * s(z, px, py)))

    def pair(axis, z, px, py):
        if axis == "x":
            lower = face("x", z, 0, py) if px else shift_x(face("x", z, 1, py), -1)
        elif axis == "y":
            lower = face("y", z, px, 0) if py else shift_y(face("y", z, px, 1), -1)
        else:
            lower = face("z", z - 1, px, py)
        return plus(face(axis, z, px, py), lower)

    pair = Lazy(pair)

    def inverse(z, px, py):
        total = mass(z, px, py)
        for axis, odd in (("x", px), ("y", py), ("z", z % 2)):
            if odd:
                total = total + pair(axis, z, px, py)
        return 1.0 / jnp.where(s(z, px, py) > 0.0, total, 1.0)

    inverse = Lazy(inverse)

    def w_x(i, a):
        return None if not 0 <= i < planes else inverse(2 * i, 1, 0) * face("x", 2 * i, a, 0)

    def w_y(i, b):
        return None if not 0 <= i < planes else inverse(2 * i, 0, 1) * face("y", 2 * i, 0, b)

    def w_z(i, c):
        return times(inverse(2 * i + 1, 0, 0), face("z", 2 * i + c, 0, 0))

    w_x, w_y, w_z = Lazy(w_x), Lazy(w_y), Lazy(w_z)
    w_x_up = Lazy(lambda i, a: shift_y(w_x(i, a), 1))
    w_y_up = Lazy(lambda i, b: shift_x(w_y(i, b), 1))
    w_z_upx = Lazy(lambda i, c: shift_x(w_z(i, c), 1))
    w_z_upy = Lazy(lambda i, c: shift_y(w_z(i, c), 1))

    def w_xy(i, a, b):
        if not 0 <= i < planes:
            return None
        z = 2 * i
        return inverse(z, 1, 1) * (
            face("x", z, a, 1) * (w_y_up(i, b) if a else w_y(i, b)) + face("y", z, 1, b) * (w_x_up(i, a) if b else w_x(i, a))
        )

    def w_xz(i, a, c):
        z = 2 * i + 1
        return times(
            inverse(z, 1, 0),
            plus(times(face("x", z, a, 0), w_z_upx(i, c) if a else w_z(i, c)), times(face("z", 2 * i + c, 1, 0), w_x(i + c, a))),
        )

    def w_yz(i, b, c):
        z = 2 * i + 1
        return times(
            inverse(z, 0, 1),
            plus(times(face("y", z, 0, b), w_z_upy(i, c) if b else w_z(i, c)), times(face("z", 2 * i + c, 0, 1), w_y(i + c, b))),
        )

    w_xy, w_xz, w_yz = Lazy(w_xy), Lazy(w_xz), Lazy(w_yz)
    w_yz_up = Lazy(lambda i, b, c: shift_x(w_yz(i, b, c), 1))
    w_xz_up = Lazy(lambda i, a, c: shift_y(w_xz(i, a, c), 1))

    def w_xyz(i, a, b, c):
        z = 2 * i + 1
        if not 0 <= i < planes or not 0 <= i + c < planes:
            return None
        return inverse(z, 1, 1) * (
            face("x", z, a, 1) * (w_yz_up(i, b, c) if a else w_yz(i, b, c))
            + face("y", z, 1, b) * (w_xz_up(i, a, c) if b else w_xz(i, a, c))
            + face("z", 2 * i + c, 1, 1) * w_xy(i + c, a, b)
        )

    w_xyz = Lazy(w_xyz)

    low_x = Lazy(lambda i, b, c, a: shift_x(times(face("x", 2 * i + 1, 1, 1), w_xyz(i, a, b, c)), -1))
    low_y = Lazy(lambda i, a, c, b: shift_y(times(face("y", 2 * i + 1, 1, 1), w_xyz(i, a, b, c)), -1))

    def t_xy(i, a, b, dz):
        z = 2 * i
        row = None
        if dz == 0:
            row = times(pair("z", z, 1, 1), w_xy(i, a, b))
        if dz >= 0:
            row = minus(row, times(face("z", z, 1, 1), w_xyz(i, a, b, dz)))
        if dz <= 0:
            row = minus(row, times(face("z", z - 1, 1, 1), w_xyz(i - 1, a, b, dz + 1)))
        return minus(w_xy(i, a, b) if dz == 0 else None, times(inverse(z, 1, 1), row))

    def t_xz(i, a, c, dy):
        z = 2 * i + 1
        if not 0 <= i < planes or not 0 <= i + c < planes:
            return None
        row = None
        if dy == 0:
            row = times(pair("y", z, 1, 0), w_xz(i, a, c))
        if dy >= 0:
            row = minus(row, times(face("y", z, 1, 0), w_xyz(i, a, dy, c)))
        if dy <= 0:
            row = minus(row, low_y(i, a, c, dy + 1))
        return minus(w_xz(i, a, c) if dy == 0 else None, times(inverse(z, 1, 0), row))

    def t_yz(i, b, c, dx):
        z = 2 * i + 1
        if not 0 <= i < planes or not 0 <= i + c < planes:
            return None
        row = None
        if dx == 0:
            row = times(pair("x", z, 0, 1), w_yz(i, b, c))
        if dx >= 0:
            row = minus(row, times(face("x", z, 0, 1), w_xyz(i, dx, b, c)))
        if dx <= 0:
            row = minus(row, low_x(i, b, c, dx + 1))
        return minus(w_yz(i, b, c) if dx == 0 else None, times(inverse(z, 0, 1), row))

    t_xy, t_xz, t_yz = Lazy(t_xy), Lazy(t_xz), Lazy(t_yz)

    def t_x(i, a, dy, dz):
        z = 2 * i
        row = None
        if dy == 0 and dz == 0:
            row = plus(pair("y", z, 1, 0), pair("z", z, 1, 0)) * w_x(i, a)
        if dy >= 0:
            row = minus(row, times(face("y", z, 1, 0), t_xy(i, a, dy, dz)))
        if dy <= 0:
            row = minus(row, shift_y(times(face("y", z, 1, 1), t_xy(i, a, dy + 1, dz)), -1))
        if dz >= 0:
            row = minus(row, times(face("z", z, 1, 0), t_xz(i, a, dz, dy)))
        if dz <= 0:
            row = minus(row, times(face("z", z - 1, 1, 0), t_xz(i - 1, a, dz + 1, dy)))
        return minus(w_x(i, a) if dy == 0 and dz == 0 else None, times(inverse(z, 1, 0), row))

    def t_y(i, b, dx, dz):
        z = 2 * i
        row = None
        if dx == 0 and dz == 0:
            row = plus(pair("x", z, 0, 1), pair("z", z, 0, 1)) * w_y(i, b)
        if dx >= 0:
            row = minus(row, times(face("x", z, 0, 1), t_xy(i, dx, b, dz)))
        if dx <= 0:
            row = minus(row, shift_x(times(face("x", z, 1, 1), t_xy(i, dx + 1, b, dz)), -1))
        if dz >= 0:
            row = minus(row, times(face("z", z, 0, 1), t_yz(i, b, dz, dx)))
        if dz <= 0:
            row = minus(row, times(face("z", z - 1, 0, 1), t_yz(i - 1, b, dz + 1, dx)))
        return minus(w_y(i, b) if dx == 0 and dz == 0 else None, times(inverse(z, 0, 1), row))

    def t_z(i, c, dx, dy):
        z = 2 * i + 1
        if not 0 <= i < planes or not 0 <= i + c < planes:
            return None
        row = None
        if dx == 0 and dy == 0:
            row = plus(pair("x", z, 0, 0), pair("y", z, 0, 0)) * w_z(i, c)
        if dx >= 0:
            row = minus(row, times(face("x", z, 0, 0), t_xz(i, dx, c, dy)))
        if dx <= 0:
            row = minus(row, shift_x(times(face("x", z, 1, 0), t_xz(i, dx + 1, c, dy)), -1))
        if dy >= 0:
            row = minus(row, times(face("y", z, 0, 0), t_yz(i, dy, c, dx)))
        if dy <= 0:
            row = minus(row, shift_y(times(face("y", z, 0, 1), t_yz(i, dy + 1, c, dx)), -1))
        return minus(w_z(i, c) if dx == 0 and dy == 0 else None, times(inverse(z, 0, 0), row))

    t_x, t_y, t_z = Lazy(t_x), Lazy(t_y), Lazy(t_z)

    def direct(i, dz, dx, dy):
        z = 2 * i
        row = None
        if dx == 0 and dy == 0 and dz == 0:
            row = plus(mass(z, 0, 0), pair("x", z, 0, 0), pair("y", z, 0, 0), pair("z", z, 0, 0))
        if dx >= 0:
            row = minus(row, times(face("x", z, 0, 0), t_x(i, dx, dy, dz)))
        if dx <= 0:
            row = minus(row, shift_x(times(face("x", z, 1, 0), t_x(i, dx + 1, dy, dz)), -1))
        if dy >= 0:
            row = minus(row, times(face("y", z, 0, 0), t_y(i, dy, dx, dz)))
        if dy <= 0:
            row = minus(row, shift_y(times(face("y", z, 0, 1), t_y(i, dy + 1, dx, dz)), -1))
        if dz >= 0:
            row = minus(row, times(face("z", z, 0, 0), t_z(i, dz, dx, dy)))
        if dz <= 0:
            row = minus(row, times(face("z", z - 1, 0, 0), t_z(i - 1, dz + 1, dx, dy)))
        return row

    def coarse(i, dz, dx, dy):
        if not 0 <= i + dz < planes:
            return None
        if (dz, dx, dy) >= (0, 0, 0):
            return direct(i, dz, dx, dy)
        return shift_y(shift_x(coarse(i + dz, -dz, -dx, -dy), dx), dy)

    coarse = Lazy(coarse)

    keep_x, keep_y = stencil_ref.shape[2:]
    for i in range(planes):
        for dz in (-1, 0, 1):
            for dx in (-1, 0, 1):
                for dy in (-1, 0, 1):
                    value = coarse(i, dz, dx, dy)
                    number = 9 * (dz + 1) + 3 * (dx + 1) + dy + 1
                    if value is None:
                        stencil_ref[number, i] = jnp.zeros((keep_x, keep_y), F32)
                    else:
                        stencil_ref[number, i] = value[:keep_x, :keep_y]

    stencil_copy = pltpu.make_async_copy(stencil_ref, stencil_hbm, sem)
    stencil_copy.start()

    resid = Lazy(lambda z, px, py: base(4, z, px, py))
    odd_z = range(planes)
    q_xyz = [inverse(2 * i + 1, 1, 1) * resid(2 * i + 1, 1, 1) for i in odd_z] + [None]
    q_xy, q_xz, q_yz, q_x, q_y, q_z, rhs = [], [], [], [], [], [], []

    def side_x(z, py, value):
        return plus(times(face("x", z, 0, py), value), shift_x(times(face("x", z, 1, py), value), -1))

    def side_y(z, px, value):
        return plus(times(face("y", z, px, 0), value), shift_y(times(face("y", z, px, 1), value), -1))

    def side_z(z, px, py, values):
        i = z // 2
        return plus(times(face("z", z, px, py), values[i]), times(face("z", z - 1, px, py), values[i - 1] if i else None))

    for i in range(planes):
        z = 2 * i
        q_xy.append(inverse(z, 1, 1) * plus(resid(z, 1, 1), side_z(z, 1, 1, q_xyz)))
        q_xz.append(inverse(z + 1, 1, 0) * plus(resid(z + 1, 1, 0), side_y(z + 1, 1, q_xyz[i])))
        q_yz.append(inverse(z + 1, 0, 1) * plus(resid(z + 1, 0, 1), side_x(z + 1, 1, q_xyz[i])))
    for i in range(planes):
        z = 2 * i
        q_x.append(inverse(z, 1, 0) * plus(resid(z, 1, 0), side_y(z, 1, q_xy[i]), side_z(z, 1, 0, q_xz)))
        q_y.append(inverse(z, 0, 1) * plus(resid(z, 0, 1), side_x(z, 1, q_xy[i]), side_z(z, 0, 1, q_yz)))
        q_z.append(
            inverse(z + 1, 0, 0) * plus(resid(z + 1, 0, 0), side_x(z + 1, 0, q_xz[i]), side_y(z + 1, 0, q_yz[i]))
        )
    for i in range(planes):
        z = 2 * i
        rhs.append(plus(resid(z, 0, 0), side_x(z, 0, q_x[i]), side_y(z, 0, q_y[i]), side_z(z, 0, 0, q_z)))

    scaled = []
    for i in range(planes):
        inside = s(2 * i, 0, 0) > 0.0
        scaled.append(jnp.where(inside, OMEGA / jnp.where(inside, coarse(i, 0, 0, 0), 1.0), 0.0))
    u = [scaled[i] * rhs[i] for i in range(planes)]
    for _ in range(SWEEPS - 1):
        moved = {}
        for i in range(planes):
            for dx in (-1, 0, 1):
                row = shift_x(u[i], dx) if dx else u[i]
                for dy in (-1, 0, 1):
                    moved[i, dx, dy] = shift_y(row, dy) if dy else row
        new = []
        for i in range(planes):
            total = None
            for dz in (-1, 0, 1):
                for dx in (-1, 0, 1):
                    for dy in (-1, 0, 1):
                        total = plus(total, times(coarse(i, dz, dx, dy), moved.get((i + dz, dx, dy))))
            new.append(u[i] + scaled[i] * (rhs[i] - total))
        u = new
    for i in range(planes):
        solution_ref[i] = u[i][:keep_x, :keep_y]
    stencil_copy.wait()


def swap(value, axis, first, wrap):
    count = lax.axis_size(axis)
    partner = list(range(count))
    for i in range(first, count if wrap else count - 1, 2):
        partner[i], partner[(i + 1) % count] = (i + 1) % count, i
    return lax.ppermute(value, axis, list(enumerate(partner)))


def on_chip(value):
    return pltpu.with_memory_space_constraint(value, pltpu.VMEM)


def on_device(base_cond, base_mass, fine_residual, point_index, gen_vector, z_offset):
    plane_count, width_x, width_y = base_mass.shape
    nx_total = width_x * lax.axis_size("gx")
    ny_total = width_y * lax.axis_size("gy")
    smem = pl.BlockSpec(memory_space=pltpu.SMEM)
    vmem = pl.BlockSpec(memory_space=pltpu.VMEM)
    hbm = pl.BlockSpec(memory_space=pl.ANY)
    strip = pltpu.VMEM((2, HALO, LANES), F32)
    groups = 5 * plane_count
    own, near_y, far_y = pl.pallas_call(
        strips_body,
        out_shape=(pltpu.VMEM((groups + 4, HALO, width_y), F32), strip, strip),
        in_specs=[hbm] * 3,
        out_specs=(vmem,) * 3,
        scratch_shapes=[pltpu.SemaphoreType.DMA((5,))],
        name="strips",
    )(base_cond, base_mass, fine_residual)
    far_y = swap(far_y, "gy", 1, True)
    near_y = swap(near_y, "gy", 0, False)
    field = pl.pallas_call(
        lambda *refs: field_body(nx_total, ny_total, width_x, width_y, *refs),
        out_shape=pltpu.VMEM((plane_count, 2, 2, ROWS, LANES), F32),
        in_specs=[smem, smem, vmem],
        out_specs=vmem,
        name="field",
    )(point_index, z_offset, gen_vector.reshape(1, -1))
    own = lax.dynamic_update_slice(own, near_y, (groups, 0, 0))
    own = lax.dynamic_update_slice(own, far_y, (groups + 2, 0, 0))
    far = swap(own, "gx", 1, False)
    near = swap(own, "gx", 0, False)
    coarse_block = (plane_count // 2, width_x // 2, width_y // 2)
    return pl.pallas_call(
        main_body,
        out_shape=(jax.ShapeDtypeStruct((27, *coarse_block), F32), jax.ShapeDtypeStruct(coarse_block, F32)),
        in_specs=[vmem] * 4,
        out_specs=(hbm, vmem),
        scratch_shapes=[
            pltpu.VMEM((groups, 2, 2 * ROWS, LANES), F32),
            pltpu.VMEM((27, *coarse_block), F32),
            pltpu.SemaphoreType.DMA,
        ],
        name="galerkin",
    )(*[on_chip(value) for value in (field, own, far, near)])


def solution(mesh):
    return jax.shard_map(
        on_device,
        mesh=mesh,
        in_specs=(
            P(None, None, "gx", "gy"),
            P(None, "gx", "gy"),
            P("parts", "gx", "gy"),
            P("parts"),
            P(),
            P(),
        ),
        out_specs=(P(None, "parts", "gx", "gy"), P("parts", "gx", "gy")),
        check_vma=False,
    )
```

```python
import math

import jax
import jax.numpy as jnp
from jax import lax
from jax.experimental import pallas as pl
from jax.experimental.pallas import tpu as pltpu
from jax.sharding import PartitionSpec as P

NZG = 512
QMCN = 1048576
SWEEPS = 4
OMEGA = 0.6
ROWS = 16
LANES = 128
HALO = 8
F32 = jnp.float32
BF16 = jnp.bfloat16


def iota(shape, dim):
    return lax.broadcasted_iota(jnp.int32, shape, dim)


def two_parts(values, axis):
    high = values.astype(BF16)
    return jnp.concatenate([high, (values - high.astype(F32)).astype(BF16)], axis)


def strips_body(cond_hbm, mass_hbm, resid_hbm, own_ref, near_ref, far_ref, sems):
    width = own_ref.shape[-1]
    planes = mass_hbm.shape[0]
    sources = [cond_hbm.at[axis] for axis in range(3)] + [mass_hbm, resid_hbm]
    copies = [
        pltpu.make_async_copy(source, own_ref.at[number * planes : (number + 1) * planes], sems.at[number])
        for number, source in enumerate(sources)
    ]
    for copy in copies:
        copy.start()
    even = lax.axis_index("gy") % 2 == 0
    row, lane = iota((2 * HALO, width), 0), iota((2 * HALO, width), 1)
    column = row % HALO + jnp.where((row < HALO) == even, width - HALO, 0)
    pick = jnp.where(lane == column, 1.0, 0.0).astype(BF16)
    for copy in copies:
        copy.wait()
    rows = two_parts(own_ref[: 5 * planes].reshape(-1, width), 1)
    taken = lax.dot_general(
        jnp.concatenate([pick, pick], 1), rows, (((1,), (1,)), ((), ())), preferred_element_type=F32
    )
    for out_ref, start in ((near_ref, 0), (far_ref, HALO)):
        part = taken[start : start + HALO]
        out_ref[0] = part[:, :LANES]
        out_ref[1] = jnp.concatenate([part[:, LANES:], jnp.zeros((HALO, 2 * LANES - part.shape[1]), F32)], 1)


def local_body(nx_total, ny_total, width_x, width_y, integers_ref, own_ref, out_ref, wide_ref, pick_own_ref, pick_strip_ref):
    for ref, pick in zip((pick_own_ref, pick_strip_ref), select_columns(width_y)):
        ref[...] = jnp.concatenate([pick, pick], 0)
    groups = wide_ref.shape[0]
    spread = spread_rows([own_ref], groups, pick_own_ref[...], pick_strip_ref[...])[0]
    for g in range(groups):
        for py in range(2):
            wide_ref[g, py] = spread[g][:, LANES * py : LANES * (py + 1)]
    modes = integers_ref.shape[1] - 2
    product = integers_ref[:, modes : modes + 1] * integers_ref[:, :modes]
    z_first = integers_ref[:, modes + 1 : modes + 2]
    x_first = lax.axis_index("gx") * width_x
    y_first = lax.axis_index("gy") * width_y
    half_x, half_y = width_x // 2, width_y // 2
    shift = (product & (QMCN - 1)).astype(F32) / QMCN - 0.5
    mode_row = iota((modes, modes), 0)
    mode_col = jnp.sum(jnp.where(mode_row == iota((modes, modes), 1), shift, 0.0), axis=1, keepdims=True)
    k = iota((modes, LANES), 0)
    lane = iota((modes, LANES), 1)
    k_f = k.astype(F32)
    amplitude = 1.2 / (1.0 + 0.5 * k_f) * mode_col
    z_local = lane // (2 * ROWS)
    px = (lane // ROWS) % 2
    r = lane % ROWS
    coarse_x = jnp.where(r < 8, r, r - ROWS)
    x = x_first + 2 * coarse_x + px
    x_angle = (x.astype(F32) + 0.5) * (math.pi / nx_total)
    z_angle = ((z_local + z_first).astype(F32) + 0.5) * (math.pi / NZG)
    phase = z_angle * (k % 5).astype(F32) + x_angle * (1 + k % 4).astype(F32) + 0.7 * k_f
    x_ok = (r < 8) | (r >= 12)
    ones = jnp.where(x_ok & (x >= 0) & (x < nx_total), 1.0, 0.0)
    left = jnp.concatenate([amplitude * jnp.cos(phase), -amplitude * jnp.sin(phase)], 0)
    inside_x = lax.dot_general(ones, jnp.ones((modes, LANES), F32), (((0,), (0,)), ((), ())), preferred_element_type=F32)
    y_mode = (1 + (k // 4) % 4).astype(F32)
    for py in range(2):
        coarse_y = jnp.where(lane < half_y + 4, lane, lane - LANES)
        y = y_first + 2 * coarse_y + py
        y_angle = (y.astype(F32) + 0.5) * (math.pi / ny_total) * y_mode
        right = jnp.concatenate([jnp.cos(y_angle), jnp.sin(y_angle)], 0)
        log_kappa = lax.dot_general(
            left, right, (((0,), (0,)), ((), ())), precision=lax.Precision.HIGHEST, preferred_element_type=F32
        )
        y_full = y[0:1, :]
        lane_full = lane[0:1, :]
        y_ok = (lane_full < half_y + 4) | (lane_full >= LANES - 4)
        y_ok = y_ok & (y_full >= 0) & (y_full < ny_total)
        value = jnp.where((inside_x > 0.5) & y_ok, jnp.exp(0.5 * log_kappa), 0.0)
        for group in range(8):
            out_ref[group // 2, group % 2, py] = value[group * ROWS : (group + 1) * ROWS]


def select_columns(width):
    half = width // 2
    column = iota((width, 2 * LANES), 1)
    own = iota((width, 2 * LANES), 0)
    parity, k = column // LANES, column % LANES
    pick_own = jnp.where((k < half) & (own == 2 * k + parity), 1.0, 0.0).astype(BF16)
    strip = iota((2 * HALO, 2 * LANES), 0)
    column = iota((2 * HALO, 2 * LANES), 1)
    parity, k = column // LANES, column % LANES
    k = jnp.where(k >= LANES - 4, k - LANES, k)
    even = lax.axis_index("gy") % 2 == 0
    below = strip % HALO - HALO
    fine = jnp.where((strip < HALO) == even, below + HALO + width, below)
    wanted = ((k < 0) | (k >= half)) & (k < half + 4)
    pick_strip = jnp.where(wanted & (fine == 2 * k + parity), 1.0, 0.0).astype(BF16)
    return pick_own, pick_strip


def spread_rows(refs, groups, pick_own, pick_strip):
    main, split = LANES // HALO, groups - LANES // HALO
    blocks = [ref[...] for ref in refs]
    rows = [block[:main].reshape(LANES, -1) for block in blocks]
    rows += [block[main:groups].reshape(split * HALO, -1) for block in blocks]
    strips = [jnp.concatenate([block[groups], block[groups + 2]], 0) for block in blocks]
    strips += [jnp.concatenate([block[groups + 1], block[groups + 3]], 0)[:, : split * HALO] for block in blocks]
    spread = lax.dot_general(
        two_parts(jnp.concatenate(rows, 0), 1), pick_own, (((1,), (0,)), ((), ())), preferred_element_type=F32
    )
    border = lax.dot_general(
        two_parts(jnp.concatenate(strips, 1), 0), pick_strip, (((0,), (0,)), ((), ())), preferred_element_type=F32
    )
    spread = spread + border
    result = []
    for number in range(len(refs)):
        first = [number * LANES + HALO * g for g in range(main)]
        first += [len(refs) * LANES + number * split * HALO + HALO * g for g in range(split)]
        result.append([spread[row : row + HALO] for row in first])
    return result


class Lazy:
    def __init__(self, rule):
        self.rule, self.known = rule, {}

    def __call__(self, *key):
        if key not in self.known:
            self.known[key] = self.rule(*key)
        return self.known[key]


def plus(*terms):
    total = None
    for term in terms:
        if term is not None:
            total = term if total is None else total + term
    return total


def times(left, right):
    return None if left is None or right is None else left * right


def minus(left, right):
    if right is None:
        return left
    return -right if left is None else left - right


def shift_x(value, steps):
    return None if value is None else pltpu.roll(value, (-steps) % ROWS, 0)


def shift_y(value, steps):
    return None if value is None else pltpu.roll(value, (-steps) % LANES, 1)


def main_body(
    field_ref,
    pick_own_ref,
    pick_strip_ref,
    own_ref,
    far_ref,
    near_ref,
    stencil_hbm,
    solution_hbm,
    wide_ref,
    stencil_ref,
    solution_ref,
    sems,
):
    groups = own_ref.shape[0]
    for g in range(groups):
        for py in range(2):
            wide_ref[g, py, 0:8, :] = own_ref[g, py]
            wide_ref[g, py, 16:24, :] = jnp.zeros((8, LANES), F32)
    above = lax.axis_index("gx") % 2 == 0
    near_place = pl.multiple_of(jnp.where(above, 8, 24), 8)
    far_place = pl.multiple_of(jnp.where(above, 24, 8), 8)
    spread = spread_rows([near_ref, far_ref], groups, pick_own_ref[...], pick_strip_ref[...])
    for place, rows in zip((near_place, far_place), spread):
        for g in range(groups):
            for py in range(2):
                wide_ref[g, py, pl.ds(place, 8), :] = rows[g][:, LANES * py : LANES * (py + 1)]

    planes = 2

    def base(kind, z, px, py):
        return wide_ref[4 * kind + z, py, pl.ds(px, ROWS, stride=2), :]

    s = Lazy(lambda z, px, py: field_ref[z, px, py])

    def face(axis, z, px, py):
        here = s(z, px, py)
        if axis == "x":
            there = s(z, 1, py) if px == 0 else shift_x(s(z, 0, py), 1)
            return base(0, z, px, py) * (here * there)
        if axis == "y":
            there = s(z, px, 1) if py == 0 else shift_y(s(z, px, 0), 1)
            return base(1, z, px, py) * (here * there)
        if z < 0 or z + 1 >= 2 * planes:
            return None
        return base(2, z, px, py) * (here * s(z + 1, px, py))

    face = Lazy(face)
    mass = Lazy(lambda z, px, py: base(3, z, px, py) * (s(z, px, py) * s(z, px, py)))

    def pair(axis, z, px, py):
        if axis == "x":
            lower = face("x", z, 0, py) if px else shift_x(face("x", z, 1, py), -1)
        elif axis == "y":
            lower = face("y", z, px, 0) if py else shift_y(face("y", z, px, 1), -1)
        else:
            lower = face("z", z - 1, px, py)
        return plus(face(axis, z, px, py), lower)

    pair = Lazy(pair)

    def inverse(z, px, py):
        total = mass(z, px, py)
        for axis, odd in (("x", px), ("y", py), ("z", z % 2)):
            if odd:
                total = total + pair(axis, z, px, py)
        return 1.0 / jnp.where(s(z, px, py) > 0.0, total, 1.0)

    inverse = Lazy(inverse)

    def w_x(i, a):
        return None if not 0 <= i < planes else inverse(2 * i, 1, 0) * face("x", 2 * i, a, 0)

    def w_y(i, b):
        return None if not 0 <= i < planes else inverse(2 * i, 0, 1) * face("y", 2 * i, 0, b)

    def w_z(i, c):
        return times(inverse(2 * i + 1, 0, 0), face("z", 2 * i + c, 0, 0))

    w_x, w_y, w_z = Lazy(w_x), Lazy(w_y), Lazy(w_z)
    w_x_up = Lazy(lambda i, a: shift_y(w_x(i, a), 1))
    w_y_up = Lazy(lambda i, b: shift_x(w_y(i, b), 1))
    w_z_upx = Lazy(lambda i, c: shift_x(w_z(i, c), 1))
    w_z_upy = Lazy(lambda i, c: shift_y(w_z(i, c), 1))

    def w_xy(i, a, b):
        if not 0 <= i < planes:
            return None
        z = 2 * i
        return inverse(z, 1, 1) * (
            face("x", z, a, 1) * (w_y_up(i, b) if a else w_y(i, b)) + face("y", z, 1, b) * (w_x_up(i, a) if b else w_x(i, a))
        )

    def w_xz(i, a, c):
        z = 2 * i + 1
        return times(
            inverse(z, 1, 0),
            plus(times(face("x", z, a, 0), w_z_upx(i, c) if a else w_z(i, c)), times(face("z", 2 * i + c, 1, 0), w_x(i + c, a))),
        )

    def w_yz(i, b, c):
        z = 2 * i + 1
        return times(
            inverse(z, 0, 1),
            plus(times(face("y", z, 0, b), w_z_upy(i, c) if b else w_z(i, c)), times(face("z", 2 * i + c, 0, 1), w_y(i + c, b))),
        )

    w_xy, w_xz, w_yz = Lazy(w_xy), Lazy(w_xz), Lazy(w_yz)
    w_yz_up = Lazy(lambda i, b, c: shift_x(w_yz(i, b, c), 1))
    w_xz_up = Lazy(lambda i, a, c: shift_y(w_xz(i, a, c), 1))

    def w_xyz(i, a, b, c):
        z = 2 * i + 1
        if not 0 <= i < planes or not 0 <= i + c < planes:
            return None
        return inverse(z, 1, 1) * (
            face("x", z, a, 1) * (w_yz_up(i, b, c) if a else w_yz(i, b, c))
            + face("y", z, 1, b) * (w_xz_up(i, a, c) if b else w_xz(i, a, c))
            + face("z", 2 * i + c, 1, 1) * w_xy(i + c, a, b)
        )

    w_xyz = Lazy(w_xyz)

    low_x = Lazy(lambda i, b, c, a: shift_x(times(face("x", 2 * i + 1, 1, 1), w_xyz(i, a, b, c)), -1))
    low_y = Lazy(lambda i, a, c, b: shift_y(times(face("y", 2 * i + 1, 1, 1), w_xyz(i, a, b, c)), -1))

    def t_xy(i, a, b, dz):
        z = 2 * i
        row = None
        if dz == 0:
            row = times(pair("z", z, 1, 1), w_xy(i, a, b))
        if dz >= 0:
            row = minus(row, times(face("z", z, 1, 1), w_xyz(i, a, b, dz)))
        if dz <= 0:
            row = minus(row, times(face("z", z - 1, 1, 1), w_xyz(i - 1, a, b, dz + 1)))
        return minus(w_xy(i, a, b) if dz == 0 else None, times(inverse(z, 1, 1), row))

    def t_xz(i, a, c, dy):
        z = 2 * i + 1
        if not 0 <= i < planes or not 0 <= i + c < planes:
            return None
        row = None
        if dy == 0:
            row = times(pair("y", z, 1, 0), w_xz(i, a, c))
        if dy >= 0:
            row = minus(row, times(face("y", z, 1, 0), w_xyz(i, a, dy, c)))
        if dy <= 0:
            row = minus(row, low_y(i, a, c, dy + 1))
        return minus(w_xz(i, a, c) if dy == 0 else None, times(inverse(z, 1, 0), row))

    def t_yz(i, b, c, dx):
        z = 2 * i + 1
        if not 0 <= i < planes or not 0 <= i + c < planes:
            return None
        row = None
        if dx == 0:
            row = times(pair("x", z, 0, 1), w_yz(i, b, c))
        if dx >= 0:
            row = minus(row, times(face("x", z, 0, 1), w_xyz(i, dx, b, c)))
        if dx <= 0:
            row = minus(row, low_x(i, b, c, dx + 1))
        return minus(w_yz(i, b, c) if dx == 0 else None, times(inverse(z, 0, 1), row))

    t_xy, t_xz, t_yz = Lazy(t_xy), Lazy(t_xz), Lazy(t_yz)

    def t_x(i, a, dy, dz):
        z = 2 * i
        row = None
        if dy == 0 and dz == 0:
            row = plus(pair("y", z, 1, 0), pair("z", z, 1, 0)) * w_x(i, a)
        if dy >= 0:
            row = minus(row, times(face("y", z, 1, 0), t_xy(i, a, dy, dz)))
        if dy <= 0:
            row = minus(row, shift_y(times(face("y", z, 1, 1), t_xy(i, a, dy + 1, dz)), -1))
        if dz >= 0:
            row = minus(row, times(face("z", z, 1, 0), t_xz(i, a, dz, dy)))
        if dz <= 0:
            row = minus(row, times(face("z", z - 1, 1, 0), t_xz(i - 1, a, dz + 1, dy)))
        return minus(w_x(i, a) if dy == 0 and dz == 0 else None, times(inverse(z, 1, 0), row))

    def t_y(i, b, dx, dz):
        z = 2 * i
        row = None
        if dx == 0 and dz == 0:
            row = plus(pair("x", z, 0, 1), pair("z", z, 0, 1)) * w_y(i, b)
        if dx >= 0:
            row = minus(row, times(face("x", z, 0, 1), t_xy(i, dx, b, dz)))
        if dx <= 0:
            row = minus(row, shift_x(times(face("x", z, 1, 1), t_xy(i, dx + 1, b, dz)), -1))
        if dz >= 0:
            row = minus(row, times(face("z", z, 0, 1), t_yz(i, b, dz, dx)))
        if dz <= 0:
            row = minus(row, times(face("z", z - 1, 0, 1), t_yz(i - 1, b, dz + 1, dx)))
        return minus(w_y(i, b) if dx == 0 and dz == 0 else None, times(inverse(z, 0, 1), row))

    def t_z(i, c, dx, dy):
        z = 2 * i + 1
        if not 0 <= i < planes or not 0 <= i + c < planes:
            return None
        row = None
        if dx == 0 and dy == 0:
            row = plus(pair("x", z, 0, 0), pair("y", z, 0, 0)) * w_z(i, c)
        if dx >= 0:
            row = minus(row, times(face("x", z, 0, 0), t_xz(i, dx, c, dy)))
        if dx <= 0:
            row = minus(row, shift_x(times(face("x", z, 1, 0), t_xz(i, dx + 1, c, dy)), -1))
        if dy >= 0:
            row = minus(row, times(face("y", z, 0, 0), t_yz(i, dy, c, dx)))
        if dy <= 0:
            row = minus(row, shift_y(times(face("y", z, 0, 1), t_yz(i, dy + 1, c, dx)), -1))
        return minus(w_z(i, c) if dx == 0 and dy == 0 else None, times(inverse(z, 0, 0), row))

    t_x, t_y, t_z = Lazy(t_x), Lazy(t_y), Lazy(t_z)

    def direct(i, dz, dx, dy):
        z = 2 * i
        row = None
        if dx == 0 and dy == 0 and dz == 0:
            row = plus(mass(z, 0, 0), pair("x", z, 0, 0), pair("y", z, 0, 0), pair("z", z, 0, 0))
        if dx >= 0:
            row = minus(row, times(face("x", z, 0, 0), t_x(i, dx, dy, dz)))
        if dx <= 0:
            row = minus(row, shift_x(times(face("x", z, 1, 0), t_x(i, dx + 1, dy, dz)), -1))
        if dy >= 0:
            row = minus(row, times(face("y", z, 0, 0), t_y(i, dy, dx, dz)))
        if dy <= 0:
            row = minus(row, shift_y(times(face("y", z, 0, 1), t_y(i, dy + 1, dx, dz)), -1))
        if dz >= 0:
            row = minus(row, times(face("z", z, 0, 0), t_z(i, dz, dx, dy)))
        if dz <= 0:
            row = minus(row, times(face("z", z - 1, 0, 0), t_z(i - 1, dz + 1, dx, dy)))
        return row

    def coarse(i, dz, dx, dy):
        if not 0 <= i + dz < planes:
            return None
        if (dz, dx, dy) >= (0, 0, 0):
            return direct(i, dz, dx, dy)
        return shift_y(shift_x(coarse(i + dz, -dz, -dx, -dy), dx), dy)

    coarse = Lazy(coarse)

    keep_x, keep_y = stencil_ref.shape[2:]
    for i in range(planes):
        for dz in (-1, 0, 1):
            for dx in (-1, 0, 1):
                for dy in (-1, 0, 1):
                    value = coarse(i, dz, dx, dy)
                    number = 9 * (dz + 1) + 3 * (dx + 1) + dy + 1
                    if value is None:
                        stencil_ref[number, i] = jnp.zeros((keep_x, keep_y), F32)
                    else:
                        stencil_ref[number, i] = value[:keep_x, :keep_y]

    stencil_copy = pltpu.make_async_copy(stencil_ref, stencil_hbm, sems.at[0])
    stencil_copy.start()

    resid = Lazy(lambda z, px, py: base(4, z, px, py))
    odd_z = range(planes)
    q_xyz = [inverse(2 * i + 1, 1, 1) * resid(2 * i + 1, 1, 1) for i in odd_z] + [None]
    q_xy, q_xz, q_yz, q_x, q_y, q_z, rhs = [], [], [], [], [], [], []

    def side_x(z, py, value):
        return plus(times(face("x", z, 0, py), value), shift_x(times(face("x", z, 1, py), value), -1))

    def side_y(z, px, value):
        return plus(times(face("y", z, px, 0), value), shift_y(times(face("y", z, px, 1), value), -1))

    def side_z(z, px, py, values):
        i = z // 2
        return plus(times(face("z", z, px, py), values[i]), times(face("z", z - 1, px, py), values[i - 1] if i else None))

    for i in range(planes):
        z = 2 * i
        q_xy.append(inverse(z, 1, 1) * plus(resid(z, 1, 1), side_z(z, 1, 1, q_xyz)))
        q_xz.append(inverse(z + 1, 1, 0) * plus(resid(z + 1, 1, 0), side_y(z + 1, 1, q_xyz[i])))
        q_yz.append(inverse(z + 1, 0, 1) * plus(resid(z + 1, 0, 1), side_x(z + 1, 1, q_xyz[i])))
    for i in range(planes):
        z = 2 * i
        q_x.append(inverse(z, 1, 0) * plus(resid(z, 1, 0), side_y(z, 1, q_xy[i]), side_z(z, 1, 0, q_xz)))
        q_y.append(inverse(z, 0, 1) * plus(resid(z, 0, 1), side_x(z, 1, q_xy[i]), side_z(z, 0, 1, q_yz)))
        q_z.append(
            inverse(z + 1, 0, 0) * plus(resid(z + 1, 0, 0), side_x(z + 1, 0, q_xz[i]), side_y(z + 1, 0, q_yz[i]))
        )
    for i in range(planes):
        z = 2 * i
        rhs.append(plus(resid(z, 0, 0), side_x(z, 0, q_x[i]), side_y(z, 0, q_y[i]), side_z(z, 0, 0, q_z)))

    scaled = []
    for i in range(planes):
        inside = s(2 * i, 0, 0) > 0.0
        scaled.append(jnp.where(inside, OMEGA / jnp.where(inside, coarse(i, 0, 0, 0), 1.0), 0.0))
    u = [scaled[i] * rhs[i] for i in range(planes)]
    for _ in range(SWEEPS - 1):
        moved = {}
        for i in range(planes):
            for dx in (-1, 0, 1):
                row = shift_x(u[i], dx) if dx else u[i]
                for dy in (-1, 0, 1):
                    moved[i, dx, dy] = shift_y(row, dy) if dy else row
        new = []
        for i in range(planes):
            total = None
            for dz in (-1, 0, 1):
                for dx in (-1, 0, 1):
                    for dy in (-1, 0, 1):
                        total = plus(total, times(coarse(i, dz, dx, dy), moved.get((i + dz, dx, dy))))
            new.append(u[i] + scaled[i] * (rhs[i] - total))
        u = new
    for i in range(planes):
        solution_ref[i] = u[i][:keep_x, :keep_y]
    solution_copy = pltpu.make_async_copy(solution_ref, solution_hbm, sems.at[1])
    solution_copy.start()
    stencil_copy.wait()
    solution_copy.wait()


def swap(value, axis, first, wrap):
    count = lax.axis_size(axis)
    partner = list(range(count))
    for i in range(first, count if wrap else count - 1, 2):
        partner[i], partner[(i + 1) % count] = (i + 1) % count, i
    return lax.ppermute(value, axis, list(enumerate(partner)))


def swap_x(value, first):
    nx, ny = lax.axis_size("gx"), lax.axis_size("gy")
    pairs = []
    for x in range(nx):
        other = x + 1 if x % 2 == first % 2 else x - 1
        for y in range(ny):
            target = (other, y) if 0 <= other < nx else (x, y + 1 if y % 2 == 0 else y - 1)
            pairs.append((x * ny + y, target[0] * ny + target[1]))
    return lax.ppermute(value, ("gx", "gy"), pairs)


def on_chip(value):
    return pltpu.with_memory_space_constraint(value, pltpu.VMEM)


def on_device(base_cond, base_mass, fine_residual, point_index, gen_vector, z_offset):
    plane_count, width_x, width_y = base_mass.shape
    nx_total = width_x * lax.axis_size("gx")
    ny_total = width_y * lax.axis_size("gy")
    vmem = pl.BlockSpec(memory_space=pltpu.VMEM)
    hbm = pl.BlockSpec(memory_space=pl.ANY)
    strip = pltpu.VMEM((2, HALO, LANES), F32)
    groups = 5 * plane_count
    own, near_y, far_y = pl.pallas_call(
        strips_body,
        out_shape=(pltpu.VMEM((groups + 4, HALO, width_y), F32), strip, strip),
        in_specs=[hbm] * 3,
        out_specs=(vmem,) * 3,
        scratch_shapes=[pltpu.SemaphoreType.DMA((5,))],
        name="strips",
    )(base_cond, base_mass, fine_residual)
    far_y = swap(far_y, "gy", 1, True)
    near_y = swap(near_y, "gy", 0, False)
    own = lax.dynamic_update_slice(own, near_y, (groups, 0, 0))
    own = lax.dynamic_update_slice(own, far_y, (groups + 2, 0, 0))
    integers = jnp.concatenate([gen_vector, point_index, z_offset]).reshape(1, -1)
    field, wide, pick_own, pick_strip = pl.pallas_call(
        lambda *refs: local_body(nx_total, ny_total, width_x, width_y, *refs),
        out_shape=(
            pltpu.VMEM((plane_count, 2, 2, ROWS, LANES), F32),
            pltpu.VMEM((groups, 2, HALO, LANES), F32),
            pltpu.VMEM((2 * width_y, 2 * LANES), BF16),
            pltpu.VMEM((4 * HALO, 2 * LANES), BF16),
        ),
        in_specs=[vmem] * 2,
        out_specs=(vmem,) * 4,
        name="local",
    )(on_chip(integers), on_chip(own))
    far = swap_x(own, 1)
    near = swap_x(own, 0)
    coarse_block = (plane_count // 2, width_x // 2, width_y // 2)
    return pl.pallas_call(
        main_body,
        out_shape=(jax.ShapeDtypeStruct((27, *coarse_block), F32), jax.ShapeDtypeStruct(coarse_block, F32)),
        in_specs=[vmem] * 6,
        out_specs=(hbm, hbm),
        scratch_shapes=[
            pltpu.VMEM((groups, 2, 2 * ROWS, LANES), F32),
            pltpu.VMEM((27, *coarse_block), F32),
            pltpu.VMEM(coarse_block, F32),
            pltpu.SemaphoreType.DMA((2,)),
        ],
        name="galerkin",
    )(*[on_chip(value) for value in (field, pick_own, pick_strip, wide, far, near)])


def solution(mesh):
    return jax.shard_map(
        on_device,
        mesh=mesh,
        in_specs=(
            P(None, None, "gx", "gy"),
            P(None, "gx", "gy"),
            P("parts", "gx", "gy"),
            P("parts"),
            P(),
            P(),
        ),
        out_specs=(P(None, "parts", "gx", "gy"), P("parts", "gx", "gy")),
        check_vma=False,
    )
```

```python
import math

import jax
import jax.numpy as jnp
from jax import lax
from jax.experimental import pallas as pl
from jax.experimental.pallas import tpu as pltpu
from jax.sharding import PartitionSpec as P

NZG = 512
QMCN = 1048576
SWEEPS = 4
OMEGA = 0.6
ROWS = 16
LANES = 128
HALO = 8
F32 = jnp.float32
BF16 = jnp.bfloat16


def iota(shape, dim):
    return lax.broadcasted_iota(jnp.int32, shape, dim)


def two_parts(values, axis):
    high = values.astype(BF16)
    return jnp.concatenate([high, (values - high.astype(F32)).astype(BF16)], axis)


def field_start(kind, planes):
    return kind * planes - (1 if kind > 2 else 0)


def strips_body(cond_hbm, mass_hbm, resid_hbm, own_ref, near_ref, far_ref, sems):
    width = own_ref.shape[-1]
    planes = mass_hbm.shape[0]
    sources = [cond_hbm.at[0], cond_hbm.at[1], cond_hbm.at[2, : planes - 1], mass_hbm, resid_hbm]
    starts = [field_start(kind, planes) for kind in range(6)]
    copies = [
        pltpu.make_async_copy(source, own_ref.at[starts[kind] : starts[kind + 1]], sems.at[kind])
        for kind, source in enumerate(sources)
    ]
    for copy in copies:
        copy.start()
    even = lax.axis_index("gy") % 2 == 0
    row, lane = iota((2 * HALO, width), 0), iota((2 * HALO, width), 1)
    column = row % HALO + jnp.where((row < HALO) == even, width - HALO, 0)
    pick = jnp.where(lane == column, 1.0, 0.0).astype(BF16)
    for copy in copies:
        copy.wait()
    rows = two_parts(own_ref[: starts[5]].reshape(-1, width), 1)
    taken = lax.dot_general(
        jnp.concatenate([pick, pick], 1), rows, (((1,), (1,)), ((), ())), preferred_element_type=F32
    )
    for out_ref, start in ((near_ref, 0), (far_ref, 1)):
        part = taken[HALO * start : HALO * (start + 1)]
        out_ref[0] = part[:, :LANES]
        rest = jnp.concatenate([part[:, LANES:], jnp.zeros((HALO, 3 * LANES // 2 - part.shape[1]), F32)], 1)
        blank = jnp.zeros_like(rest)
        out_ref[1] = jnp.concatenate([blank, rest] if start else [rest, blank], 1)


def local_body(nx_total, ny_total, width_x, width_y, integers_ref, own_ref, out_ref, wide_ref, pick_strip_ref):
    pick_strip_ref[...] = select_strips(width_y)
    groups = wide_ref.shape[0]
    spread = spread_rows([own_ref[...]], groups, pick_strip_ref[...])[0]
    for g in range(groups):
        for py in range(2):
            wide_ref[g, py] = spread[g][py]
    modes = integers_ref.shape[1] - 2
    product = integers_ref[:, modes : modes + 1] * integers_ref[:, :modes]
    z_first = integers_ref[:, modes + 1 : modes + 2]
    x_first = lax.axis_index("gx") * width_x
    y_first = lax.axis_index("gy") * width_y
    half_x, half_y = width_x // 2, width_y // 2
    shift = (product & (QMCN - 1)).astype(F32) / QMCN - 0.5
    mode_row = iota((modes, modes), 0)
    mode_col = jnp.sum(jnp.where(mode_row == iota((modes, modes), 1), shift, 0.0), axis=1, keepdims=True)
    k = iota((modes, LANES), 0)
    lane = iota((modes, LANES), 1)
    k_f = k.astype(F32)
    amplitude = 1.2 / (1.0 + 0.5 * k_f) * mode_col
    z_local = lane // (2 * ROWS)
    px = (lane // ROWS) % 2
    r = lane % ROWS
    coarse_x = jnp.where(r < 8, r, r - ROWS)
    x = x_first + 2 * coarse_x + px
    x_angle = (x.astype(F32) + 0.5) * (math.pi / nx_total)
    z_angle = ((z_local + z_first).astype(F32) + 0.5) * (math.pi / NZG)
    phase = z_angle * (k % 5).astype(F32) + x_angle * (1 + k % 4).astype(F32) + 0.7 * k_f
    x_ok = (r < 8) | (r >= 12)
    ones = jnp.where(x_ok & (x >= 0) & (x < nx_total), 1.0, 0.0)
    left = jnp.concatenate([amplitude * jnp.cos(phase), -amplitude * jnp.sin(phase)], 0)
    inside_x = lax.dot_general(ones, jnp.ones((modes, LANES), F32), (((0,), (0,)), ((), ())), preferred_element_type=F32)
    y_mode = (1 + (k // 4) % 4).astype(F32)
    for py in range(2):
        coarse_y = jnp.where(lane < half_y + 4, lane, lane - LANES)
        y = y_first + 2 * coarse_y + py
        y_angle = (y.astype(F32) + 0.5) * (math.pi / ny_total) * y_mode
        right = jnp.concatenate([jnp.cos(y_angle), jnp.sin(y_angle)], 0)
        log_kappa = lax.dot_general(
            left, right, (((0,), (0,)), ((), ())), precision=lax.Precision.HIGHEST, preferred_element_type=F32
        )
        y_full = y[0:1, :]
        lane_full = lane[0:1, :]
        y_ok = (lane_full < half_y + 4) | (lane_full >= LANES - 4)
        y_ok = y_ok & (y_full >= 0) & (y_full < ny_total)
        value = jnp.where((inside_x > 0.5) & y_ok, jnp.exp(0.5 * log_kappa), 0.0)
        for group in range(8):
            out_ref[group // 2, group % 2, py] = value[group * ROWS : (group + 1) * ROWS]


def select_strips(width):
    half = width // 2
    strip = iota((4 * HALO, 2 * LANES), 0) % (2 * HALO)
    column = iota((4 * HALO, 2 * LANES), 1)
    parity, k = column // LANES, column % LANES
    k = jnp.where(k >= LANES - 4, k - LANES, k)
    even = lax.axis_index("gy") % 2 == 0
    below = strip % HALO - HALO
    fine = jnp.where((strip < HALO) == even, below + HALO + width, below)
    wanted = ((k < 0) | (k >= half)) & (k < half + 4)
    return jnp.where(wanted & (fine == 2 * k + parity), 1.0, 0.0).astype(BF16)


def halves_body(own_ref, out_ref):
    groups, _, width = own_ref.shape
    row, lane = iota((2 * width, LANES), 0) % width, iota((2 * width, LANES), 1)
    half = width // 2
    pick = jnp.where(row == 2 * (lane % half) + lane // half, 1.0, 0.0).astype(BF16)
    rows = two_parts(own_ref[...].reshape(groups * HALO, width), 1)
    spread = lax.dot_general(rows, pick, (((1,), (0,)), ((), ())), preferred_element_type=F32)
    out_ref[:groups] = spread.reshape(groups, HALO, LANES)


def spread_rows(blocks, groups, pick_strip):
    main, split = LANES // HALO, groups - LANES // HALO
    strips = [jnp.concatenate([block[groups], block[groups + 1]], 0) for block in blocks]
    for block in blocks:
        rest = block[groups + 2]
        strips.append(jnp.concatenate([rest[:, : split * HALO], rest[:, LANES // 2 : LANES // 2 + split * HALO]], 0))
    border = lax.dot_general(
        two_parts(jnp.concatenate(strips, 1), 0), pick_strip, (((0,), (0,)), ((), ())), preferred_element_type=F32
    )
    inner = iota((HALO, LANES), 1) < LANES // 2
    result = []
    for number, block in enumerate(blocks):
        first = [number * LANES + HALO * g for g in range(main)]
        first += [len(blocks) * LANES + number * split * HALO + HALO * g for g in range(split)]
        classes = []
        for g, row in enumerate(first):
            odd = pltpu.roll(block[g], LANES // 2, 1)
            classes.append(
                [
                    jnp.where(inner, values, border[row : row + HALO, LANES * py : LANES * (py + 1)])
                    for py, values in enumerate((block[g], odd))
                ]
            )
        result.append(classes)
    return result


class Lazy:
    def __init__(self, rule):
        self.rule, self.known = rule, {}

    def __call__(self, *key):
        if key not in self.known:
            self.known[key] = self.rule(*key)
        return self.known[key]


def plus(*terms):
    total = None
    for term in terms:
        if term is not None:
            total = term if total is None else total + term
    return total


def times(left, right):
    return None if left is None or right is None else left * right


def minus(left, right):
    if right is None:
        return left
    return -right if left is None else left - right


def tree_sum(terms):
    while len(terms) > 1:
        terms = [terms[k] + terms[k + 1] if k + 1 < len(terms) else terms[k] for k in range(0, len(terms), 2)]
    return terms[0]


def shift_x(value, steps):
    return None if value is None else pltpu.roll(value, (-steps) % ROWS, 0)


def shift_y(value, steps):
    return None if value is None else pltpu.roll(value, (-steps) % LANES, 1)


def main_body(
    field_ref,
    pick_strip_ref,
    own_ref,
    far_ref,
    near_ref,
    stencil_hbm,
    solution_hbm,
    wide_ref,
    stencil_ref,
    solution_ref,
    sems,
):
    groups = own_ref.shape[0]
    for g in range(groups):
        for py in range(2):
            wide_ref[g, py, 0:8, :] = own_ref[g, py]
            wide_ref[g, py, 16:24, :] = jnp.zeros((8, LANES), F32)
    above = lax.axis_index("gx") % 2 == 0
    near_place = pl.multiple_of(jnp.where(above, 8, 24), 8)
    far_place = pl.multiple_of(jnp.where(above, 24, 8), 8)
    spread = spread_rows([near_ref[...], far_ref[...]], groups, pick_strip_ref[...])
    for place, rows in zip((near_place, far_place), spread):
        for g in range(groups):
            for py in range(2):
                wide_ref[g, py, pl.ds(place, 8), :] = rows[g][py]

    planes = 2

    def base(kind, z, px, py):
        return wide_ref[field_start(kind, 2 * planes) + z, py, pl.ds(px, ROWS, stride=2), :]

    s = Lazy(lambda z, px, py: field_ref[z, px, py])

    def face(axis, z, px, py):
        here = s(z, px, py)
        if axis == "x":
            there = s(z, 1, py) if px == 0 else shift_x(s(z, 0, py), 1)
            return base(0, z, px, py) * (here * there)
        if axis == "y":
            there = s(z, px, 1) if py == 0 else shift_y(s(z, px, 0), 1)
            return base(1, z, px, py) * (here * there)
        if z < 0 or z + 1 >= 2 * planes:
            return None
        return base(2, z, px, py) * (here * s(z + 1, px, py))

    face = Lazy(face)
    mass = Lazy(lambda z, px, py: base(3, z, px, py) * (s(z, px, py) * s(z, px, py)))

    def pair(axis, z, px, py):
        if axis == "x":
            lower = face("x", z, 0, py) if px else shift_x(face("x", z, 1, py), -1)
        elif axis == "y":
            lower = face("y", z, px, 0) if py else shift_y(face("y", z, px, 1), -1)
        else:
            lower = face("z", z - 1, px, py)
        return plus(face(axis, z, px, py), lower)

    pair = Lazy(pair)

    def inverse(z, px, py):
        total = mass(z, px, py)
        for axis, odd in (("x", px), ("y", py), ("z", z % 2)):
            if odd:
                total = total + pair(axis, z, px, py)
        return 1.0 / jnp.where(s(z, px, py) > 0.0, total, 1.0)

    inverse = Lazy(inverse)

    def w_x(i, a):
        return None if not 0 <= i < planes else inverse(2 * i, 1, 0) * face("x", 2 * i, a, 0)

    def w_y(i, b):
        return None if not 0 <= i < planes else inverse(2 * i, 0, 1) * face("y", 2 * i, 0, b)

    def w_z(i, c):
        return times(inverse(2 * i + 1, 0, 0), face("z", 2 * i + c, 0, 0))

    w_x, w_y, w_z = Lazy(w_x), Lazy(w_y), Lazy(w_z)
    w_x_up = Lazy(lambda i, a: shift_y(w_x(i, a), 1))
    w_y_up = Lazy(lambda i, b: shift_x(w_y(i, b), 1))
    w_z_upx = Lazy(lambda i, c: shift_x(w_z(i, c), 1))
    w_z_upy = Lazy(lambda i, c: shift_y(w_z(i, c), 1))

    def w_xy(i, a, b):
        if not 0 <= i < planes:
            return None
        z = 2 * i
        return inverse(z, 1, 1) * (
            face("x", z, a, 1) * (w_y_up(i, b) if a else w_y(i, b)) + face("y", z, 1, b) * (w_x_up(i, a) if b else w_x(i, a))
        )

    def w_xz(i, a, c):
        z = 2 * i + 1
        return times(
            inverse(z, 1, 0),
            plus(times(face("x", z, a, 0), w_z_upx(i, c) if a else w_z(i, c)), times(face("z", 2 * i + c, 1, 0), w_x(i + c, a))),
        )

    def w_yz(i, b, c):
        z = 2 * i + 1
        return times(
            inverse(z, 0, 1),
            plus(times(face("y", z, 0, b), w_z_upy(i, c) if b else w_z(i, c)), times(face("z", 2 * i + c, 0, 1), w_y(i + c, b))),
        )

    w_xy, w_xz, w_yz = Lazy(w_xy), Lazy(w_xz), Lazy(w_yz)
    w_yz_up = Lazy(lambda i, b, c: shift_x(w_yz(i, b, c), 1))
    w_xz_up = Lazy(lambda i, a, c: shift_y(w_xz(i, a, c), 1))

    def w_xyz(i, a, b, c):
        z = 2 * i + 1
        if not 0 <= i < planes or not 0 <= i + c < planes:
            return None
        return inverse(z, 1, 1) * (
            face("x", z, a, 1) * (w_yz_up(i, b, c) if a else w_yz(i, b, c))
            + face("y", z, 1, b) * (w_xz_up(i, a, c) if b else w_xz(i, a, c))
            + face("z", 2 * i + c, 1, 1) * w_xy(i + c, a, b)
        )

    w_xyz = Lazy(w_xyz)

    low_x = Lazy(lambda i, b, c, a: shift_x(times(face("x", 2 * i + 1, 1, 1), w_xyz(i, a, b, c)), -1))
    low_y = Lazy(lambda i, a, c, b: shift_y(times(face("y", 2 * i + 1, 1, 1), w_xyz(i, a, b, c)), -1))

    def t_xy(i, a, b, dz):
        z = 2 * i
        row = None
        if dz == 0:
            row = times(pair("z", z, 1, 1), w_xy(i, a, b))
        if dz >= 0:
            row = minus(row, times(face("z", z, 1, 1), w_xyz(i, a, b, dz)))
        if dz <= 0:
            row = minus(row, times(face("z", z - 1, 1, 1), w_xyz(i - 1, a, b, dz + 1)))
        return minus(w_xy(i, a, b) if dz == 0 else None, times(inverse(z, 1, 1), row))

    def t_xz(i, a, c, dy):
        z = 2 * i + 1
        if not 0 <= i < planes or not 0 <= i + c < planes:
            return None
        row = None
        if dy == 0:
            row = times(pair("y", z, 1, 0), w_xz(i, a, c))
        if dy >= 0:
            row = minus(row, times(face("y", z, 1, 0), w_xyz(i, a, dy, c)))
        if dy <= 0:
            row = minus(row, low_y(i, a, c, dy + 1))
        return minus(w_xz(i, a, c) if dy == 0 else None, times(inverse(z, 1, 0), row))

    def t_yz(i, b, c, dx):
        z = 2 * i + 1
        if not 0 <= i < planes or not 0 <= i + c < planes:
            return None
        row = None
        if dx == 0:
            row = times(pair("x", z, 0, 1), w_yz(i, b, c))
        if dx >= 0:
            row = minus(row, times(face("x", z, 0, 1), w_xyz(i, dx, b, c)))
        if dx <= 0:
            row = minus(row, low_x(i, b, c, dx + 1))
        return minus(w_yz(i, b, c) if dx == 0 else None, times(inverse(z, 0, 1), row))

    t_xy, t_xz, t_yz = Lazy(t_xy), Lazy(t_xz), Lazy(t_yz)

    def t_x(i, a, dy, dz):
        z = 2 * i
        row = None
        if dy == 0 and dz == 0:
            row = plus(pair("y", z, 1, 0), pair("z", z, 1, 0)) * w_x(i, a)
        if dy >= 0:
            row = minus(row, times(face("y", z, 1, 0), t_xy(i, a, dy, dz)))
        if dy <= 0:
            row = minus(row, shift_y(times(face("y", z, 1, 1), t_xy(i, a, dy + 1, dz)), -1))
        if dz >= 0:
            row = minus(row, times(face("z", z, 1, 0), t_xz(i, a, dz, dy)))
        if dz <= 0:
            row = minus(row, times(face("z", z - 1, 1, 0), t_xz(i - 1, a, dz + 1, dy)))
        return minus(w_x(i, a) if dy == 0 and dz == 0 else None, times(inverse(z, 1, 0), row))

    def t_y(i, b, dx, dz):
        z = 2 * i
        row = None
        if dx == 0 and dz == 0:
            row = plus(pair("x", z, 0, 1), pair("z", z, 0, 1)) * w_y(i, b)
        if dx >= 0:
            row = minus(row, times(face("x", z, 0, 1), t_xy(i, dx, b, dz)))
        if dx <= 0:
            row = minus(row, shift_x(times(face("x", z, 1, 1), t_xy(i, dx + 1, b, dz)), -1))
        if dz >= 0:
            row = minus(row, times(face("z", z, 0, 1), t_yz(i, b, dz, dx)))
        if dz <= 0:
            row = minus(row, times(face("z", z - 1, 0, 1), t_yz(i - 1, b, dz + 1, dx)))
        return minus(w_y(i, b) if dx == 0 and dz == 0 else None, times(inverse(z, 0, 1), row))

    def t_z(i, c, dx, dy):
        z = 2 * i + 1
        if not 0 <= i < planes or not 0 <= i + c < planes:
            return None
        row = None
        if dx == 0 and dy == 0:
            row = plus(pair("x", z, 0, 0), pair("y", z, 0, 0)) * w_z(i, c)
        if dx >= 0:
            row = minus(row, times(face("x", z, 0, 0), t_xz(i, dx, c, dy)))
        if dx <= 0:
            row = minus(row, shift_x(times(face("x", z, 1, 0), t_xz(i, dx + 1, c, dy)), -1))
        if dy >= 0:
            row = minus(row, times(face("y", z, 0, 0), t_yz(i, dy, c, dx)))
        if dy <= 0:
            row = minus(row, shift_y(times(face("y", z, 0, 1), t_yz(i, dy + 1, c, dx)), -1))
        return minus(w_z(i, c) if dx == 0 and dy == 0 else None, times(inverse(z, 0, 0), row))

    t_x, t_y, t_z = Lazy(t_x), Lazy(t_y), Lazy(t_z)

    def direct(i, dz, dx, dy):
        z = 2 * i
        row = None
        if dx == 0 and dy == 0 and dz == 0:
            row = plus(mass(z, 0, 0), pair("x", z, 0, 0), pair("y", z, 0, 0), pair("z", z, 0, 0))
        if dx >= 0:
            row = minus(row, times(face("x", z, 0, 0), t_x(i, dx, dy, dz)))
        if dx <= 0:
            row = minus(row, shift_x(times(face("x", z, 1, 0), t_x(i, dx + 1, dy, dz)), -1))
        if dy >= 0:
            row = minus(row, times(face("y", z, 0, 0), t_y(i, dy, dx, dz)))
        if dy <= 0:
            row = minus(row, shift_y(times(face("y", z, 0, 1), t_y(i, dy + 1, dx, dz)), -1))
        if dz >= 0:
            row = minus(row, times(face("z", z, 0, 0), t_z(i, dz, dx, dy)))
        if dz <= 0:
            row = minus(row, times(face("z", z - 1, 0, 0), t_z(i - 1, dz + 1, dx, dy)))
        return row

    def coarse(i, dz, dx, dy):
        if not 0 <= i + dz < planes:
            return None
        if (dz, dx, dy) >= (0, 0, 0):
            return direct(i, dz, dx, dy)
        return shift_y(shift_x(coarse(i + dz, -dz, -dx, -dy), dx), dy)

    coarse = Lazy(coarse)

    resid = Lazy(lambda z, px, py: base(4, z, px, py))
    odd_z = range(planes)
    q_xyz = [inverse(2 * i + 1, 1, 1) * resid(2 * i + 1, 1, 1) for i in odd_z] + [None]
    q_xy, q_xz, q_yz, q_x, q_y, q_z, rhs = [], [], [], [], [], [], []

    def side_x(z, py, value):
        return plus(times(face("x", z, 0, py), value), shift_x(times(face("x", z, 1, py), value), -1))

    def side_y(z, px, value):
        return plus(times(face("y", z, px, 0), value), shift_y(times(face("y", z, px, 1), value), -1))

    def side_z(z, px, py, values):
        i = z // 2
        return plus(times(face("z", z, px, py), values[i]), times(face("z", z - 1, px, py), values[i - 1] if i else None))

    for i in range(planes):
        z = 2 * i
        q_xy.append(inverse(z, 1, 1) * plus(resid(z, 1, 1), side_z(z, 1, 1, q_xyz)))
        q_xz.append(inverse(z + 1, 1, 0) * plus(resid(z + 1, 1, 0), side_y(z + 1, 1, q_xyz[i])))
        q_yz.append(inverse(z + 1, 0, 1) * plus(resid(z + 1, 0, 1), side_x(z + 1, 1, q_xyz[i])))
    for i in range(planes):
        z = 2 * i
        q_x.append(inverse(z, 1, 0) * plus(resid(z, 1, 0), side_y(z, 1, q_xy[i]), side_z(z, 1, 0, q_xz)))
        q_y.append(inverse(z, 0, 1) * plus(resid(z, 0, 1), side_x(z, 1, q_xy[i]), side_z(z, 0, 1, q_yz)))
        q_z.append(
            inverse(z + 1, 0, 0) * plus(resid(z + 1, 0, 0), side_x(z + 1, 0, q_xz[i]), side_y(z + 1, 0, q_yz[i]))
        )
    for i in range(planes):
        z = 2 * i
        rhs.append(plus(resid(z, 0, 0), side_x(z, 0, q_x[i]), side_y(z, 0, q_y[i]), side_z(z, 0, 0, q_z)))

    keep_x, keep_y = stencil_ref.shape[2:]
    for i in range(planes):
        for dz in (-1, 0, 1):
            for dx in (-1, 0, 1):
                for dy in (-1, 0, 1):
                    value = coarse(i, dz, dx, dy)
                    number = 9 * (dz + 1) + 3 * (dx + 1) + dy + 1
                    if value is None:
                        stencil_ref[number, i] = jnp.zeros((keep_x, keep_y), F32)
                    else:
                        stencil_ref[number, i] = value[:keep_x, :keep_y]

    stencil_copy = pltpu.make_async_copy(stencil_ref, stencil_hbm, sems.at[0])
    stencil_copy.start()

    scaled = []
    for i in range(planes):
        inside = s(2 * i, 0, 0) > 0.0
        scaled.append(jnp.where(inside, OMEGA / jnp.where(inside, coarse(i, 0, 0, 0), 1.0), 0.0))
    near_row = {}
    for i in range(planes):
        for dz in range(-i, planes - i):
            for dy in (-1, 0, 1):
                near_row[i, dz, 0, dy] = coarse(i, dz, 0, dy)
                for dx in (-1, 1):
                    near_row[i, dz, dx, dy] = shift_x(coarse(i, dz, dx, dy), -dx)
    u = [scaled[i] * rhs[i] for i in range(planes)]
    for _ in range(SWEEPS - 1):
        moved = {(i, dy): shift_y(u[i], dy) if dy else u[i] for i in range(planes) for dy in (-1, 0, 1)}
        new = []
        for i in range(planes):
            sums = {}
            for dx in (-1, 0, 1):
                sums[dx] = tree_sum(
                    [near_row[i, dz, dx, dy] * moved[i + dz, dy] for dz in range(-i, planes - i) for dy in (-1, 0, 1)]
                )
            total = sums[0] + (shift_x(sums[1], 1) + shift_x(sums[-1], -1))
            new.append(u[i] + scaled[i] * (rhs[i] - total))
        u = new
    for i in range(planes):
        solution_ref[i] = u[i][:keep_x, :keep_y]
    solution_copy = pltpu.make_async_copy(solution_ref, solution_hbm, sems.at[1])
    solution_copy.start()
    stencil_copy.wait()
    solution_copy.wait()


def swap(value, axis, first, wrap):
    count = lax.axis_size(axis)
    partner = list(range(count))
    for i in range(first, count if wrap else count - 1, 2):
        partner[i], partner[(i + 1) % count] = (i + 1) % count, i
    return lax.ppermute(value, axis, list(enumerate(partner)))


def swap_x(value, first):
    nx, ny = lax.axis_size("gx"), lax.axis_size("gy")
    pairs = []
    for x in range(nx):
        other = x + 1 if x % 2 == first % 2 else x - 1
        for y in range(ny):
            target = (other, y) if 0 <= other < nx else (x, y + 1 if y % 2 == 0 else y - 1)
            pairs.append((x * ny + y, target[0] * ny + target[1]))
    return lax.ppermute(value, ("gx", "gy"), pairs)


def on_chip(value):
    return pltpu.with_memory_space_constraint(value, pltpu.VMEM)


def on_device(base_cond, base_mass, fine_residual, point_index, gen_vector, z_offset):
    plane_count, width_x, width_y = base_mass.shape
    nx_total = width_x * lax.axis_size("gx")
    ny_total = width_y * lax.axis_size("gy")
    vmem = pl.BlockSpec(memory_space=pltpu.VMEM)
    hbm = pl.BlockSpec(memory_space=pl.ANY)
    strip = pltpu.VMEM((2, HALO, LANES), F32)
    groups = field_start(5, plane_count)
    raw, near_y, far_y = pl.pallas_call(
        strips_body,
        out_shape=(pltpu.VMEM((groups, HALO, width_y), F32), strip, strip),
        in_specs=[hbm] * 3,
        out_specs=(vmem,) * 3,
        scratch_shapes=[pltpu.SemaphoreType.DMA((5,))],
        name="strips",
    )(base_cond, base_mass, fine_residual)
    far_y = swap(far_y, "gy", 1, True)
    near_y = swap(near_y, "gy", 0, False)
    own = pl.pallas_call(
        halves_body,
        out_shape=pltpu.VMEM((groups + 3, HALO, LANES), F32),
        in_specs=[vmem],
        out_specs=vmem,
        name="halves",
    )(on_chip(raw))
    own = lax.dynamic_update_slice(own, far_y[:1], (groups + 1, 0, 0))
    own = lax.dynamic_update_slice(own, near_y[:1], (groups, 0, 0))
    own = lax.dynamic_update_slice(own, far_y[1:] + near_y[1:], (groups + 2, 0, 0))
    point_index, z_offset, gen_vector, own = lax.optimization_barrier((point_index, z_offset, gen_vector, own))
    integers = jnp.concatenate([gen_vector, point_index, z_offset]).reshape(1, -1)
    field, wide, pick_strip = pl.pallas_call(
        lambda *refs: local_body(nx_total, ny_total, width_x, width_y, *refs),
        out_shape=(
            pltpu.VMEM((plane_count, 2, 2, ROWS, LANES), F32),
            pltpu.VMEM((groups, 2, HALO, LANES), F32),
            pltpu.VMEM((4 * HALO, 2 * LANES), BF16),
        ),
        in_specs=[vmem] * 2,
        out_specs=(vmem,) * 3,
        name="local",
    )(on_chip(integers), on_chip(own))
    far = swap_x(own, 1)
    near = swap_x(own, 0)
    coarse_block = (plane_count // 2, width_x // 2, width_y // 2)
    return pl.pallas_call(
        main_body,
        out_shape=(jax.ShapeDtypeStruct((27, *coarse_block), F32), jax.ShapeDtypeStruct(coarse_block, F32)),
        in_specs=[vmem] * 5,
        out_specs=(hbm, hbm),
        scratch_shapes=[
            pltpu.VMEM((groups, 2, 2 * ROWS, LANES), F32),
            pltpu.VMEM((27, *coarse_block), F32),
            pltpu.VMEM(coarse_block, F32),
            pltpu.SemaphoreType.DMA((2,)),
        ],
        name="galerkin",
    )(*[on_chip(value) for value in (field, pick_strip, wide, far, near)])


def solution(mesh):
    return jax.shard_map(
        on_device,
        mesh=mesh,
        in_specs=(
            P(None, None, "gx", "gy"),
            P(None, "gx", "gy"),
            P("parts", "gx", "gy"),
            P("parts"),
            P(),
            P(),
        ),
        out_specs=(P(None, "parts", "gx", "gy"), P("parts", "gx", "gy")),
        check_vma=False,
    )
```

```python
import itertools
import math

import jax
import jax.numpy as jnp
from jax import lax
from jax.experimental import pallas as pl
from jax.experimental.pallas import tpu as pltpu
from jax.sharding import PartitionSpec as P

NZG = 512
QMCN = 1048576
SWEEPS = 4
OMEGA = 0.6
ROWS = 16
LANES = 128
HALO = 8
F32 = jnp.float32
BF16 = jnp.bfloat16


def iota(shape, dim):
    return lax.broadcasted_iota(jnp.int32, shape, dim)


def two_parts(values, axis):
    high = values.astype(BF16)
    return jnp.concatenate([high, (values - high.astype(F32)).astype(BF16)], axis)


def field_start(kind, planes):
    return kind * planes - (1 if kind > 2 else 0)


def strips_body(cond_hbm, mass_hbm, resid_hbm, own_ref, near_ref, far_ref, sems):
    width = own_ref.shape[-1]
    planes = mass_hbm.shape[0]
    sources = [cond_hbm.at[0], cond_hbm.at[1], cond_hbm.at[2, : planes - 1], mass_hbm, resid_hbm]
    starts = [field_start(kind, planes) for kind in range(6)]
    copies = [
        pltpu.make_async_copy(source, own_ref.at[starts[kind] : starts[kind + 1]], sems.at[kind])
        for kind, source in enumerate(sources)
    ]
    for copy in copies:
        copy.start()
    even = lax.axis_index("gy") % 2 == 0
    row, lane = iota((2 * HALO, width), 0), iota((2 * HALO, width), 1)
    column = row % HALO + jnp.where((row < HALO) == even, width - HALO, 0)
    pick = jnp.where(lane == column, 1.0, 0.0).astype(BF16)
    for copy in copies:
        copy.wait()
    rows = own_ref[: starts[5]].reshape(-1, width)
    flip = rows.T
    low, high = flip[:HALO], flip[width - HALO :]
    taken = jnp.concatenate([jnp.where(even, high, low), jnp.where(even, low, high)], 0)
    for out_ref, start in ((near_ref, 0), (far_ref, 1)):
        part = taken[HALO * start : HALO * (start + 1)]
        out_ref[0] = part[:, :LANES]
        rest = jnp.concatenate([part[:, LANES:], jnp.zeros((HALO, 3 * LANES // 2 - part.shape[1]), F32)], 1)
        blank = jnp.zeros_like(rest)
        out_ref[1] = jnp.concatenate([blank, rest] if start else [rest, blank], 1)


def local_body(nx_total, ny_total, width_x, width_y, integers_ref, own_ref, out_ref, wide_ref, pick_strip_ref):
    pick_strip_ref[...] = select_strips(width_y)
    groups = wide_ref.shape[0]
    spread = spread_rows([own_ref[...]], groups, pick_strip_ref[...])[0]
    for g in range(groups):
        for py in range(2):
            wide_ref[g, py] = spread[g][py]
    modes = integers_ref.shape[1] - 2
    product = integers_ref[:, modes : modes + 1] * integers_ref[:, :modes]
    z_first = integers_ref[:, modes + 1 : modes + 2]
    x_first = lax.axis_index("gx") * width_x
    y_first = lax.axis_index("gy") * width_y
    half_x, half_y = width_x // 2, width_y // 2
    shift = (product & (QMCN - 1)).astype(F32) / QMCN - 0.5
    mode_row = iota((modes, modes), 0)
    mode_col = jnp.sum(jnp.where(mode_row == iota((modes, modes), 1), shift, 0.0), axis=1, keepdims=True)
    k = iota((modes, LANES), 0)
    lane = iota((modes, LANES), 1)
    k_f = k.astype(F32)
    amplitude = 1.2 / (1.0 + 0.5 * k_f) * mode_col
    z_local = lane // (2 * ROWS)
    px = (lane // ROWS) % 2
    r = lane % ROWS
    place = r % HALO
    coarse_x = 2 * jnp.where(place < 6, place, place - HALO) + r // HALO
    x = x_first + 2 * coarse_x + px
    x_angle = (x.astype(F32) + 0.5) * (math.pi / nx_total)
    z_angle = ((z_local + z_first).astype(F32) + 0.5) * (math.pi / NZG)
    phase = z_angle * (k % 5).astype(F32) + x_angle * (1 + k % 4).astype(F32) + 0.7 * k_f
    x_ok = (place < 4) | (place >= 6)
    ones = jnp.where(x_ok & (x >= 0) & (x < nx_total), 1.0, 0.0)
    left = jnp.concatenate([amplitude * jnp.cos(phase), -amplitude * jnp.sin(phase)], 0)
    inside_x = lax.dot_general(ones, jnp.ones((modes, LANES), F32), (((0,), (0,)), ((), ())), preferred_element_type=F32)
    y_mode = (1 + (k // 4) % 4).astype(F32)
    root = {}
    for py in range(2):
        coarse_y = jnp.where(lane < half_y + 4, lane, lane - LANES)
        y = y_first + 2 * coarse_y + py
        y_angle = (y.astype(F32) + 0.5) * (math.pi / ny_total) * y_mode
        right = jnp.concatenate([jnp.cos(y_angle), jnp.sin(y_angle)], 0)
        log_kappa = lax.dot_general(
            left, right, (((0,), (0,)), ((), ())), precision=lax.Precision.HIGHEST, preferred_element_type=F32
        )
        y_full = y[0:1, :]
        lane_full = lane[0:1, :]
        y_ok = (lane_full < half_y + 4) | (lane_full >= LANES - 4)
        y_ok = y_ok & (y_full >= 0) & (y_full < ny_total)
        value = jnp.where((inside_x > 0.5) & y_ok, jnp.exp(0.5 * log_kappa), 0.0)
        for group in range(8):
            root[group // 2, group % 2, py] = value[group * ROWS : (group + 1) * ROWS]
    planes = out_ref.shape[1]
    for (z, px, py), here in root.items():
        out_ref[0, z, px, py] = here * (shift_x(root[z, 0, py], 1) if px else root[z, 1, py])
        out_ref[1, z, px, py] = here * (shift_y(root[z, px, 0], 1) if py else root[z, px, 1])
        out_ref[2, z, px, py] = here * root[z + 1, px, py] if z + 1 < planes else jnp.zeros((ROWS, LANES), F32)
        out_ref[3, z, px, py] = here * here


def select_strips(width):
    half = width // 2
    strip = iota((4 * HALO, 2 * LANES), 0) % (2 * HALO)
    column = iota((4 * HALO, 2 * LANES), 1)
    parity, k = column // LANES, column % LANES
    k = jnp.where(k >= LANES - 4, k - LANES, k)
    even = lax.axis_index("gy") % 2 == 0
    below = strip % HALO - HALO
    fine = jnp.where((strip < HALO) == even, below + HALO + width, below)
    wanted = ((k < 0) | (k >= half)) & (k < half + 4)
    return jnp.where(wanted & (fine == 2 * k + parity), 1.0, 0.0).astype(BF16)


def halves_body(own_ref, out_ref):
    groups, _, width = own_ref.shape
    row, lane = iota((2 * width, LANES), 0) % width, iota((2 * width, LANES), 1)
    half = width // 2
    pick = jnp.where(row == 2 * (lane % half) + lane // half, 1.0, 0.0).astype(BF16)
    rows = two_parts(own_ref[...].reshape(groups * HALO, width), 1)
    spread = lax.dot_general(rows, pick, (((1,), (0,)), ((), ())), preferred_element_type=F32)
    out_ref[:groups] = spread.reshape(groups, HALO, LANES)


def spread_rows(blocks, groups, pick_strip):
    main, split = LANES // HALO, groups - LANES // HALO
    strips = [jnp.concatenate([block[groups], block[groups + 1]], 0) for block in blocks]
    for block in blocks:
        rest = block[groups + 2]
        strips.append(jnp.concatenate([rest[:, : split * HALO], rest[:, LANES // 2 : LANES // 2 + split * HALO]], 0))
    border = lax.dot_general(
        two_parts(jnp.concatenate(strips, 1), 0), pick_strip, (((0,), (0,)), ((), ())), preferred_element_type=F32
    )
    inner = iota((HALO, LANES), 1) < LANES // 2
    result = []
    for number, block in enumerate(blocks):
        first = [number * LANES + HALO * g for g in range(main)]
        first += [len(blocks) * LANES + number * split * HALO + HALO * g for g in range(split)]
        classes = []
        for g, row in enumerate(first):
            odd = pltpu.roll(block[g], LANES // 2, 1)
            classes.append(
                [
                    jnp.where(inner, values, border[row : row + HALO, LANES * py : LANES * (py + 1)])
                    for py, values in enumerate((block[g], odd))
                ]
            )
        result.append(classes)
    return result


class Lazy:
    def __init__(self, rule):
        self.rule, self.known = rule, {}

    def __call__(self, *key):
        if key not in self.known:
            self.known[key] = self.rule(*key)
        return self.known[key]


def plus(*terms):
    total = None
    for term in terms:
        if term is not None:
            total = term if total is None else total + term
    return total


def times(left, right):
    return None if left is None or right is None else left * right


def minus(left, right):
    if right is None:
        return left
    return -right if left is None else left - right


def tree_sum(terms):
    while len(terms) > 1:
        terms = [terms[k] + terms[k + 1] if k + 1 < len(terms) else terms[k] for k in range(0, len(terms), 2)]
    return terms[0]


def shift_x(value, steps):
    if value is None or steps == 0:
        return value
    even, odd = value[:HALO], value[HALO:]
    if steps > 0:
        return jnp.concatenate([odd, pltpu.roll(even, HALO - 1, 0)], 0)
    return jnp.concatenate([pltpu.roll(odd, 1, 0), even], 0)


def shift_y(value, steps):
    return value if value is None or steps == 0 else pltpu.roll(value, (-steps) % LANES, 1)


def main_body(
    factor_ref,
    pick_strip_ref,
    own_ref,
    far_ref,
    near_ref,
    stencil_hbm,
    solution_hbm,
    wide_ref,
    stencil_ref,
    solution_ref,
    sems,
):
    groups = own_ref.shape[0]
    for g in range(groups):
        for py in range(2):
            wide_ref[g, py, 0:8, :] = own_ref[g, py]
            wide_ref[g, py, 16:24, :] = jnp.zeros((8, LANES), F32)
    above = lax.axis_index("gx") % 2 == 0
    near_place = pl.multiple_of(jnp.where(above, 8, 24), 8)
    far_place = pl.multiple_of(jnp.where(above, 24, 8), 8)
    spread = spread_rows([near_ref[...], far_ref[...]], groups, pick_strip_ref[...])
    for place, rows in zip((near_place, far_place), spread):
        for g in range(groups):
            for py in range(2):
                wide_ref[g, py, pl.ds(place, 8), :] = rows[g][py]

    planes = 2

    def base(kind, z, px, py):
        group = field_start(kind, 2 * planes) + z
        tiles = [wide_ref[group, py, pl.ds(2 * odd + px, HALO, stride=4), :] for odd in range(2)]
        return jnp.concatenate(tiles, 0)

    def face(axis, z, px, py):
        kind = "xyz".index(axis)
        if kind == 2 and not 0 <= z < 2 * planes - 1:
            return None
        return base(kind, z, px, py) * factor_ref[kind, z, px, py]

    face = Lazy(face)
    mass = Lazy(lambda z, px, py: base(3, z, px, py) * factor_ref[3, z, px, py])

    def pair(axis, z, px, py):
        if axis == "x":
            lower = face("x", z, 0, py) if px else shift_x(face("x", z, 1, py), -1)
        elif axis == "y":
            lower = face("y", z, px, 0) if py else shift_y(face("y", z, px, 1), -1)
        else:
            lower = face("z", z - 1, px, py)
        return plus(face(axis, z, px, py), lower)

    pair = Lazy(pair)

    def inverse(z, px, py):
        total = mass(z, px, py)
        for axis, odd in (("x", px), ("y", py), ("z", z % 2)):
            if odd:
                total = total + pair(axis, z, px, py)
        return 1.0 / jnp.where(factor_ref[3, z, px, py] > 0.0, total, 1.0)

    inverse = Lazy(inverse)

    def w_x(i, a):
        return None if not 0 <= i < planes else inverse(2 * i, 1, 0) * face("x", 2 * i, a, 0)

    def w_y(i, b):
        return None if not 0 <= i < planes else inverse(2 * i, 0, 1) * face("y", 2 * i, 0, b)

    def w_z(i, c):
        return times(inverse(2 * i + 1, 0, 0), face("z", 2 * i + c, 0, 0))

    w_x, w_y, w_z = Lazy(w_x), Lazy(w_y), Lazy(w_z)
    w_x_up = Lazy(lambda i, a: shift_y(w_x(i, a), 1))
    w_y_up = Lazy(lambda i, b: shift_x(w_y(i, b), 1))
    w_z_upx = Lazy(lambda i, c: shift_x(w_z(i, c), 1))
    w_z_upy = Lazy(lambda i, c: shift_y(w_z(i, c), 1))

    def w_xy(i, a, b):
        if not 0 <= i < planes:
            return None
        z = 2 * i
        return inverse(z, 1, 1) * (
            face("x", z, a, 1) * (w_y_up(i, b) if a else w_y(i, b)) + face("y", z, 1, b) * (w_x_up(i, a) if b else w_x(i, a))
        )

    def w_xz(i, a, c):
        z = 2 * i + 1
        return times(
            inverse(z, 1, 0),
            plus(times(face("x", z, a, 0), w_z_upx(i, c) if a else w_z(i, c)), times(face("z", 2 * i + c, 1, 0), w_x(i + c, a))),
        )

    def w_yz(i, b, c):
        z = 2 * i + 1
        return times(
            inverse(z, 0, 1),
            plus(times(face("y", z, 0, b), w_z_upy(i, c) if b else w_z(i, c)), times(face("z", 2 * i + c, 0, 1), w_y(i + c, b))),
        )

    w_xy, w_xz, w_yz = Lazy(w_xy), Lazy(w_xz), Lazy(w_yz)
    w_yz_up = Lazy(lambda i, b, c: shift_x(w_yz(i, b, c), 1))
    w_xz_up = Lazy(lambda i, a, c: shift_y(w_xz(i, a, c), 1))

    def w_xyz(i, a, b, c):
        z = 2 * i + 1
        if not 0 <= i < planes or not 0 <= i + c < planes:
            return None
        return inverse(z, 1, 1) * (
            face("x", z, a, 1) * (w_yz_up(i, b, c) if a else w_yz(i, b, c))
            + face("y", z, 1, b) * (w_xz_up(i, a, c) if b else w_xz(i, a, c))
            + face("z", 2 * i + c, 1, 1) * w_xy(i + c, a, b)
        )

    w_xyz = Lazy(w_xyz)

    def weights_of(i, pz, px, py, moved=None):
        plain = {
            (0, 1, 0): lambda c, a, b: w_x(i, a),
            (0, 0, 1): lambda c, a, b: w_y(i, b),
            (1, 0, 0): lambda c, a, b: w_z(i, c),
            (0, 1, 1): lambda c, a, b: w_xy(i, a, b),
            (1, 1, 0): lambda c, a, b: w_xz(i, a, c),
            (1, 0, 1): lambda c, a, b: w_yz(i, b, c),
            (1, 1, 1): lambda c, a, b: w_xyz(i, a, b, c),
        }
        up_x = {
            (0, 0, 1): lambda c, a, b: w_y_up(i, b),
            (1, 0, 0): lambda c, a, b: w_z_upx(i, c),
            (1, 0, 1): lambda c, a, b: w_yz_up(i, b, c),
        }
        up_y = {
            (0, 1, 0): lambda c, a, b: w_x_up(i, a),
            (1, 0, 0): lambda c, a, b: w_z_upy(i, c),
            (1, 1, 0): lambda c, a, b: w_xz_up(i, a, c),
        }
        if (pz, px, py) == (0, 0, 0):
            return {(0, 0, 0): None}
        rule = {"x": up_x, "y": up_y, None: plain}[moved][pz, px, py]
        values = {(c, a, b): rule(c, a, b) for c in range(pz + 1) for a in range(px + 1) for b in range(py + 1)}
        return {sides: value for sides, value in values.items() if value is not None}

    parts = {}

    def keep(i, step, place, value):
        key = (i, *step, *place)
        parts[key] = plus(parts.get(key), value)

    for i in range(planes):
        keep(i, (0, 0, 0), (0, 0), mass(2 * i, 0, 0))
    for i, pz, px, py, axis, side in itertools.product(range(planes), (0, 1), (0, 1), (0, 1), "zxy", (0, 1)):
        parity = {"z": pz, "x": px, "y": py}
        if not parity[axis] or (axis == "z" and i + side >= planes):
            continue
        parity[axis] = 0
        lower = (parity["z"], parity["x"], parity["y"])
        offset = tuple(side if axis == name else 0 for name in "zxy")
        z = 2 * i + pz
        if axis == "z":
            here, joined = weights_of(i + side, *lower), face("z", 2 * i + side, px, py)
        elif axis == "x":
            here, joined = weights_of(i, *lower, "x" if side else None), face("x", z, side, py)
        else:
            here, joined = weights_of(i, *lower, "y" if side else None), face("y", z, px, side)
        there = weights_of(i, pz, px, py)
        drop = {}
        for column, value in there.items():
            own = tuple(at - by for at, by in zip(column, offset))
            drop[column] = -value
            if own in here:
                drop[column] = (1.0 if here[own] is None else here[own]) - value
        for sides, value in here.items():
            row = tuple(at + by for at, by in zip(sides, offset))
            scaled_row = joined if value is None else joined * value
            for column, change in drop.items():
                step = tuple(to - at for to, at in zip(column, row))
                if step >= (0, 0, 0):
                    keep(i + row[0], step, row[1:], scaled_row * change)

    def direct(i, dz, dx, dy):
        low, high = (
            plus(parts.get((i, dz, dx, dy, 0, side)), shift_x(parts.get((i, dz, dx, dy, 1, side)), -1)) for side in (0, 1)
        )
        return plus(low, shift_y(high, -1))

    def coarse(i, dz, dx, dy):
        if not 0 <= i + dz < planes:
            return None
        if (dz, dx, dy) >= (0, 0, 0):
            return direct(i, dz, dx, dy)
        return shift_y(shift_x(coarse(i + dz, -dz, -dx, -dy), dx), dy)

    coarse = Lazy(coarse)

    resid = Lazy(lambda z, px, py: base(4, z, px, py))
    odd_z = range(planes)
    q_xyz = [inverse(2 * i + 1, 1, 1) * resid(2 * i + 1, 1, 1) for i in odd_z] + [None]
    q_xy, q_xz, q_yz, q_x, q_y, q_z, rhs = [], [], [], [], [], [], []

    def side_x(z, py, value):
        return plus(times(face("x", z, 0, py), value), shift_x(times(face("x", z, 1, py), value), -1))

    def side_y(z, px, value):
        return plus(times(face("y", z, px, 0), value), shift_y(times(face("y", z, px, 1), value), -1))

    def side_z(z, px, py, values):
        i = z // 2
        return plus(times(face("z", z, px, py), values[i]), times(face("z", z - 1, px, py), values[i - 1] if i else None))

    for i in range(planes):
        z = 2 * i
        q_xy.append(inverse(z, 1, 1) * plus(resid(z, 1, 1), side_z(z, 1, 1, q_xyz)))
        q_xz.append(inverse(z + 1, 1, 0) * plus(resid(z + 1, 1, 0), side_y(z + 1, 1, q_xyz[i])))
        q_yz.append(inverse(z + 1, 0, 1) * plus(resid(z + 1, 0, 1), side_x(z + 1, 1, q_xyz[i])))
    for i in range(planes):
        z = 2 * i
        q_x.append(inverse(z, 1, 0) * plus(resid(z, 1, 0), side_y(z, 1, q_xy[i]), side_z(z, 1, 0, q_xz)))
        q_y.append(inverse(z, 0, 1) * plus(resid(z, 0, 1), side_x(z, 1, q_xy[i]), side_z(z, 0, 1, q_yz)))
        q_z.append(
            inverse(z + 1, 0, 0) * plus(resid(z + 1, 0, 0), side_x(z + 1, 0, q_xz[i]), side_y(z + 1, 0, q_yz[i]))
        )
    for i in range(planes):
        z = 2 * i
        rhs.append(plus(resid(z, 0, 0), side_x(z, 0, q_x[i]), side_y(z, 0, q_y[i]), side_z(z, 0, 0, q_z)))

    keep_x, keep_y = stencil_ref.shape[2:]
    for i in range(planes):
        for dz in (-1, 0, 1):
            for dx in (-1, 0, 1):
                for dy in (-1, 0, 1):
                    value = coarse(i, dz, dx, dy)
                    number = 9 * (dz + 1) + 3 * (dx + 1) + dy + 1
                    if value is None:
                        stencil_ref[number, i] = jnp.zeros((keep_x, keep_y), F32)
                    else:
                        for odd in range(2):
                            rows = value[HALO * odd : HALO * odd + keep_x // 2, :keep_y]
                            stencil_ref[number, i, pl.ds(odd, keep_x // 2, stride=2), :] = rows

    stencil_copy = pltpu.make_async_copy(stencil_ref, stencil_hbm, sems.at[0])
    stencil_copy.start()

    scaled = []
    for i in range(planes):
        inside = factor_ref[3, 2 * i, 0, 0] > 0.0
        scaled.append(jnp.where(inside, OMEGA / jnp.where(inside, coarse(i, 0, 0, 0), 1.0), 0.0))
    near_row = {}
    for i in range(planes):
        for dz in range(-i, planes - i):
            for dy in (-1, 0, 1):
                near_row[i, dz, 0, dy] = coarse(i, dz, 0, dy)
                for dx in (-1, 1):
                    near_row[i, dz, dx, dy] = shift_x(coarse(i, dz, dx, dy), -dx)
    u = [scaled[i] * rhs[i] for i in range(planes)]
    for _ in range(SWEEPS - 1):
        moved = {(i, dy): shift_y(u[i], dy) if dy else u[i] for i in range(planes) for dy in (-1, 0, 1)}
        new = []
        for i in range(planes):
            sums = {}
            for dx in (-1, 0, 1):
                sums[dx] = tree_sum(
                    [near_row[i, dz, dx, dy] * moved[i + dz, dy] for dz in range(-i, planes - i) for dy in (-1, 0, 1)]
                )
            total = sums[0] + (shift_x(sums[1], 1) + shift_x(sums[-1], -1))
            new.append(u[i] + scaled[i] * (rhs[i] - total))
        u = new
    for i in range(planes):
        for odd in range(2):
            rows = u[i][HALO * odd : HALO * odd + keep_x // 2, :keep_y]
            solution_ref[i, pl.ds(odd, keep_x // 2, stride=2), :] = rows
    solution_copy = pltpu.make_async_copy(solution_ref, solution_hbm, sems.at[1])
    solution_copy.start()
    stencil_copy.wait()
    solution_copy.wait()


def swap(value, axis, first, wrap):
    count = lax.axis_size(axis)
    partner = list(range(count))
    for i in range(first, count if wrap else count - 1, 2):
        partner[i], partner[(i + 1) % count] = (i + 1) % count, i
    return lax.ppermute(value, axis, list(enumerate(partner)))


def swap_x(value, first):
    nx, ny = lax.axis_size("gx"), lax.axis_size("gy")
    pairs = []
    for x in range(nx):
        other = x + 1 if x % 2 == first % 2 else x - 1
        for y in range(ny):
            target = (other, y) if 0 <= other < nx else (x, y + 1 if y % 2 == 0 else y - 1)
            pairs.append((x * ny + y, target[0] * ny + target[1]))
    return lax.ppermute(value, ("gx", "gy"), pairs)


def on_chip(value):
    return pltpu.with_memory_space_constraint(value, pltpu.VMEM)


def on_device(base_cond, base_mass, fine_residual, point_index, gen_vector, z_offset):
    plane_count, width_x, width_y = base_mass.shape
    nx_total = width_x * lax.axis_size("gx")
    ny_total = width_y * lax.axis_size("gy")
    vmem = pl.BlockSpec(memory_space=pltpu.VMEM)
    hbm = pl.BlockSpec(memory_space=pl.ANY)
    strip = pltpu.VMEM((2, HALO, LANES), F32)
    groups = field_start(5, plane_count)
    raw, near_y, far_y = pl.pallas_call(
        strips_body,
        out_shape=(pltpu.VMEM((groups, HALO, width_y), F32), strip, strip),
        in_specs=[hbm] * 3,
        out_specs=(vmem,) * 3,
        scratch_shapes=[pltpu.SemaphoreType.DMA((5,))],
        name="strips",
    )(base_cond, base_mass, fine_residual)
    far_y = swap(far_y, "gy", 1, True)
    near_y = swap(near_y, "gy", 0, False)
    own = pl.pallas_call(
        halves_body,
        out_shape=pltpu.VMEM((groups + 3, HALO, LANES), F32),
        in_specs=[vmem],
        out_specs=vmem,
        name="halves",
    )(on_chip(raw))
    own = lax.dynamic_update_slice(own, far_y[:1], (groups + 1, 0, 0))
    own = lax.dynamic_update_slice(own, near_y[:1], (groups, 0, 0))
    own = lax.dynamic_update_slice(own, far_y[1:] + near_y[1:], (groups + 2, 0, 0))
    point_index, z_offset, gen_vector, own = lax.optimization_barrier((point_index, z_offset, gen_vector, own))
    integers = jnp.concatenate([gen_vector, point_index, z_offset]).reshape(1, -1)
    factors, wide, pick_strip = pl.pallas_call(
        lambda *refs: local_body(nx_total, ny_total, width_x, width_y, *refs),
        out_shape=(
            pltpu.VMEM((4, plane_count, 2, 2, ROWS, LANES), F32),
            pltpu.VMEM((groups, 2, HALO, LANES), F32),
            pltpu.VMEM((4 * HALO, 2 * LANES), BF16),
        ),
        in_specs=[vmem] * 2,
        out_specs=(vmem,) * 3,
        name="local",
    )(on_chip(integers), on_chip(own))
    far = swap_x(own, 1)
    near = swap_x(own, 0)
    coarse_block = (plane_count // 2, width_x // 2, width_y // 2)
    return pl.pallas_call(
        main_body,
        out_shape=(jax.ShapeDtypeStruct((27, *coarse_block), F32), jax.ShapeDtypeStruct(coarse_block, F32)),
        in_specs=[vmem] * 5,
        out_specs=(hbm, hbm),
        scratch_shapes=[
            pltpu.VMEM((groups, 2, 2 * ROWS, LANES), F32),
            pltpu.VMEM((27, *coarse_block), F32),
            pltpu.VMEM(coarse_block, F32),
            pltpu.SemaphoreType.DMA((2,)),
        ],
        name="galerkin",
    )(*[on_chip(value) for value in (factors, pick_strip, wide, far, near)])


def solution(mesh):
    return jax.shard_map(
        on_device,
        mesh=mesh,
        in_specs=(
            P(None, None, "gx", "gy"),
            P(None, "gx", "gy"),
            P("parts", "gx", "gy"),
            P("parts"),
            P(),
            P(),
        ),
        out_specs=(P(None, "parts", "gx", "gy"), P("parts", "gx", "gy")),
        check_vma=False,
    )
```

```python
import itertools
import math

import jax
import jax.numpy as jnp
from jax import lax
from jax.experimental import pallas as pl
from jax.experimental.pallas import tpu as pltpu
from jax.sharding import PartitionSpec as P

NZG = 512
QMCN = 1048576
SWEEPS = 4
OMEGA = 0.6
ROWS = 16
LANES = 128
HALO = 8
F32 = jnp.float32
BF16 = jnp.bfloat16


def iota(shape, dim):
    return lax.broadcasted_iota(jnp.int32, shape, dim)


def two_parts(values, axis):
    high = values.astype(BF16)
    return jnp.concatenate([high, (values - high.astype(F32)).astype(BF16)], axis)


def field_start(kind, planes):
    return kind * planes - (1 if kind > 2 else 0)


def strips_body(cond_hbm, mass_hbm, resid_hbm, own_ref, near_ref, far_ref, sems):
    width = own_ref.shape[-1]
    planes = mass_hbm.shape[0]
    sources = [cond_hbm.at[0], cond_hbm.at[1], cond_hbm.at[2, : planes - 1], mass_hbm, resid_hbm]
    starts = [field_start(kind, planes) for kind in range(6)]
    copies = [
        pltpu.make_async_copy(source, own_ref.at[starts[kind] : starts[kind + 1]], sems.at[kind])
        for kind, source in enumerate(sources)
    ]
    for copy in copies:
        copy.start()
    even = lax.axis_index("gy") % 2 == 0
    row, lane = iota((2 * HALO, width), 0), iota((2 * HALO, width), 1)
    column = row % HALO + jnp.where((row < HALO) == even, width - HALO, 0)
    pick = jnp.where(lane == column, 1.0, 0.0).astype(BF16)
    for copy in copies:
        copy.wait()
    rows = own_ref[: starts[5]].reshape(-1, width)
    flip = rows.T
    low, high = flip[:HALO], flip[width - HALO :]
    taken = jnp.concatenate([jnp.where(even, high, low), jnp.where(even, low, high)], 0)
    for out_ref, start in ((near_ref, 0), (far_ref, 1)):
        part = taken[HALO * start : HALO * (start + 1)]
        out_ref[0] = part[:, :LANES]
        rest = jnp.concatenate([part[:, LANES:], jnp.zeros((HALO, 3 * LANES // 2 - part.shape[1]), F32)], 1)
        blank = jnp.zeros_like(rest)
        out_ref[1] = jnp.concatenate([blank, rest] if start else [rest, blank], 1)


def local_body(nx_total, ny_total, width_x, width_y, integers_ref, own_ref, out_ref, wide_ref, pick_strip_ref):
    pick_strip_ref[...] = select_strips(width_y)
    groups = wide_ref.shape[0]
    spread = spread_rows([own_ref[...]], groups, pick_strip_ref[...])[0]
    for g in range(groups):
        for py in range(2):
            wide_ref[g, py] = spread[g][py]
    modes = integers_ref.shape[1] - 2
    product = integers_ref[:, modes : modes + 1] * integers_ref[:, :modes]
    z_first = integers_ref[:, modes + 1 : modes + 2]
    x_first = lax.axis_index("gx") * width_x
    y_first = lax.axis_index("gy") * width_y
    half_x, half_y = width_x // 2, width_y // 2
    shift = (product & (QMCN - 1)).astype(F32) / QMCN - 0.5
    mode_row = iota((modes, modes), 0)
    mode_col = jnp.sum(jnp.where(mode_row == iota((modes, modes), 1), shift, 0.0), axis=1, keepdims=True)
    k = iota((modes, LANES), 0)
    lane = iota((modes, LANES), 1)
    k_f = k.astype(F32)
    amplitude = 1.2 / (1.0 + 0.5 * k_f) * mode_col
    z_local = lane // (2 * ROWS)
    px = (lane // ROWS) % 2
    r = lane % ROWS
    place = r % HALO
    coarse_x = 2 * jnp.where(place < 6, place, place - HALO) + r // HALO
    x = x_first + 2 * coarse_x + px
    x_angle = (x.astype(F32) + 0.5) * (math.pi / nx_total)
    z_angle = ((z_local + z_first).astype(F32) + 0.5) * (math.pi / NZG)
    phase = z_angle * (k % 5).astype(F32) + x_angle * (1 + k % 4).astype(F32) + 0.7 * k_f
    x_ok = (place < 4) | (place >= 6)
    ones = jnp.where(x_ok & (x >= 0) & (x < nx_total), 1.0, 0.0)
    left = jnp.concatenate([amplitude * jnp.cos(phase), -amplitude * jnp.sin(phase)], 0)
    inside_x = lax.dot_general(ones, jnp.ones((modes, LANES), F32), (((0,), (0,)), ((), ())), preferred_element_type=F32)
    y_mode = (1 + (k // 4) % 4).astype(F32)
    root = {}
    for py in range(2):
        coarse_y = jnp.where(lane < half_y + 4, lane, lane - LANES)
        y = y_first + 2 * coarse_y + py
        y_angle = (y.astype(F32) + 0.5) * (math.pi / ny_total) * y_mode
        right = jnp.concatenate([jnp.cos(y_angle), jnp.sin(y_angle)], 0)
        log_kappa = lax.dot_general(
            left, right, (((0,), (0,)), ((), ())), precision=lax.Precision.HIGHEST, preferred_element_type=F32
        )
        y_full = y[0:1, :]
        lane_full = lane[0:1, :]
        y_ok = (lane_full < half_y + 4) | (lane_full >= LANES - 4)
        y_ok = y_ok & (y_full >= 0) & (y_full < ny_total)
        value = jnp.where((inside_x > 0.5) & y_ok, jnp.exp(0.5 * log_kappa), 0.0)
        for group in range(8):
            root[group // 2, group % 2, py] = value[group * ROWS : (group + 1) * ROWS]
    planes = out_ref.shape[1]
    for (z, px, py), here in root.items():
        out_ref[0, z, px, py] = here * (shift_x(root[z, 0, py], 1) if px else root[z, 1, py])
        out_ref[1, z, px, py] = here * (shift_y(root[z, px, 0], 1) if py else root[z, px, 1])
        out_ref[2, z, px, py] = here * root[z + 1, px, py] if z + 1 < planes else jnp.zeros((ROWS, LANES), F32)
        out_ref[3, z, px, py] = here * here


def select_strips(width):
    half = width // 2
    strip = iota((4 * HALO, 2 * LANES), 0) % (2 * HALO)
    column = iota((4 * HALO, 2 * LANES), 1)
    parity, k = column // LANES, column % LANES
    k = jnp.where(k >= LANES - 4, k - LANES, k)
    even = lax.axis_index("gy") % 2 == 0
    below = strip % HALO - HALO
    fine = jnp.where((strip < HALO) == even, below + HALO + width, below)
    wanted = ((k < 0) | (k >= half)) & (k < half + 4)
    return jnp.where(wanted & (fine == 2 * k + parity), 1.0, 0.0).astype(BF16)


def halves_body(own_ref, out_ref):
    groups, _, width = own_ref.shape
    row, lane = iota((2 * width, LANES), 0) % width, iota((2 * width, LANES), 1)
    half = width // 2
    pick = jnp.where(row == 2 * (lane % half) + lane // half, 1.0, 0.0).astype(BF16)
    rows = two_parts(own_ref[...].reshape(groups * HALO, width), 1)
    spread = lax.dot_general(rows, pick, (((1,), (0,)), ((), ())), preferred_element_type=F32)
    out_ref[:groups] = spread.reshape(groups, HALO, LANES)


def spread_rows(blocks, groups, pick_strip):
    main, split = LANES // HALO, groups - LANES // HALO
    strips = [jnp.concatenate([block[groups], block[groups + 1]], 0) for block in blocks]
    for block in blocks:
        rest = block[groups + 2]
        strips.append(jnp.concatenate([rest[:, : split * HALO], rest[:, LANES // 2 : LANES // 2 + split * HALO]], 0))
    border = lax.dot_general(
        two_parts(jnp.concatenate(strips, 1), 0), pick_strip, (((0,), (0,)), ((), ())), preferred_element_type=F32
    )
    inner = iota((HALO, LANES), 1) < LANES // 2
    result = []
    for number, block in enumerate(blocks):
        first = [number * LANES + HALO * g for g in range(main)]
        first += [len(blocks) * LANES + number * split * HALO + HALO * g for g in range(split)]
        classes = []
        for g, row in enumerate(first):
            odd = pltpu.roll(block[g], LANES // 2, 1)
            classes.append(
                [
                    jnp.where(inner, values, border[row : row + HALO, LANES * py : LANES * (py + 1)])
                    for py, values in enumerate((block[g], odd))
                ]
            )
        result.append(classes)
    return result


class Lazy:
    def __init__(self, rule):
        self.rule, self.known = rule, {}

    def __call__(self, *key):
        if key not in self.known:
            self.known[key] = self.rule(*key)
        return self.known[key]


def plus(*terms):
    total = None
    for term in terms:
        if term is not None:
            total = term if total is None else total + term
    return total


def times(left, right):
    return None if left is None or right is None else left * right


def minus(left, right):
    if right is None:
        return left
    return -right if left is None else left - right


def tree_sum(terms):
    while len(terms) > 1:
        terms = [terms[k] + terms[k + 1] if k + 1 < len(terms) else terms[k] for k in range(0, len(terms), 2)]
    return terms[0]


def shift_x(value, steps):
    if value is None or steps == 0:
        return value
    even, odd = value[:HALO], value[HALO:]
    if steps > 0:
        return jnp.concatenate([odd, pltpu.roll(even, HALO - 1, 0)], 0)
    return jnp.concatenate([pltpu.roll(odd, 1, 0), even], 0)


def shift_y(value, steps):
    return value if value is None or steps == 0 else pltpu.roll(value, (-steps) % LANES, 1)


def main_body(
    factor_ref,
    pick_strip_ref,
    own_ref,
    last_ref,
    far_ref,
    first_ref,
    stencil_hbm,
    solution_hbm,
    wide_ref,
    stencil_ref,
    solution_ref,
    sems,
):
    groups = own_ref.shape[0]
    for g in range(groups):
        for py in range(2):
            wide_ref[g, py, 0:8, :] = own_ref[g, py]
            wide_ref[g, py, 16:24, :] = jnp.zeros((8, LANES), F32)
    above = lax.axis_index("gx") % 2 == 0
    near_place = pl.multiple_of(jnp.where(above, 8, 24), 8)
    far_place = pl.multiple_of(jnp.where(above, 24, 8), 8)
    near = jnp.where(lax.axis_index("gx") % 4 < 2, first_ref[...], last_ref[...])
    spread = spread_rows([near, far_ref[...]], groups, pick_strip_ref[...])
    for place, rows in zip((near_place, far_place), spread):
        for g in range(groups):
            for py in range(2):
                wide_ref[g, py, pl.ds(place, 8), :] = rows[g][py]

    planes = 2

    def base(kind, z, px, py):
        group = field_start(kind, 2 * planes) + z
        tiles = [wide_ref[group, py, pl.ds(2 * odd + px, HALO, stride=4), :] for odd in range(2)]
        return jnp.concatenate(tiles, 0)

    def face(axis, z, px, py):
        kind = "xyz".index(axis)
        if kind == 2 and not 0 <= z < 2 * planes - 1:
            return None
        return base(kind, z, px, py) * factor_ref[kind, z, px, py]

    face = Lazy(face)
    mass = Lazy(lambda z, px, py: base(3, z, px, py) * factor_ref[3, z, px, py])

    def pair(axis, z, px, py):
        if axis == "x":
            lower = face("x", z, 0, py) if px else shift_x(face("x", z, 1, py), -1)
        elif axis == "y":
            lower = face("y", z, px, 0) if py else shift_y(face("y", z, px, 1), -1)
        else:
            lower = face("z", z - 1, px, py)
        return plus(face(axis, z, px, py), lower)

    pair = Lazy(pair)

    def inverse(z, px, py):
        total = mass(z, px, py)
        for axis, odd in (("x", px), ("y", py), ("z", z % 2)):
            if odd:
                total = total + pair(axis, z, px, py)
        return 1.0 / jnp.where(factor_ref[3, z, px, py] > 0.0, total, 1.0)

    inverse = Lazy(inverse)

    def w_x(i, a):
        return None if not 0 <= i < planes else inverse(2 * i, 1, 0) * face("x", 2 * i, a, 0)

    def w_y(i, b):
        return None if not 0 <= i < planes else inverse(2 * i, 0, 1) * face("y", 2 * i, 0, b)

    def w_z(i, c):
        return times(inverse(2 * i + 1, 0, 0), face("z", 2 * i + c, 0, 0))

    w_x, w_y, w_z = Lazy(w_x), Lazy(w_y), Lazy(w_z)
    w_x_up = Lazy(lambda i, a: shift_y(w_x(i, a), 1))
    w_y_up = Lazy(lambda i, b: shift_x(w_y(i, b), 1))
    w_z_upx = Lazy(lambda i, c: shift_x(w_z(i, c), 1))
    w_z_upy = Lazy(lambda i, c: shift_y(w_z(i, c), 1))

    def w_xy(i, a, b):
        if not 0 <= i < planes:
            return None
        z = 2 * i
        return inverse(z, 1, 1) * (
            face("x", z, a, 1) * (w_y_up(i, b) if a else w_y(i, b)) + face("y", z, 1, b) * (w_x_up(i, a) if b else w_x(i, a))
        )

    def w_xz(i, a, c):
        z = 2 * i + 1
        return times(
            inverse(z, 1, 0),
            plus(times(face("x", z, a, 0), w_z_upx(i, c) if a else w_z(i, c)), times(face("z", 2 * i + c, 1, 0), w_x(i + c, a))),
        )

    def w_yz(i, b, c):
        z = 2 * i + 1
        return times(
            inverse(z, 0, 1),
            plus(times(face("y", z, 0, b), w_z_upy(i, c) if b else w_z(i, c)), times(face("z", 2 * i + c, 0, 1), w_y(i + c, b))),
        )

    w_xy, w_xz, w_yz = Lazy(w_xy), Lazy(w_xz), Lazy(w_yz)
    w_yz_up = Lazy(lambda i, b, c: shift_x(w_yz(i, b, c), 1))
    w_xz_up = Lazy(lambda i, a, c: shift_y(w_xz(i, a, c), 1))

    def w_xyz(i, a, b, c):
        z = 2 * i + 1
        if not 0 <= i < planes or not 0 <= i + c < planes:
            return None
        return inverse(z, 1, 1) * (
            face("x", z, a, 1) * (w_yz_up(i, b, c) if a else w_yz(i, b, c))
            + face("y", z, 1, b) * (w_xz_up(i, a, c) if b else w_xz(i, a, c))
            + face("z", 2 * i + c, 1, 1) * w_xy(i + c, a, b)
        )

    w_xyz = Lazy(w_xyz)

    def weights_of(i, pz, px, py, moved=None):
        plain = {
            (0, 1, 0): lambda c, a, b: w_x(i, a),
            (0, 0, 1): lambda c, a, b: w_y(i, b),
            (1, 0, 0): lambda c, a, b: w_z(i, c),
            (0, 1, 1): lambda c, a, b: w_xy(i, a, b),
            (1, 1, 0): lambda c, a, b: w_xz(i, a, c),
            (1, 0, 1): lambda c, a, b: w_yz(i, b, c),
            (1, 1, 1): lambda c, a, b: w_xyz(i, a, b, c),
        }
        up_x = {
            (0, 0, 1): lambda c, a, b: w_y_up(i, b),
            (1, 0, 0): lambda c, a, b: w_z_upx(i, c),
            (1, 0, 1): lambda c, a, b: w_yz_up(i, b, c),
        }
        up_y = {
            (0, 1, 0): lambda c, a, b: w_x_up(i, a),
            (1, 0, 0): lambda c, a, b: w_z_upy(i, c),
            (1, 1, 0): lambda c, a, b: w_xz_up(i, a, c),
        }
        if (pz, px, py) == (0, 0, 0):
            return {(0, 0, 0): None}
        rule = {"x": up_x, "y": up_y, None: plain}[moved][pz, px, py]
        values = {(c, a, b): rule(c, a, b) for c in range(pz + 1) for a in range(px + 1) for b in range(py + 1)}
        return {sides: value for sides, value in values.items() if value is not None}

    parts = {}

    def keep(i, step, place, value):
        key = (i, *step, *place)
        parts[key] = plus(parts.get(key), value)

    for i in range(planes):
        keep(i, (0, 0, 0), (0, 0), mass(2 * i, 0, 0))
    for i, pz, px, py, axis, side in itertools.product(range(planes), (0, 1), (0, 1), (0, 1), "zxy", (0, 1)):
        parity = {"z": pz, "x": px, "y": py}
        if not parity[axis] or (axis == "z" and i + side >= planes):
            continue
        parity[axis] = 0
        lower = (parity["z"], parity["x"], parity["y"])
        offset = tuple(side if axis == name else 0 for name in "zxy")
        z = 2 * i + pz
        if axis == "z":
            here, joined = weights_of(i + side, *lower), face("z", 2 * i + side, px, py)
        elif axis == "x":
            here, joined = weights_of(i, *lower, "x" if side else None), face("x", z, side, py)
        else:
            here, joined = weights_of(i, *lower, "y" if side else None), face("y", z, px, side)
        there = weights_of(i, pz, px, py)
        drop = {}
        for column, value in there.items():
            own = tuple(at - by for at, by in zip(column, offset))
            drop[column] = -value
            if own in here:
                drop[column] = (1.0 if here[own] is None else here[own]) - value
        for sides, value in here.items():
            row = tuple(at + by for at, by in zip(sides, offset))
            scaled_row = joined if value is None else joined * value
            for column, change in drop.items():
                step = tuple(to - at for to, at in zip(column, row))
                if step >= (0, 0, 0):
                    keep(i + row[0], step, row[1:], scaled_row * change)

    def direct(i, dz, dx, dy):
        low, high = (
            plus(parts.get((i, dz, dx, dy, 0, side)), shift_x(parts.get((i, dz, dx, dy, 1, side)), -1)) for side in (0, 1)
        )
        return plus(low, shift_y(high, -1))

    def coarse(i, dz, dx, dy):
        if not 0 <= i + dz < planes:
            return None
        if (dz, dx, dy) >= (0, 0, 0):
            return direct(i, dz, dx, dy)
        return shift_y(shift_x(coarse(i + dz, -dz, -dx, -dy), dx), dy)

    coarse = Lazy(coarse)

    resid = Lazy(lambda z, px, py: base(4, z, px, py))
    odd_z = range(planes)
    q_xyz = [inverse(2 * i + 1, 1, 1) * resid(2 * i + 1, 1, 1) for i in odd_z] + [None]
    q_xy, q_xz, q_yz, q_x, q_y, q_z, rhs = [], [], [], [], [], [], []

    def side_x(z, py, value):
        return plus(times(face("x", z, 0, py), value), shift_x(times(face("x", z, 1, py), value), -1))

    def side_y(z, px, value):
        return plus(times(face("y", z, px, 0), value), shift_y(times(face("y", z, px, 1), value), -1))

    def side_z(z, px, py, values):
        i = z // 2
        return plus(times(face("z", z, px, py), values[i]), times(face("z", z - 1, px, py), values[i - 1] if i else None))

    for i in range(planes):
        z = 2 * i
        q_xy.append(inverse(z, 1, 1) * plus(resid(z, 1, 1), side_z(z, 1, 1, q_xyz)))
        q_xz.append(inverse(z + 1, 1, 0) * plus(resid(z + 1, 1, 0), side_y(z + 1, 1, q_xyz[i])))
        q_yz.append(inverse(z + 1, 0, 1) * plus(resid(z + 1, 0, 1), side_x(z + 1, 1, q_xyz[i])))
    for i in range(planes):
        z = 2 * i
        q_x.append(inverse(z, 1, 0) * plus(resid(z, 1, 0), side_y(z, 1, q_xy[i]), side_z(z, 1, 0, q_xz)))
        q_y.append(inverse(z, 0, 1) * plus(resid(z, 0, 1), side_x(z, 1, q_xy[i]), side_z(z, 0, 1, q_yz)))
        q_z.append(
            inverse(z + 1, 0, 0) * plus(resid(z + 1, 0, 0), side_x(z + 1, 0, q_xz[i]), side_y(z + 1, 0, q_yz[i]))
        )
    for i in range(planes):
        z = 2 * i
        rhs.append(plus(resid(z, 0, 0), side_x(z, 0, q_x[i]), side_y(z, 0, q_y[i]), side_z(z, 0, 0, q_z)))

    keep_x, keep_y = stencil_ref.shape[2:]
    for i in range(planes):
        for dz in (-1, 0, 1):
            for dx in (-1, 0, 1):
                for dy in (-1, 0, 1):
                    value = coarse(i, dz, dx, dy)
                    number = 9 * (dz + 1) + 3 * (dx + 1) + dy + 1
                    if value is None:
                        stencil_ref[number, i] = jnp.zeros((keep_x, keep_y), F32)
                    else:
                        for odd in range(2):
                            rows = value[HALO * odd : HALO * odd + keep_x // 2, :keep_y]
                            stencil_ref[number, i, pl.ds(odd, keep_x // 2, stride=2), :] = rows

    stencil_copy = pltpu.make_async_copy(stencil_ref, stencil_hbm, sems.at[0])
    stencil_copy.start()

    scaled = []
    for i in range(planes):
        inside = factor_ref[3, 2 * i, 0, 0] > 0.0
        scaled.append(jnp.where(inside, OMEGA / jnp.where(inside, coarse(i, 0, 0, 0), 1.0), 0.0))
    near_row = {}
    for i in range(planes):
        for dz in range(-i, planes - i):
            for dy in (-1, 0, 1):
                near_row[i, dz, 0, dy] = coarse(i, dz, 0, dy)
                for dx in (-1, 1):
                    near_row[i, dz, dx, dy] = shift_x(coarse(i, dz, dx, dy), -dx)
    u = [scaled[i] * rhs[i] for i in range(planes)]
    for _ in range(SWEEPS - 1):
        moved = {(i, dy): shift_y(u[i], dy) if dy else u[i] for i in range(planes) for dy in (-1, 0, 1)}
        new = []
        for i in range(planes):
            sums = {}
            for dx in (-1, 0, 1):
                sums[dx] = tree_sum(
                    [near_row[i, dz, dx, dy] * moved[i + dz, dy] for dz in range(-i, planes - i) for dy in (-1, 0, 1)]
                )
            total = sums[0] + (shift_x(sums[1], 1) + shift_x(sums[-1], -1))
            new.append(u[i] + scaled[i] * (rhs[i] - total))
        u = new
    for i in range(planes):
        for odd in range(2):
            rows = u[i][HALO * odd : HALO * odd + keep_x // 2, :keep_y]
            solution_ref[i, pl.ds(odd, keep_x // 2, stride=2), :] = rows
    solution_copy = pltpu.make_async_copy(solution_ref, solution_hbm, sems.at[1])
    solution_copy.start()
    stencil_copy.wait()
    solution_copy.wait()


def swap(value, axis, first, wrap):
    count = lax.axis_size(axis)
    partner = list(range(count))
    for i in range(first, count if wrap else count - 1, 2):
        partner[i], partner[(i + 1) % count] = (i + 1) % count, i
    return lax.ppermute(value, axis, list(enumerate(partner)))


def swap_x(value, first, step=2):
    nx, ny = lax.axis_size("gx"), lax.axis_size("gy")
    partner = {}
    for x in range(first, nx - 1, step):
        partner[x], partner[x + 1] = x + 1, x
    pairs = []
    for x in range(nx):
        for y in range(ny):
            target = (partner[x], y) if x in partner else (x, y + 1 if y % 2 == 0 else y - 1)
            pairs.append((x * ny + y, target[0] * ny + target[1]))
    return lax.ppermute(value, ("gx", "gy"), pairs)


def on_chip(value):
    return pltpu.with_memory_space_constraint(value, pltpu.VMEM)


def on_device(base_cond, base_mass, fine_residual, point_index, gen_vector, z_offset):
    plane_count, width_x, width_y = base_mass.shape
    nx_total = width_x * lax.axis_size("gx")
    ny_total = width_y * lax.axis_size("gy")
    vmem = pl.BlockSpec(memory_space=pltpu.VMEM)
    hbm = pl.BlockSpec(memory_space=pl.ANY)
    strip = pltpu.VMEM((2, HALO, LANES), F32)
    groups = field_start(5, plane_count)
    raw, near_y, far_y = pl.pallas_call(
        strips_body,
        out_shape=(pltpu.VMEM((groups, HALO, width_y), F32), strip, strip),
        in_specs=[hbm] * 3,
        out_specs=(vmem,) * 3,
        scratch_shapes=[pltpu.SemaphoreType.DMA((5,))],
        name="strips",
    )(base_cond, base_mass, fine_residual)
    far_y = swap(far_y, "gy", 1, True)
    near_y = swap(near_y, "gy", 0, False)
    own = pl.pallas_call(
        halves_body,
        out_shape=pltpu.VMEM((groups + 3, HALO, LANES), F32),
        in_specs=[vmem],
        out_specs=vmem,
        name="halves",
    )(on_chip(raw))
    own = lax.dynamic_update_slice(own, far_y[:1], (groups + 1, 0, 0))
    own = lax.dynamic_update_slice(own, near_y[:1], (groups, 0, 0))
    own = lax.dynamic_update_slice(own, far_y[1:] + near_y[1:], (groups + 2, 0, 0))
    point_index, z_offset, gen_vector, own = lax.optimization_barrier((point_index, z_offset, gen_vector, own))
    integers = jnp.concatenate([gen_vector, point_index, z_offset]).reshape(1, -1)
    factors, wide, pick_strip = pl.pallas_call(
        lambda *refs: local_body(nx_total, ny_total, width_x, width_y, *refs),
        out_shape=(
            pltpu.VMEM((4, plane_count, 2, 2, ROWS, LANES), F32),
            pltpu.VMEM((groups, 2, HALO, LANES), F32),
            pltpu.VMEM((4 * HALO, 2 * LANES), BF16),
        ),
        in_specs=[vmem] * 2,
        out_specs=(vmem,) * 3,
        name="local",
    )(on_chip(integers), on_chip(own))
    far = swap_x(own, 1)
    first = swap_x(own, 0, 4)
    last = swap_x(own, 2, 4)
    coarse_block = (plane_count // 2, width_x // 2, width_y // 2)
    return pl.pallas_call(
        main_body,
        out_shape=(jax.ShapeDtypeStruct((27, *coarse_block), F32), jax.ShapeDtypeStruct(coarse_block, F32)),
        in_specs=[vmem] * 6,
        out_specs=(hbm, hbm),
        scratch_shapes=[
            pltpu.VMEM((groups, 2, 2 * ROWS, LANES), F32),
            pltpu.VMEM((27, *coarse_block), F32),
            pltpu.VMEM(coarse_block, F32),
            pltpu.SemaphoreType.DMA((2,)),
        ],
        name="galerkin",
    )(*[on_chip(value) for value in (factors, pick_strip, wide, last, far, first)])


def solution(mesh):
    return jax.shard_map(
        on_device,
        mesh=mesh,
        in_specs=(
            P(None, None, "gx", "gy"),
            P(None, "gx", "gy"),
            P("parts", "gx", "gy"),
            P("parts"),
            P(),
            P(),
        ),
        out_specs=(P(None, "parts", "gx", "gy"), P("parts", "gx", "gy")),
        check_vma=False,
    )
```

```python
import itertools
import math

import jax
import jax.numpy as jnp
from jax import lax
from jax.experimental import pallas as pl
from jax.experimental.pallas import tpu as pltpu
from jax.sharding import PartitionSpec as P

NZG = 512
QMCN = 1048576
SWEEPS = 4
OMEGA = 0.6
ROWS = 16
LANES = 128
HALO = 8
F32 = jnp.float32
BF16 = jnp.bfloat16


def iota(shape, dim):
    return lax.broadcasted_iota(jnp.int32, shape, dim)


def two_parts(values, axis):
    high = values.astype(BF16)
    return jnp.concatenate([high, (values - high.astype(F32)).astype(BF16)], axis)


def field_start(kind, planes):
    return kind * planes - (1 if kind > 2 else 0)


def strips_body(cond_hbm, mass_hbm, resid_hbm, gen_hbm, own_ref, near_ref, far_ref, gen_ref, sems):
    width = own_ref.shape[-1]
    planes = mass_hbm.shape[0]
    sources = [cond_hbm.at[0], cond_hbm.at[1], cond_hbm.at[2, : planes - 1], mass_hbm, resid_hbm]
    starts = [field_start(kind, planes) for kind in range(6)]
    copies = [
        pltpu.make_async_copy(source, own_ref.at[starts[kind] : starts[kind + 1]], sems.at[kind])
        for kind, source in enumerate(sources)
    ]
    copies.append(pltpu.make_async_copy(gen_hbm, gen_ref, sems.at[len(sources)]))
    for copy in copies:
        copy.start()
    even = lax.axis_index("gy") % 2 == 0
    row, lane = iota((2 * HALO, width), 0), iota((2 * HALO, width), 1)
    column = row % HALO + jnp.where((row < HALO) == even, width - HALO, 0)
    pick = jnp.where(lane == column, 1.0, 0.0).astype(BF16)
    for copy in copies:
        copy.wait()
    rows = own_ref[: starts[5]].reshape(-1, width)
    flip = rows.T
    low, high = flip[:HALO], flip[width - HALO :]
    taken = jnp.concatenate([jnp.where(even, high, low), jnp.where(even, low, high)], 0)
    for out_ref, start in ((near_ref, 0), (far_ref, 1)):
        part = taken[HALO * start : HALO * (start + 1)]
        out_ref[0] = part[:, :LANES]
        rest = jnp.concatenate([part[:, LANES:], jnp.zeros((HALO, 3 * LANES // 2 - part.shape[1]), F32)], 1)
        blank = jnp.zeros_like(rest)
        out_ref[1] = jnp.concatenate([blank, rest] if start else [rest, blank], 1)


def local_body(nx_total, ny_total, width_x, width_y, point_ref, offset_ref, gen_ref, own_ref, out_ref, wide_ref, pick_strip_ref):
    pick_strip_ref[...] = select_strips(width_y)
    groups = wide_ref.shape[0]
    spread = spread_rows([own_ref[...]], groups, pick_strip_ref[...])[0]
    for g in range(groups):
        for py in range(2):
            wide_ref[g, py] = spread[g][py]
    modes = gen_ref.shape[1]
    product = point_ref[0] * gen_ref[...]
    z_first = offset_ref[0]
    x_first = lax.axis_index("gx") * width_x
    y_first = lax.axis_index("gy") * width_y
    half_x, half_y = width_x // 2, width_y // 2
    shift = (product & (QMCN - 1)).astype(F32) / QMCN - 0.5
    mode_row = iota((modes, modes), 0)
    mode_col = jnp.sum(jnp.where(mode_row == iota((modes, modes), 1), shift, 0.0), axis=1, keepdims=True)
    k = iota((modes, LANES), 0)
    lane = iota((modes, LANES), 1)
    k_f = k.astype(F32)
    amplitude = 1.2 / (1.0 + 0.5 * k_f) * mode_col
    z_local = lane // (2 * ROWS)
    px = (lane // ROWS) % 2
    r = lane % ROWS
    place = r % HALO
    coarse_x = 2 * jnp.where(place < 6, place, place - HALO) + r // HALO
    x = x_first + 2 * coarse_x + px
    x_angle = (x.astype(F32) + 0.5) * (math.pi / nx_total)
    z_angle = ((z_local + z_first).astype(F32) + 0.5) * (math.pi / NZG)
    phase = z_angle * (k % 5).astype(F32) + x_angle * (1 + k % 4).astype(F32) + 0.7 * k_f
    x_ok = (place < 4) | (place >= 6)
    ones = jnp.where(x_ok & (x >= 0) & (x < nx_total), 1.0, 0.0)
    left = jnp.concatenate([amplitude * jnp.cos(phase), -amplitude * jnp.sin(phase)], 0)
    inside_x = lax.dot_general(ones, jnp.ones((modes, LANES), F32), (((0,), (0,)), ((), ())), preferred_element_type=F32)
    y_mode = (1 + (k // 4) % 4).astype(F32)
    root = {}
    for py in range(2):
        coarse_y = jnp.where(lane < half_y + 4, lane, lane - LANES)
        y = y_first + 2 * coarse_y + py
        y_angle = (y.astype(F32) + 0.5) * (math.pi / ny_total) * y_mode
        right = jnp.concatenate([jnp.cos(y_angle), jnp.sin(y_angle)], 0)
        log_kappa = lax.dot_general(
            left, right, (((0,), (0,)), ((), ())), precision=lax.Precision.HIGHEST, preferred_element_type=F32
        )
        y_full = y[0:1, :]
        lane_full = lane[0:1, :]
        y_ok = (lane_full < half_y + 4) | (lane_full >= LANES - 4)
        y_ok = y_ok & (y_full >= 0) & (y_full < ny_total)
        value = jnp.where((inside_x > 0.5) & y_ok, jnp.exp(0.5 * log_kappa), 0.0)
        for group in range(8):
            root[group // 2, group % 2, py] = value[group * ROWS : (group + 1) * ROWS]
    planes = out_ref.shape[1]
    for (z, px, py), here in root.items():
        out_ref[0, z, px, py] = here * (shift_x(root[z, 0, py], 1) if px else root[z, 1, py])
        out_ref[1, z, px, py] = here * (shift_y(root[z, px, 0], 1) if py else root[z, px, 1])
        out_ref[2, z, px, py] = here * root[z + 1, px, py] if z + 1 < planes else jnp.zeros((ROWS, LANES), F32)
        out_ref[3, z, px, py] = here * here


def select_strips(width):
    half = width // 2
    strip = iota((4 * HALO, 2 * LANES), 0) % (2 * HALO)
    column = iota((4 * HALO, 2 * LANES), 1)
    parity, k = column // LANES, column % LANES
    k = jnp.where(k >= LANES - 4, k - LANES, k)
    even = lax.axis_index("gy") % 2 == 0
    below = strip % HALO - HALO
    fine = jnp.where((strip < HALO) == even, below + HALO + width, below)
    wanted = ((k < 0) | (k >= half)) & (k < half + 4)
    return jnp.where(wanted & (fine == 2 * k + parity), 1.0, 0.0).astype(BF16)


def halves_body(own_ref, out_ref):
    groups, _, width = own_ref.shape
    row, lane = iota((2 * width, LANES), 0) % width, iota((2 * width, LANES), 1)
    half = width // 2
    pick = jnp.where(row == 2 * (lane % half) + lane // half, 1.0, 0.0).astype(BF16)
    rows = two_parts(own_ref[...].reshape(groups * HALO, width), 1)
    spread = lax.dot_general(rows, pick, (((1,), (0,)), ((), ())), preferred_element_type=F32)
    out_ref[:groups] = spread.reshape(groups, HALO, LANES)


def spread_rows(blocks, groups, pick_strip):
    main, split = LANES // HALO, groups - LANES // HALO
    strips = [jnp.concatenate([block[groups], block[groups + 1]], 0) for block in blocks]
    for block in blocks:
        rest = block[groups + 2]
        strips.append(jnp.concatenate([rest[:, : split * HALO], rest[:, LANES // 2 : LANES // 2 + split * HALO]], 0))
    border = lax.dot_general(
        two_parts(jnp.concatenate(strips, 1), 0), pick_strip, (((0,), (0,)), ((), ())), preferred_element_type=F32
    )
    inner = iota((HALO, LANES), 1) < LANES // 2
    result = []
    for number, block in enumerate(blocks):
        first = [number * LANES + HALO * g for g in range(main)]
        first += [len(blocks) * LANES + number * split * HALO + HALO * g for g in range(split)]
        classes = []
        for g, row in enumerate(first):
            odd = pltpu.roll(block[g], LANES // 2, 1)
            classes.append(
                [
                    jnp.where(inner, values, border[row : row + HALO, LANES * py : LANES * (py + 1)])
                    for py, values in enumerate((block[g], odd))
                ]
            )
        result.append(classes)
    return result


class Lazy:
    def __init__(self, rule):
        self.rule, self.known = rule, {}

    def __call__(self, *key):
        if key not in self.known:
            self.known[key] = self.rule(*key)
        return self.known[key]


def plus(*terms):
    total = None
    for term in terms:
        if term is not None:
            total = term if total is None else total + term
    return total


def times(left, right):
    return None if left is None or right is None else left * right


def minus(left, right):
    if right is None:
        return left
    return -right if left is None else left - right


def tree_sum(terms):
    while len(terms) > 1:
        terms = [terms[k] + terms[k + 1] if k + 1 < len(terms) else terms[k] for k in range(0, len(terms), 2)]
    return terms[0]


def shift_x(value, steps):
    if value is None or steps == 0:
        return value
    even, odd = value[:HALO], value[HALO:]
    if steps > 0:
        return jnp.concatenate([odd, pltpu.roll(even, HALO - 1, 0)], 0)
    return jnp.concatenate([pltpu.roll(odd, 1, 0), even], 0)


def shift_y(value, steps):
    return value if value is None or steps == 0 else pltpu.roll(value, (-steps) % LANES, 1)


def main_body(
    factor_ref,
    pick_strip_ref,
    own_ref,
    last_ref,
    far_ref,
    first_ref,
    stencil_hbm,
    solution_hbm,
    wide_ref,
    stencil_ref,
    solution_ref,
    sems,
):
    groups = own_ref.shape[0]
    for g in range(groups):
        for py in range(2):
            wide_ref[g, py, 0:8, :] = own_ref[g, py]
            wide_ref[g, py, 16:24, :] = jnp.zeros((8, LANES), F32)
    above = lax.axis_index("gx") % 2 == 0
    near_place = pl.multiple_of(jnp.where(above, 8, 24), 8)
    far_place = pl.multiple_of(jnp.where(above, 24, 8), 8)
    near = jnp.where(lax.axis_index("gx") % 4 < 2, first_ref[...], last_ref[...])
    spread = spread_rows([near, far_ref[...]], groups, pick_strip_ref[...])
    for place, rows in zip((near_place, far_place), spread):
        for g in range(groups):
            for py in range(2):
                wide_ref[g, py, pl.ds(place, 8), :] = rows[g][py]

    planes = 2

    def base(kind, z, px, py):
        group = field_start(kind, 2 * planes) + z
        tiles = [wide_ref[group, py, pl.ds(2 * odd + px, HALO, stride=4), :] for odd in range(2)]
        return jnp.concatenate(tiles, 0)

    def face(axis, z, px, py):
        kind = "xyz".index(axis)
        if kind == 2 and not 0 <= z < 2 * planes - 1:
            return None
        return base(kind, z, px, py) * factor_ref[kind, z, px, py]

    face = Lazy(face)
    mass = Lazy(lambda z, px, py: base(3, z, px, py) * factor_ref[3, z, px, py])

    def pair(axis, z, px, py):
        if axis == "x":
            lower = face("x", z, 0, py) if px else shift_x(face("x", z, 1, py), -1)
        elif axis == "y":
            lower = face("y", z, px, 0) if py else shift_y(face("y", z, px, 1), -1)
        else:
            lower = face("z", z - 1, px, py)
        return plus(face(axis, z, px, py), lower)

    pair = Lazy(pair)

    def inverse(z, px, py):
        total = mass(z, px, py)
        for axis, odd in (("x", px), ("y", py), ("z", z % 2)):
            if odd:
                total = total + pair(axis, z, px, py)
        return 1.0 / jnp.where(factor_ref[3, z, px, py] > 0.0, total, 1.0)

    inverse = Lazy(inverse)

    def w_x(i, a):
        return None if not 0 <= i < planes else inverse(2 * i, 1, 0) * face("x", 2 * i, a, 0)

    def w_y(i, b):
        return None if not 0 <= i < planes else inverse(2 * i, 0, 1) * face("y", 2 * i, 0, b)

    def w_z(i, c):
        return times(inverse(2 * i + 1, 0, 0), face("z", 2 * i + c, 0, 0))

    w_x, w_y, w_z = Lazy(w_x), Lazy(w_y), Lazy(w_z)
    w_x_up = Lazy(lambda i, a: shift_y(w_x(i, a), 1))
    w_y_up = Lazy(lambda i, b: shift_x(w_y(i, b), 1))
    w_z_upx = Lazy(lambda i, c: shift_x(w_z(i, c), 1))
    w_z_upy = Lazy(lambda i, c: shift_y(w_z(i, c), 1))

    def w_xy(i, a, b):
        if not 0 <= i < planes:
            return None
        z = 2 * i
        return inverse(z, 1, 1) * (
            face("x", z, a, 1) * (w_y_up(i, b) if a else w_y(i, b)) + face("y", z, 1, b) * (w_x_up(i, a) if b else w_x(i, a))
        )

    def w_xz(i, a, c):
        z = 2 * i + 1
        return times(
            inverse(z, 1, 0),
            plus(times(face("x", z, a, 0), w_z_upx(i, c) if a else w_z(i, c)), times(face("z", 2 * i + c, 1, 0), w_x(i + c, a))),
        )

    def w_yz(i, b, c):
        z = 2 * i + 1
        return times(
            inverse(z, 0, 1),
            plus(times(face("y", z, 0, b), w_z_upy(i, c) if b else w_z(i, c)), times(face("z", 2 * i + c, 0, 1), w_y(i + c, b))),
        )

    w_xy, w_xz, w_yz = Lazy(w_xy), Lazy(w_xz), Lazy(w_yz)
    w_yz_up = Lazy(lambda i, b, c: shift_x(w_yz(i, b, c), 1))
    w_xz_up = Lazy(lambda i, a, c: shift_y(w_xz(i, a, c), 1))

    def w_xyz(i, a, b, c):
        z = 2 * i + 1
        if not 0 <= i < planes or not 0 <= i + c < planes:
            return None
        return inverse(z, 1, 1) * (
            face("x", z, a, 1) * (w_yz_up(i, b, c) if a else w_yz(i, b, c))
            + face("y", z, 1, b) * (w_xz_up(i, a, c) if b else w_xz(i, a, c))
            + face("z", 2 * i + c, 1, 1) * w_xy(i + c, a, b)
        )

    w_xyz = Lazy(w_xyz)

    def weights_of(i, pz, px, py, moved=None):
        plain = {
            (0, 1, 0): lambda c, a, b: w_x(i, a),
            (0, 0, 1): lambda c, a, b: w_y(i, b),
            (1, 0, 0): lambda c, a, b: w_z(i, c),
            (0, 1, 1): lambda c, a, b: w_xy(i, a, b),
            (1, 1, 0): lambda c, a, b: w_xz(i, a, c),
            (1, 0, 1): lambda c, a, b: w_yz(i, b, c),
            (1, 1, 1): lambda c, a, b: w_xyz(i, a, b, c),
        }
        up_x = {
            (0, 0, 1): lambda c, a, b: w_y_up(i, b),
            (1, 0, 0): lambda c, a, b: w_z_upx(i, c),
            (1, 0, 1): lambda c, a, b: w_yz_up(i, b, c),
        }
        up_y = {
            (0, 1, 0): lambda c, a, b: w_x_up(i, a),
            (1, 0, 0): lambda c, a, b: w_z_upy(i, c),
            (1, 1, 0): lambda c, a, b: w_xz_up(i, a, c),
        }
        if (pz, px, py) == (0, 0, 0):
            return {(0, 0, 0): None}
        rule = {"x": up_x, "y": up_y, None: plain}[moved][pz, px, py]
        values = {(c, a, b): rule(c, a, b) for c in range(pz + 1) for a in range(px + 1) for b in range(py + 1)}
        return {sides: value for sides, value in values.items() if value is not None}

    parts = {}

    def keep(i, step, place, value):
        key = (i, *step, *place)
        parts[key] = plus(parts.get(key), value)

    for i in range(planes):
        keep(i, (0, 0, 0), (0, 0), mass(2 * i, 0, 0))
    for i, pz, px, py, axis, side in itertools.product(range(planes), (0, 1), (0, 1), (0, 1), "zxy", (0, 1)):
        parity = {"z": pz, "x": px, "y": py}
        if not parity[axis] or (axis == "z" and i + side >= planes):
            continue
        parity[axis] = 0
        lower = (parity["z"], parity["x"], parity["y"])
        offset = tuple(side if axis == name else 0 for name in "zxy")
        z = 2 * i + pz
        if axis == "z":
            here, joined = weights_of(i + side, *lower), face("z", 2 * i + side, px, py)
        elif axis == "x":
            here, joined = weights_of(i, *lower, "x" if side else None), face("x", z, side, py)
        else:
            here, joined = weights_of(i, *lower, "y" if side else None), face("y", z, px, side)
        there = weights_of(i, pz, px, py)
        drop = {}
        for column, value in there.items():
            own = tuple(at - by for at, by in zip(column, offset))
            drop[column] = -value
            if own in here:
                drop[column] = (1.0 if here[own] is None else here[own]) - value
        for sides, value in here.items():
            row = tuple(at + by for at, by in zip(sides, offset))
            scaled_row = joined if value is None else joined * value
            for column, change in drop.items():
                step = tuple(to - at for to, at in zip(column, row))
                if step >= (0, 0, 0):
                    keep(i + row[0], step, row[1:], scaled_row * change)

    def direct(i, dz, dx, dy):
        low, high = (
            plus(parts.get((i, dz, dx, dy, 0, side)), shift_x(parts.get((i, dz, dx, dy, 1, side)), -1)) for side in (0, 1)
        )
        return plus(low, shift_y(high, -1))

    def coarse(i, dz, dx, dy):
        if not 0 <= i + dz < planes:
            return None
        if (dz, dx, dy) >= (0, 0, 0):
            return direct(i, dz, dx, dy)
        return shift_y(shift_x(coarse(i + dz, -dz, -dx, -dy), dx), dy)

    coarse = Lazy(coarse)

    resid = Lazy(lambda z, px, py: base(4, z, px, py))
    odd_z = range(planes)
    q_xyz = [inverse(2 * i + 1, 1, 1) * resid(2 * i + 1, 1, 1) for i in odd_z] + [None]
    q_xy, q_xz, q_yz, q_x, q_y, q_z, rhs = [], [], [], [], [], [], []

    def side_x(z, py, value):
        return plus(times(face("x", z, 0, py), value), shift_x(times(face("x", z, 1, py), value), -1))

    def side_y(z, px, value):
        return plus(times(face("y", z, px, 0), value), shift_y(times(face("y", z, px, 1), value), -1))

    def side_z(z, px, py, values):
        i = z // 2
        return plus(times(face("z", z, px, py), values[i]), times(face("z", z - 1, px, py), values[i - 1] if i else None))

    for i in range(planes):
        z = 2 * i
        q_xy.append(inverse(z, 1, 1) * plus(resid(z, 1, 1), side_z(z, 1, 1, q_xyz)))
        q_xz.append(inverse(z + 1, 1, 0) * plus(resid(z + 1, 1, 0), side_y(z + 1, 1, q_xyz[i])))
        q_yz.append(inverse(z + 1, 0, 1) * plus(resid(z + 1, 0, 1), side_x(z + 1, 1, q_xyz[i])))
    for i in range(planes):
        z = 2 * i
        q_x.append(inverse(z, 1, 0) * plus(resid(z, 1, 0), side_y(z, 1, q_xy[i]), side_z(z, 1, 0, q_xz)))
        q_y.append(inverse(z, 0, 1) * plus(resid(z, 0, 1), side_x(z, 1, q_xy[i]), side_z(z, 0, 1, q_yz)))
        q_z.append(
            inverse(z + 1, 0, 0) * plus(resid(z + 1, 0, 0), side_x(z + 1, 0, q_xz[i]), side_y(z + 1, 0, q_yz[i]))
        )
    for i in range(planes):
        z = 2 * i
        rhs.append(plus(resid(z, 0, 0), side_x(z, 0, q_x[i]), side_y(z, 0, q_y[i]), side_z(z, 0, 0, q_z)))

    keep_x, keep_y = stencil_ref.shape[2:]
    for i in range(planes):
        for dz in (-1, 0, 1):
            for dx in (-1, 0, 1):
                for dy in (-1, 0, 1):
                    value = coarse(i, dz, dx, dy)
                    number = 9 * (dz + 1) + 3 * (dx + 1) + dy + 1
                    if value is None:
                        stencil_ref[number, i] = jnp.zeros((keep_x, keep_y), F32)
                    else:
                        for odd in range(2):
                            rows = value[HALO * odd : HALO * odd + keep_x // 2, :keep_y]
                            stencil_ref[number, i, pl.ds(odd, keep_x // 2, stride=2), :] = rows

    stencil_copy = pltpu.make_async_copy(stencil_ref, stencil_hbm, sems.at[0])
    stencil_copy.start()

    scaled = []
    for i in range(planes):
        inside = factor_ref[3, 2 * i, 0, 0] > 0.0
        scaled.append(jnp.where(inside, OMEGA / jnp.where(inside, coarse(i, 0, 0, 0), 1.0), 0.0))
    near_row = {}
    for i in range(planes):
        for dz in range(-i, planes - i):
            for dy in (-1, 0, 1):
                near_row[i, dz, 0, dy] = coarse(i, dz, 0, dy)
                for dx in (-1, 1):
                    near_row[i, dz, dx, dy] = shift_x(coarse(i, dz, dx, dy), -dx)
    u = [scaled[i] * rhs[i] for i in range(planes)]
    for _ in range(SWEEPS - 1):
        moved = {(i, dy): shift_y(u[i], dy) if dy else u[i] for i in range(planes) for dy in (-1, 0, 1)}
        new = []
        for i in range(planes):
            sums = {}
            for dx in (-1, 0, 1):
                sums[dx] = tree_sum(
                    [near_row[i, dz, dx, dy] * moved[i + dz, dy] for dz in range(-i, planes - i) for dy in (-1, 0, 1)]
                )
            total = sums[0] + (shift_x(sums[1], 1) + shift_x(sums[-1], -1))
            new.append(u[i] + scaled[i] * (rhs[i] - total))
        u = new
    for i in range(planes):
        for odd in range(2):
            rows = u[i][HALO * odd : HALO * odd + keep_x // 2, :keep_y]
            solution_ref[i, pl.ds(odd, keep_x // 2, stride=2), :] = rows
    solution_copy = pltpu.make_async_copy(solution_ref, solution_hbm, sems.at[1])
    solution_copy.start()
    stencil_copy.wait()
    solution_copy.wait()


def swap(value, axis, first, wrap):
    count = lax.axis_size(axis)
    partner = list(range(count))
    for i in range(first, count if wrap else count - 1, 2):
        partner[i], partner[(i + 1) % count] = (i + 1) % count, i
    return lax.ppermute(value, axis, list(enumerate(partner)))


def swap_x(value, first, step=2):
    nx, ny = lax.axis_size("gx"), lax.axis_size("gy")
    partner = {}
    for x in range(first, nx - 1, step):
        partner[x], partner[x + 1] = x + 1, x
    pairs = []
    for x in range(nx):
        for y in range(ny):
            target = (partner[x], y) if x in partner else (x, y + 1 if y % 2 == 0 else y - 1)
            pairs.append((x * ny + y, target[0] * ny + target[1]))
    return lax.ppermute(value, ("gx", "gy"), pairs)


def on_chip(value):
    return pltpu.with_memory_space_constraint(value, pltpu.VMEM)


def on_device(base_cond, base_mass, fine_residual, point_index, gen_vector, z_offset):
    plane_count, width_x, width_y = base_mass.shape
    nx_total = width_x * lax.axis_size("gx")
    ny_total = width_y * lax.axis_size("gy")
    vmem = pl.BlockSpec(memory_space=pltpu.VMEM)
    hbm = pl.BlockSpec(memory_space=pl.ANY)
    strip = pltpu.VMEM((2, HALO, LANES), F32)
    groups = field_start(5, plane_count)
    raw, near_y, far_y, gen = pl.pallas_call(
        strips_body,
        out_shape=(pltpu.VMEM((groups, HALO, width_y), F32), strip, strip, pltpu.VMEM((1, gen_vector.size), jnp.int32)),
        in_specs=[hbm] * 4,
        out_specs=(vmem,) * 4,
        scratch_shapes=[pltpu.SemaphoreType.DMA((6,))],
        name="strips",
    )(base_cond, base_mass, fine_residual, gen_vector.reshape(1, -1))
    far_y = swap(far_y, "gy", 1, True)
    near_y = swap(near_y, "gy", 0, False)
    own = pl.pallas_call(
        halves_body,
        out_shape=pltpu.VMEM((groups + 3, HALO, LANES), F32),
        in_specs=[vmem],
        out_specs=vmem,
        name="halves",
    )(on_chip(raw))
    own = lax.dynamic_update_slice(own, far_y[:1], (groups + 1, 0, 0))
    own = lax.dynamic_update_slice(own, near_y[:1], (groups, 0, 0))
    own = lax.dynamic_update_slice(own, far_y[1:] + near_y[1:], (groups + 2, 0, 0))
    smem = pl.BlockSpec(memory_space=pltpu.SMEM)
    factors, wide, pick_strip = pl.pallas_call(
        lambda *refs: local_body(nx_total, ny_total, width_x, width_y, *refs),
        out_shape=(
            pltpu.VMEM((4, plane_count, 2, 2, ROWS, LANES), F32),
            pltpu.VMEM((groups, 2, HALO, LANES), F32),
            pltpu.VMEM((4 * HALO, 2 * LANES), BF16),
        ),
        in_specs=[smem, smem, vmem, vmem],
        out_specs=(vmem,) * 3,
        name="local",
    )(point_index, z_offset, on_chip(gen), on_chip(own))
    far = swap_x(own, 1)
    first = swap_x(own, 0, 4)
    last = swap_x(own, 2, 4)
    coarse_block = (plane_count // 2, width_x // 2, width_y // 2)
    return pl.pallas_call(
        main_body,
        out_shape=(jax.ShapeDtypeStruct((27, *coarse_block), F32), jax.ShapeDtypeStruct(coarse_block, F32)),
        in_specs=[vmem] * 6,
        out_specs=(hbm, hbm),
        scratch_shapes=[
            pltpu.VMEM((groups, 2, 2 * ROWS, LANES), F32),
            pltpu.VMEM((27, *coarse_block), F32),
            pltpu.VMEM(coarse_block, F32),
            pltpu.SemaphoreType.DMA((2,)),
        ],
        name="galerkin",
    )(*[on_chip(value) for value in (factors, pick_strip, wide, last, far, first)])


def solution(mesh):
    return jax.shard_map(
        on_device,
        mesh=mesh,
        in_specs=(
            P(None, None, "gx", "gy"),
            P(None, "gx", "gy"),
            P("parts", "gx", "gy"),
            P("parts"),
            P(),
            P(),
        ),
        out_specs=(P(None, "parts", "gx", "gy"), P("parts", "gx", "gy")),
        check_vma=False,
    )
```

```python
import itertools
import math

import jax
import jax.numpy as jnp
from jax import lax
from jax.experimental import pallas as pl
from jax.experimental.pallas import tpu as pltpu
from jax.sharding import PartitionSpec as P

NZG = 512
QMCN = 1048576
SWEEPS = 4
OMEGA = 0.6
ROWS = 16
LANES = 128
HALO = 8
F32 = jnp.float32
BF16 = jnp.bfloat16


def iota(shape, dim):
    return lax.broadcasted_iota(jnp.int32, shape, dim)


def two_parts(values, axis):
    high = values.astype(BF16)
    return jnp.concatenate([high, (values - high.astype(F32)).astype(BF16)], axis)


def field_start(kind, planes):
    return kind * planes - (1 if kind > 2 else 0)


def strips_body(cond_hbm, mass_hbm, resid_hbm, gen_hbm, own_ref, near_ref, far_ref, gen_ref, sems):
    width = own_ref.shape[-1]
    planes = mass_hbm.shape[0]
    sources = [cond_hbm.at[0], cond_hbm.at[1], cond_hbm.at[2, : planes - 1], mass_hbm, resid_hbm]
    starts = [field_start(kind, planes) for kind in range(6)]
    copies = [
        pltpu.make_async_copy(source, own_ref.at[starts[kind] : starts[kind + 1]], sems.at[kind])
        for kind, source in enumerate(sources)
    ]
    copies.append(pltpu.make_async_copy(gen_hbm, gen_ref, sems.at[len(sources)]))
    for copy in copies:
        copy.start()
    even = lax.axis_index("gy") % 2 == 0
    row, lane = iota((2 * HALO, width), 0), iota((2 * HALO, width), 1)
    column = row % HALO + jnp.where((row < HALO) == even, width - HALO, 0)
    pick = jnp.where(lane == column, 1.0, 0.0).astype(BF16)
    for copy in copies:
        copy.wait()
    rows = own_ref[: starts[5]].reshape(-1, width)
    flip = rows.T
    low, high = flip[:HALO], flip[width - HALO :]
    taken = jnp.concatenate([jnp.where(even, high, low), jnp.where(even, low, high)], 0)
    for out_ref, start in ((near_ref, 0), (far_ref, 1)):
        part = taken[HALO * start : HALO * (start + 1)]
        out_ref[0] = part[:, :LANES]
        rest = jnp.concatenate([part[:, LANES:], jnp.zeros((HALO, 3 * LANES // 2 - part.shape[1]), F32)], 1)
        blank = jnp.zeros_like(rest)
        out_ref[1] = jnp.concatenate([blank, rest] if start else [rest, blank], 1)


def local_body(nx_total, ny_total, width_x, width_y, point_ref, offset_ref, gen_ref, own_ref, out_ref, wide_ref, pick_strip_ref):
    pick_strip_ref[...] = select_strips(width_y)
    groups = wide_ref.shape[0]
    spread = spread_rows([own_ref[...]], groups, pick_strip_ref[...])[0]
    for g in range(groups):
        for py in range(2):
            wide_ref[g, py] = spread[g][py]
    modes = gen_ref.shape[1]
    product = point_ref[0] * gen_ref[...]
    z_first = offset_ref[0]
    x_first = lax.axis_index("gx") * width_x
    y_first = lax.axis_index("gy") * width_y
    half_x, half_y = width_x // 2, width_y // 2
    shift = (product & (QMCN - 1)).astype(F32) / QMCN - 0.5
    mode_row = iota((modes, modes), 0)
    mode_col = jnp.sum(jnp.where(mode_row == iota((modes, modes), 1), shift, 0.0), axis=1, keepdims=True)
    k = iota((modes, LANES), 0)
    lane = iota((modes, LANES), 1)
    k_f = k.astype(F32)
    amplitude = 1.2 / (1.0 + 0.5 * k_f) * mode_col
    z_local = lane // (2 * ROWS)
    px = (lane // ROWS) % 2
    r = lane % ROWS
    place = r % HALO
    coarse_x = 2 * jnp.where(place < 6, place, place - HALO) + r // HALO
    x = x_first + 2 * coarse_x + px
    x_angle = (x.astype(F32) + 0.5) * (math.pi / nx_total)
    z_angle = ((z_local + z_first).astype(F32) + 0.5) * (math.pi / NZG)
    phase = z_angle * (k % 5).astype(F32) + x_angle * (1 + k % 4).astype(F32) + 0.7 * k_f
    x_ok = (place < 4) | (place >= 6)
    ones = jnp.where(x_ok & (x >= 0) & (x < nx_total), 1.0, 0.0)
    left = jnp.concatenate([amplitude * jnp.cos(phase), -amplitude * jnp.sin(phase)], 0)
    inside_x = lax.dot_general(ones, jnp.ones((modes, LANES), F32), (((0,), (0,)), ((), ())), preferred_element_type=F32)
    y_mode = (1 + (k // 4) % 4).astype(F32)
    root = {}
    for py in range(2):
        coarse_y = jnp.where(lane < half_y + 4, lane, lane - LANES)
        y = y_first + 2 * coarse_y + py
        y_angle = (y.astype(F32) + 0.5) * (math.pi / ny_total) * y_mode
        right = jnp.concatenate([jnp.cos(y_angle), jnp.sin(y_angle)], 0)
        log_kappa = lax.dot_general(
            left, right, (((0,), (0,)), ((), ())), precision=lax.Precision.HIGHEST, preferred_element_type=F32
        )
        y_full = y[0:1, :]
        lane_full = lane[0:1, :]
        y_ok = (lane_full < half_y + 4) | (lane_full >= LANES - 4)
        y_ok = y_ok & (y_full >= 0) & (y_full < ny_total)
        value = jnp.where((inside_x > 0.5) & y_ok, jnp.exp(0.5 * log_kappa), 0.0)
        for group in range(8):
            root[group // 2, group % 2, py] = value[group * ROWS : (group + 1) * ROWS]
    planes = out_ref.shape[1]
    for (z, px, py), here in root.items():
        out_ref[0, z, px, py] = here * (shift_x(root[z, 0, py], 1) if px else root[z, 1, py])
        out_ref[1, z, px, py] = here * (shift_y(root[z, px, 0], 1) if py else root[z, px, 1])
        out_ref[2, z, px, py] = here * root[z + 1, px, py] if z + 1 < planes else jnp.zeros((ROWS, LANES), F32)
        out_ref[3, z, px, py] = here * here


def select_strips(width):
    half = width // 2
    strip = iota((4 * HALO, 2 * LANES), 0) % (2 * HALO)
    column = iota((4 * HALO, 2 * LANES), 1)
    parity, k = column // LANES, column % LANES
    k = jnp.where(k >= LANES - 4, k - LANES, k)
    even = lax.axis_index("gy") % 2 == 0
    below = strip % HALO - HALO
    fine = jnp.where((strip < HALO) == even, below + HALO + width, below)
    wanted = ((k < 0) | (k >= half)) & (k < half + 4)
    return jnp.where(wanted & (fine == 2 * k + parity), 1.0, 0.0).astype(BF16)


def halves_body(own_ref, out_ref):
    groups, _, width = own_ref.shape
    row, lane = iota((2 * width, LANES), 0) % width, iota((2 * width, LANES), 1)
    half = width // 2
    pick = jnp.where(row == 2 * (lane % half) + lane // half, 1.0, 0.0).astype(BF16)
    rows = two_parts(own_ref[...].reshape(groups * HALO, width), 1)
    spread = lax.dot_general(rows, pick, (((1,), (0,)), ((), ())), preferred_element_type=F32)
    out_ref[:groups] = spread.reshape(groups, HALO, LANES)


def spread_rows(blocks, groups, pick_strip):
    main, split = LANES // HALO, groups - LANES // HALO
    strips = [jnp.concatenate([block[groups], block[groups + 1]], 0) for block in blocks]
    for block in blocks:
        rest = block[groups + 2]
        strips.append(jnp.concatenate([rest[:, : split * HALO], rest[:, LANES // 2 : LANES // 2 + split * HALO]], 0))
    border = lax.dot_general(
        two_parts(jnp.concatenate(strips, 1), 0), pick_strip, (((0,), (0,)), ((), ())), preferred_element_type=F32
    )
    inner = iota((HALO, LANES), 1) < LANES // 2
    result = []
    for number, block in enumerate(blocks):
        first = [number * LANES + HALO * g for g in range(main)]
        first += [len(blocks) * LANES + number * split * HALO + HALO * g for g in range(split)]
        classes = []
        for g, row in enumerate(first):
            odd = pltpu.roll(block[g], LANES // 2, 1)
            classes.append(
                [
                    jnp.where(inner, values, border[row : row + HALO, LANES * py : LANES * (py + 1)])
                    for py, values in enumerate((block[g], odd))
                ]
            )
        result.append(classes)
    return result


class Lazy:
    def __init__(self, rule):
        self.rule, self.known = rule, {}

    def __call__(self, *key):
        if key not in self.known:
            self.known[key] = self.rule(*key)
        return self.known[key]


def plus(*terms):
    total = None
    for term in terms:
        if term is not None:
            total = term if total is None else total + term
    return total


def times(left, right):
    return None if left is None or right is None else left * right


def minus(left, right):
    if right is None:
        return left
    return -right if left is None else left - right


def tree_sum(terms):
    while len(terms) > 1:
        terms = [terms[k] + terms[k + 1] if k + 1 < len(terms) else terms[k] for k in range(0, len(terms), 2)]
    return terms[0]


def shift_x(value, steps):
    if value is None or steps == 0:
        return value
    even, odd = value[:HALO], value[HALO:]
    if steps > 0:
        return jnp.concatenate([odd, pltpu.roll(even, HALO - 1, 0)], 0)
    return jnp.concatenate([pltpu.roll(odd, 1, 0), even], 0)


def shift_y(value, steps):
    return value if value is None or steps == 0 else pltpu.roll(value, (-steps) % LANES, 1)


def main_body(
    factor_ref,
    pick_strip_ref,
    own_ref,
    last_ref,
    far_ref,
    first_ref,
    stencil_hbm,
    solution_hbm,
    wide_ref,
    stencil_ref,
    solution_ref,
    sems,
):
    groups = own_ref.shape[0]
    for g in range(groups):
        for py in range(2):
            wide_ref[g, py, 0:8, :] = own_ref[g, py]
            wide_ref[g, py, 16:24, :] = jnp.zeros((8, LANES), F32)
    above = lax.axis_index("gx") % 2 == 0
    near_place = pl.multiple_of(jnp.where(above, 8, 24), 8)
    far_place = pl.multiple_of(jnp.where(above, 24, 8), 8)
    near = jnp.where(lax.axis_index("gx") % 4 < 2, first_ref[...], last_ref[...])
    spread = spread_rows([near, far_ref[...]], groups, pick_strip_ref[...])
    for place, rows in zip((near_place, far_place), spread):
        for g in range(groups):
            for py in range(2):
                wide_ref[g, py, pl.ds(place, 8), :] = rows[g][py]

    planes = 2

    def base(kind, z, px, py):
        group = field_start(kind, 2 * planes) + z
        tiles = [wide_ref[group, py, pl.ds(2 * odd + px, HALO, stride=4), :] for odd in range(2)]
        return jnp.concatenate(tiles, 0)

    def face(axis, z, px, py):
        kind = "xyz".index(axis)
        if kind == 2 and not 0 <= z < 2 * planes - 1:
            return None
        return base(kind, z, px, py) * factor_ref[kind, z, px, py]

    face = Lazy(face)
    mass = Lazy(lambda z, px, py: base(3, z, px, py) * factor_ref[3, z, px, py])

    def pair(axis, z, px, py):
        if axis == "x":
            lower = face("x", z, 0, py) if px else shift_x(face("x", z, 1, py), -1)
        elif axis == "y":
            lower = face("y", z, px, 0) if py else shift_y(face("y", z, px, 1), -1)
        else:
            lower = face("z", z - 1, px, py)
        return plus(face(axis, z, px, py), lower)

    pair = Lazy(pair)

    def inverse(z, px, py):
        total = mass(z, px, py)
        for axis, odd in (("x", px), ("y", py), ("z", z % 2)):
            if odd:
                total = total + pair(axis, z, px, py)
        return 1.0 / jnp.where(factor_ref[3, z, px, py] > 0.0, total, 1.0)

    inverse = Lazy(inverse)

    def w_x(i, a):
        return None if not 0 <= i < planes else inverse(2 * i, 1, 0) * face("x", 2 * i, a, 0)

    def w_y(i, b):
        return None if not 0 <= i < planes else inverse(2 * i, 0, 1) * face("y", 2 * i, 0, b)

    def w_z(i, c):
        return times(inverse(2 * i + 1, 0, 0), face("z", 2 * i + c, 0, 0))

    w_x, w_y, w_z = Lazy(w_x), Lazy(w_y), Lazy(w_z)
    w_x_up = Lazy(lambda i, a: shift_y(w_x(i, a), 1))
    w_y_up = Lazy(lambda i, b: shift_x(w_y(i, b), 1))
    w_z_upx = Lazy(lambda i, c: shift_x(w_z(i, c), 1))
    w_z_upy = Lazy(lambda i, c: shift_y(w_z(i, c), 1))

    def w_xy(i, a, b):
        if not 0 <= i < planes:
            return None
        z = 2 * i
        return inverse(z, 1, 1) * (
            face("x", z, a, 1) * (w_y_up(i, b) if a else w_y(i, b)) + face("y", z, 1, b) * (w_x_up(i, a) if b else w_x(i, a))
        )

    def w_xz(i, a, c):
        z = 2 * i + 1
        return times(
            inverse(z, 1, 0),
            plus(times(face("x", z, a, 0), w_z_upx(i, c) if a else w_z(i, c)), times(face("z", 2 * i + c, 1, 0), w_x(i + c, a))),
        )

    def w_yz(i, b, c):
        z = 2 * i + 1
        return times(
            inverse(z, 0, 1),
            plus(times(face("y", z, 0, b), w_z_upy(i, c) if b else w_z(i, c)), times(face("z", 2 * i + c, 0, 1), w_y(i + c, b))),
        )

    w_xy, w_xz, w_yz = Lazy(w_xy), Lazy(w_xz), Lazy(w_yz)
    w_yz_up = Lazy(lambda i, b, c: shift_x(w_yz(i, b, c), 1))
    w_xz_up = Lazy(lambda i, a, c: shift_y(w_xz(i, a, c), 1))

    def w_xyz(i, a, b, c):
        z = 2 * i + 1
        if not 0 <= i < planes or not 0 <= i + c < planes:
            return None
        return inverse(z, 1, 1) * (
            face("x", z, a, 1) * (w_yz_up(i, b, c) if a else w_yz(i, b, c))
            + face("y", z, 1, b) * (w_xz_up(i, a, c) if b else w_xz(i, a, c))
            + face("z", 2 * i + c, 1, 1) * w_xy(i + c, a, b)
        )

    w_xyz = Lazy(w_xyz)

    def weights_of(i, pz, px, py, moved=None):
        plain = {
            (0, 1, 0): lambda c, a, b: w_x(i, a),
            (0, 0, 1): lambda c, a, b: w_y(i, b),
            (1, 0, 0): lambda c, a, b: w_z(i, c),
            (0, 1, 1): lambda c, a, b: w_xy(i, a, b),
            (1, 1, 0): lambda c, a, b: w_xz(i, a, c),
            (1, 0, 1): lambda c, a, b: w_yz(i, b, c),
            (1, 1, 1): lambda c, a, b: w_xyz(i, a, b, c),
        }
        up_x = {
            (0, 0, 1): lambda c, a, b: w_y_up(i, b),
            (1, 0, 0): lambda c, a, b: w_z_upx(i, c),
            (1, 0, 1): lambda c, a, b: w_yz_up(i, b, c),
        }
        up_y = {
            (0, 1, 0): lambda c, a, b: w_x_up(i, a),
            (1, 0, 0): lambda c, a, b: w_z_upy(i, c),
            (1, 1, 0): lambda c, a, b: w_xz_up(i, a, c),
        }
        if (pz, px, py) == (0, 0, 0):
            return {(0, 0, 0): None}
        rule = {"x": up_x, "y": up_y, None: plain}[moved][pz, px, py]
        values = {(c, a, b): rule(c, a, b) for c in range(pz + 1) for a in range(px + 1) for b in range(py + 1)}
        return {sides: value for sides, value in values.items() if value is not None}

    parts = {}

    def keep(i, step, place, value):
        key = (i, *step, *place)
        parts[key] = plus(parts.get(key), value)

    for i in range(planes):
        keep(i, (0, 0, 0), (0, 0), mass(2 * i, 0, 0))
    for i, pz, px, py, axis, side in itertools.product(range(planes), (0, 1), (0, 1), (0, 1), "zxy", (0, 1)):
        parity = {"z": pz, "x": px, "y": py}
        if not parity[axis] or (axis == "z" and i + side >= planes):
            continue
        parity[axis] = 0
        lower = (parity["z"], parity["x"], parity["y"])
        offset = tuple(side if axis == name else 0 for name in "zxy")
        z = 2 * i + pz
        if axis == "z":
            here, joined = weights_of(i + side, *lower), face("z", 2 * i + side, px, py)
        elif axis == "x":
            here, joined = weights_of(i, *lower, "x" if side else None), face("x", z, side, py)
        else:
            here, joined = weights_of(i, *lower, "y" if side else None), face("y", z, px, side)
        there = weights_of(i, pz, px, py)
        drop = {}
        for column, value in there.items():
            own = tuple(at - by for at, by in zip(column, offset))
            drop[column] = -value
            if own in here:
                drop[column] = (1.0 if here[own] is None else here[own]) - value
        for sides, value in here.items():
            row = tuple(at + by for at, by in zip(sides, offset))
            scaled_row = joined if value is None else joined * value
            for column, change in drop.items():
                step = tuple(to - at for to, at in zip(column, row))
                if step >= (0, 0, 0):
                    keep(i + row[0], step, row[1:], scaled_row * change)

    def direct(i, dz, dx, dy):
        low, high = (
            plus(parts.get((i, dz, dx, dy, 0, side)), shift_x(parts.get((i, dz, dx, dy, 1, side)), -1)) for side in (0, 1)
        )
        return plus(low, shift_y(high, -1))

    def coarse(i, dz, dx, dy):
        if not 0 <= i + dz < planes:
            return None
        if (dz, dx, dy) >= (0, 0, 0):
            return direct(i, dz, dx, dy)
        return shift_y(shift_x(coarse(i + dz, -dz, -dx, -dy), dx), dy)

    coarse = Lazy(coarse)

    resid = Lazy(lambda z, px, py: base(4, z, px, py))
    odd_z = range(planes)
    q_xyz = [inverse(2 * i + 1, 1, 1) * resid(2 * i + 1, 1, 1) for i in odd_z] + [None]
    q_xy, q_xz, q_yz, q_x, q_y, q_z, rhs = [], [], [], [], [], [], []

    def side_x(z, py, value):
        return plus(times(face("x", z, 0, py), value), shift_x(times(face("x", z, 1, py), value), -1))

    def side_y(z, px, value):
        return plus(times(face("y", z, px, 0), value), shift_y(times(face("y", z, px, 1), value), -1))

    def side_z(z, px, py, values):
        i = z // 2
        return plus(times(face("z", z, px, py), values[i]), times(face("z", z - 1, px, py), values[i - 1] if i else None))

    for i in range(planes):
        z = 2 * i
        q_xy.append(inverse(z, 1, 1) * plus(resid(z, 1, 1), side_z(z, 1, 1, q_xyz)))
        q_xz.append(inverse(z + 1, 1, 0) * plus(resid(z + 1, 1, 0), side_y(z + 1, 1, q_xyz[i])))
        q_yz.append(inverse(z + 1, 0, 1) * plus(resid(z + 1, 0, 1), side_x(z + 1, 1, q_xyz[i])))
    for i in range(planes):
        z = 2 * i
        q_x.append(inverse(z, 1, 0) * plus(resid(z, 1, 0), side_y(z, 1, q_xy[i]), side_z(z, 1, 0, q_xz)))
        q_y.append(inverse(z, 0, 1) * plus(resid(z, 0, 1), side_x(z, 1, q_xy[i]), side_z(z, 0, 1, q_yz)))
        q_z.append(
            inverse(z + 1, 0, 0) * plus(resid(z + 1, 0, 0), side_x(z + 1, 0, q_xz[i]), side_y(z + 1, 0, q_yz[i]))
        )
    for i in range(planes):
        z = 2 * i
        rhs.append(plus(resid(z, 0, 0), side_x(z, 0, q_x[i]), side_y(z, 0, q_y[i]), side_z(z, 0, 0, q_z)))

    keep_x, keep_y = stencil_ref.shape[2:]
    for i in range(planes):
        for dz in (-1, 0, 1):
            for dx in (-1, 0, 1):
                for dy in (-1, 0, 1):
                    value = coarse(i, dz, dx, dy)
                    number = 9 * (dz + 1) + 3 * (dx + 1) + dy + 1
                    if value is None:
                        stencil_ref[number, i] = jnp.zeros((keep_x, keep_y), F32)
                    else:
                        for odd in range(2):
                            rows = value[HALO * odd : HALO * odd + keep_x // 2, :keep_y]
                            stencil_ref[number, i, pl.ds(odd, keep_x // 2, stride=2), :] = rows

    stencil_copy = pltpu.make_async_copy(stencil_ref, stencil_hbm, sems.at[0])
    stencil_copy.start()

    scaled = []
    for i in range(planes):
        inside = factor_ref[3, 2 * i, 0, 0] > 0.0
        scaled.append(jnp.where(inside, OMEGA / jnp.where(inside, coarse(i, 0, 0, 0), 1.0), 0.0))
    near_row = {}
    for i in range(planes):
        for dz in range(-i, planes - i):
            for dy in (-1, 0, 1):
                near_row[i, dz, 0, dy] = coarse(i, dz, 0, dy)
                for dx in (-1, 1):
                    near_row[i, dz, dx, dy] = shift_x(coarse(i, dz, dx, dy), -dx)
    u = [scaled[i] * rhs[i] for i in range(planes)]
    for _ in range(SWEEPS - 1):
        moved = {(i, dy): shift_y(u[i], dy) if dy else u[i] for i in range(planes) for dy in (-1, 0, 1)}
        new = []
        for i in range(planes):
            sums = {}
            for dx in (-1, 0, 1):
                sums[dx] = tree_sum(
                    [near_row[i, dz, dx, dy] * moved[i + dz, dy] for dz in range(-i, planes - i) for dy in (-1, 0, 1)]
                )
            kept = u[i] + scaled[i] * (rhs[i] - sums[0])
            new.append(kept - scaled[i] * (shift_x(sums[1], 1) + shift_x(sums[-1], -1)))
        u = new
    for i in range(planes):
        for odd in range(2):
            rows = u[i][HALO * odd : HALO * odd + keep_x // 2, :keep_y]
            solution_ref[i, pl.ds(odd, keep_x // 2, stride=2), :] = rows
    solution_copy = pltpu.make_async_copy(solution_ref, solution_hbm, sems.at[1])
    solution_copy.start()
    stencil_copy.wait()
    solution_copy.wait()


def swap(value, axis, first, wrap):
    count = lax.axis_size(axis)
    partner = list(range(count))
    for i in range(first, count if wrap else count - 1, 2):
        partner[i], partner[(i + 1) % count] = (i + 1) % count, i
    return lax.ppermute(value, axis, list(enumerate(partner)))


def swap_x(value, first, step=2):
    nx, ny = lax.axis_size("gx"), lax.axis_size("gy")
    partner = {}
    for x in range(first, nx - 1, step):
        partner[x], partner[x + 1] = x + 1, x
    pairs = []
    for x in range(nx):
        for y in range(ny):
            target = (partner[x], y) if x in partner else (x, y + 1 if y % 2 == 0 else y - 1)
            pairs.append((x * ny + y, target[0] * ny + target[1]))
    return lax.ppermute(value, ("gx", "gy"), pairs)


def on_chip(value):
    return pltpu.with_memory_space_constraint(value, pltpu.VMEM)


def on_device(base_cond, base_mass, fine_residual, point_index, gen_vector, z_offset):
    plane_count, width_x, width_y = base_mass.shape
    nx_total = width_x * lax.axis_size("gx")
    ny_total = width_y * lax.axis_size("gy")
    vmem = pl.BlockSpec(memory_space=pltpu.VMEM)
    hbm = pl.BlockSpec(memory_space=pl.ANY)
    strip = pltpu.VMEM((2, HALO, LANES), F32)
    groups = field_start(5, plane_count)
    raw, near_y, far_y, gen = pl.pallas_call(
        strips_body,
        out_shape=(pltpu.VMEM((groups, HALO, width_y), F32), strip, strip, pltpu.VMEM((1, gen_vector.size), jnp.int32)),
        in_specs=[hbm] * 4,
        out_specs=(vmem,) * 4,
        scratch_shapes=[pltpu.SemaphoreType.DMA((6,))],
        name="strips",
    )(base_cond, base_mass, fine_residual, gen_vector.reshape(1, -1))
    far_y = swap(far_y, "gy", 1, True)
    near_y = swap(near_y, "gy", 0, False)
    own = pl.pallas_call(
        halves_body,
        out_shape=pltpu.VMEM((groups + 3, HALO, LANES), F32),
        in_specs=[vmem],
        out_specs=vmem,
        name="halves",
    )(on_chip(raw))
    own = lax.dynamic_update_slice(own, far_y[:1], (groups + 1, 0, 0))
    own = lax.dynamic_update_slice(own, near_y[:1], (groups, 0, 0))
    own = lax.dynamic_update_slice(own, far_y[1:] + near_y[1:], (groups + 2, 0, 0))
    smem = pl.BlockSpec(memory_space=pltpu.SMEM)
    factors, wide, pick_strip = pl.pallas_call(
        lambda *refs: local_body(nx_total, ny_total, width_x, width_y, *refs),
        out_shape=(
            pltpu.VMEM((4, plane_count, 2, 2, ROWS, LANES), F32),
            pltpu.VMEM((groups, 2, HALO, LANES), F32),
            pltpu.VMEM((4 * HALO, 2 * LANES), BF16),
        ),
        in_specs=[smem, smem, vmem, vmem],
        out_specs=(vmem,) * 3,
        name="local",
    )(point_index, z_offset, on_chip(gen), on_chip(own))
    far = swap_x(own, 1)
    first = swap_x(own, 0, 4)
    last = swap_x(own, 2, 4)
    coarse_block = (plane_count // 2, width_x // 2, width_y // 2)
    return pl.pallas_call(
        main_body,
        out_shape=(jax.ShapeDtypeStruct((27, *coarse_block), F32), jax.ShapeDtypeStruct(coarse_block, F32)),
        in_specs=[vmem] * 6,
        out_specs=(hbm, hbm),
        scratch_shapes=[
            pltpu.VMEM((groups, 2, 2 * ROWS, LANES), F32),
            pltpu.VMEM((27, *coarse_block), F32),
            pltpu.VMEM(coarse_block, F32),
            pltpu.SemaphoreType.DMA((2,)),
        ],
        name="galerkin",
    )(*[on_chip(value) for value in (factors, pick_strip, wide, last, far, first)])


def solution(mesh):
    return jax.shard_map(
        on_device,
        mesh=mesh,
        in_specs=(
            P(None, None, "gx", "gy"),
            P(None, "gx", "gy"),
            P("parts", "gx", "gy"),
            P("parts"),
            P(),
            P(),
        ),
        out_specs=(P(None, "parts", "gx", "gy"), P("parts", "gx", "gy")),
        check_vma=False,
    )
```

```python
import itertools
import math

import jax
import jax.numpy as jnp
from jax import lax
from jax.experimental import pallas as pl
from jax.experimental.pallas import tpu as pltpu
from jax.sharding import PartitionSpec as P

NZG = 512
QMCN = 1048576
SWEEPS = 4
OMEGA = 0.6
ROWS = 16
LANES = 128
HALO = 8
F32 = jnp.float32
BF16 = jnp.bfloat16


def iota(shape, dim):
    return lax.broadcasted_iota(jnp.int32, shape, dim)


def two_parts(values, axis):
    high = values.astype(BF16)
    return jnp.concatenate([high, (values - high.astype(F32)).astype(BF16)], axis)


def field_start(kind, planes):
    return kind * planes - (1 if kind > 2 else 0)


def strips_body(cond_hbm, mass_hbm, resid_hbm, gen_hbm, own_ref, near_ref, far_ref, gen_ref, sems):
    width = own_ref.shape[-1]
    planes = mass_hbm.shape[0]
    sources = [cond_hbm.at[0], cond_hbm.at[1], cond_hbm.at[2, : planes - 1], mass_hbm, resid_hbm]
    starts = [field_start(kind, planes) for kind in range(6)]
    copies = [
        pltpu.make_async_copy(source, own_ref.at[starts[kind] : starts[kind + 1]], sems.at[kind])
        for kind, source in enumerate(sources)
    ]
    copies.append(pltpu.make_async_copy(gen_hbm, gen_ref, sems.at[len(sources)]))
    for copy in copies:
        copy.start()
    even = lax.axis_index("gy") % 2 == 0
    row, lane = iota((2 * HALO, width), 0), iota((2 * HALO, width), 1)
    column = row % HALO + jnp.where((row < HALO) == even, width - HALO, 0)
    pick = jnp.where(lane == column, 1.0, 0.0).astype(BF16)
    for copy in copies:
        copy.wait()
    rows = own_ref[: starts[5]].reshape(-1, width)
    flip = rows.T
    low, high = flip[:HALO], flip[width - HALO :]
    taken = jnp.concatenate([jnp.where(even, high, low), jnp.where(even, low, high)], 0)
    for out_ref, start in ((near_ref, 0), (far_ref, 1)):
        part = taken[HALO * start : HALO * (start + 1)]
        out_ref[0] = part[:, :LANES]
        rest = jnp.concatenate([part[:, LANES:], jnp.zeros((HALO, 3 * LANES // 2 - part.shape[1]), F32)], 1)
        blank = jnp.zeros_like(rest)
        out_ref[1] = jnp.concatenate([blank, rest] if start else [rest, blank], 1)


def local_body(nx_total, ny_total, width_x, width_y, point_ref, offset_ref, gen_ref, own_ref, out_ref, wide_ref, pick_strip_ref):
    pick_strip_ref[...] = select_strips(width_y)
    groups = wide_ref.shape[0]
    spread = spread_rows([own_ref[...]], groups, pick_strip_ref[...])[0]
    for g in range(groups):
        for py in range(2):
            wide_ref[g, py] = spread[g][py]
    modes = gen_ref.shape[1]
    product = point_ref[0] * gen_ref[...]
    z_first = offset_ref[0]
    x_first = lax.axis_index("gx") * width_x
    y_first = lax.axis_index("gy") * width_y
    half_x, half_y = width_x // 2, width_y // 2
    shift = (product & (QMCN - 1)).astype(F32) / QMCN - 0.5
    mode_row = iota((modes, modes), 0)
    mode_col = jnp.sum(jnp.where(mode_row == iota((modes, modes), 1), shift, 0.0), axis=1, keepdims=True)
    k = iota((modes, LANES), 0)
    lane = iota((modes, LANES), 1)
    k_f = k.astype(F32)
    amplitude = 1.2 / (1.0 + 0.5 * k_f) * mode_col
    z_local = lane // (2 * ROWS)
    px = (lane // ROWS) % 2
    r = lane % ROWS
    place = r % HALO
    coarse_x = 2 * jnp.where(place < 6, place, place - HALO) + r // HALO
    x = x_first + 2 * coarse_x + px
    x_angle = (x.astype(F32) + 0.5) * (math.pi / nx_total)
    z_angle = ((z_local + z_first).astype(F32) + 0.5) * (math.pi / NZG)
    phase = z_angle * (k % 5).astype(F32) + x_angle * (1 + k % 4).astype(F32) + 0.7 * k_f
    x_ok = (place < 4) | (place >= 6)
    ones = jnp.where(x_ok & (x >= 0) & (x < nx_total), 1.0, 0.0)
    left = jnp.concatenate([amplitude * jnp.cos(phase), -amplitude * jnp.sin(phase)], 0)
    inside_x = lax.dot_general(ones, jnp.ones((modes, LANES), F32), (((0,), (0,)), ((), ())), preferred_element_type=F32)
    y_mode = (1 + (k // 4) % 4).astype(F32)
    root = {}
    for py in range(2):
        coarse_y = jnp.where(lane < half_y + 4, lane, lane - LANES)
        y = y_first + 2 * coarse_y + py
        y_angle = (y.astype(F32) + 0.5) * (math.pi / ny_total) * y_mode
        right = jnp.concatenate([jnp.cos(y_angle), jnp.sin(y_angle)], 0)
        log_kappa = lax.dot_general(
            left, right, (((0,), (0,)), ((), ())), precision=lax.Precision.HIGHEST, preferred_element_type=F32
        )
        y_full = y[0:1, :]
        lane_full = lane[0:1, :]
        y_ok = (lane_full < half_y + 4) | (lane_full >= LANES - 4)
        y_ok = y_ok & (y_full >= 0) & (y_full < ny_total)
        value = jnp.where((inside_x > 0.5) & y_ok, jnp.exp(0.5 * log_kappa), 0.0)
        for group in range(8):
            root[group // 2, group % 2, py] = value[group * ROWS : (group + 1) * ROWS]
    planes = out_ref.shape[1]
    for (z, px, py), here in root.items():
        out_ref[0, z, px, py] = here * (shift_x(root[z, 0, py], 1) if px else root[z, 1, py])
        out_ref[1, z, px, py] = here * (shift_y(root[z, px, 0], 1) if py else root[z, px, 1])
        out_ref[2, z, px, py] = here * root[z + 1, px, py] if z + 1 < planes else jnp.zeros((ROWS, LANES), F32)
        out_ref[3, z, px, py] = here * here


def select_strips(width):
    half = width // 2
    strip = iota((4 * HALO, 2 * LANES), 0) % (2 * HALO)
    column = iota((4 * HALO, 2 * LANES), 1)
    parity, k = column // LANES, column % LANES
    k = jnp.where(k >= LANES - 4, k - LANES, k)
    even = lax.axis_index("gy") % 2 == 0
    below = strip % HALO - HALO
    fine = jnp.where((strip < HALO) == even, below + HALO + width, below)
    wanted = ((k < 0) | (k >= half)) & (k < half + 4)
    return jnp.where(wanted & (fine == 2 * k + parity), 1.0, 0.0).astype(BF16)


def halves_body(own_ref, out_ref):
    groups, _, width = own_ref.shape
    row, lane = iota((2 * width, LANES), 0) % width, iota((2 * width, LANES), 1)
    half = width // 2
    pick = jnp.where(row == 2 * (lane % half) + lane // half, 1.0, 0.0).astype(BF16)
    rows = two_parts(own_ref[...].reshape(groups * HALO, width), 1)
    spread = lax.dot_general(rows, pick, (((1,), (0,)), ((), ())), preferred_element_type=F32)
    out_ref[:groups] = spread.reshape(groups, HALO, LANES)


def spread_rows(blocks, groups, pick_strip):
    main, split = LANES // HALO, groups - LANES // HALO
    strips = [jnp.concatenate([block[groups], block[groups + 1]], 0) for block in blocks]
    for block in blocks:
        rest = block[groups + 2]
        strips.append(jnp.concatenate([rest[:, : split * HALO], rest[:, LANES // 2 : LANES // 2 + split * HALO]], 0))
    border = lax.dot_general(
        two_parts(jnp.concatenate(strips, 1), 0), pick_strip, (((0,), (0,)), ((), ())), preferred_element_type=F32
    )
    inner = iota((HALO, LANES), 1) < LANES // 2
    result = []
    for number, block in enumerate(blocks):
        first = [number * LANES + HALO * g for g in range(main)]
        first += [len(blocks) * LANES + number * split * HALO + HALO * g for g in range(split)]
        classes = []
        for g, row in enumerate(first):
            odd = pltpu.roll(block[g], LANES // 2, 1)
            classes.append(
                [
                    jnp.where(inner, values, border[row : row + HALO, LANES * py : LANES * (py + 1)])
                    for py, values in enumerate((block[g], odd))
                ]
            )
        result.append(classes)
    return result


class Lazy:
    def __init__(self, rule):
        self.rule, self.known = rule, {}

    def __call__(self, *key):
        if key not in self.known:
            self.known[key] = self.rule(*key)
        return self.known[key]


def plus(*terms):
    total = None
    for term in terms:
        if term is not None:
            total = term if total is None else total + term
    return total


def times(left, right):
    return None if left is None or right is None else left * right


def minus(left, right):
    if right is None:
        return left
    return -right if left is None else left - right


def tree_sum(terms):
    while len(terms) > 1:
        terms = [terms[k] + terms[k + 1] if k + 1 < len(terms) else terms[k] for k in range(0, len(terms), 2)]
    return terms[0]


def shift_x(value, steps):
    if value is None or steps == 0:
        return value
    even, odd = value[:HALO], value[HALO:]
    if steps > 0:
        return jnp.concatenate([odd, pltpu.roll(even, HALO - 1, 0)], 0)
    return jnp.concatenate([pltpu.roll(odd, 1, 0), even], 0)


def shift_y(value, steps):
    return value if value is None or steps == 0 else pltpu.roll(value, (-steps) % LANES, 1)


def main_body(
    factor_ref,
    pick_strip_ref,
    own_ref,
    last_ref,
    far_ref,
    first_ref,
    stencil_hbm,
    solution_hbm,
    wide_ref,
    stencil_ref,
    solution_ref,
    sems,
):
    groups = own_ref.shape[0]
    for g in range(groups):
        for py in range(2):
            wide_ref[g, py, 0:8, :] = own_ref[g, py]
            wide_ref[g, py, 16:24, :] = jnp.zeros((8, LANES), F32)
    above = lax.axis_index("gx") % 2 == 0
    near_place = pl.multiple_of(jnp.where(above, 8, 24), 8)
    far_place = pl.multiple_of(jnp.where(above, 24, 8), 8)
    near = jnp.where(lax.axis_index("gx") % 4 < 2, first_ref[...], last_ref[...])
    spread = spread_rows([near, far_ref[...]], groups, pick_strip_ref[...])
    for place, rows in zip((near_place, far_place), spread):
        for g in range(groups):
            for py in range(2):
                wide_ref[g, py, pl.ds(place, 8), :] = rows[g][py]

    planes = 2

    def base(kind, z, px, py):
        group = field_start(kind, 2 * planes) + z
        tiles = [wide_ref[group, py, pl.ds(2 * odd + px, HALO, stride=4), :] for odd in range(2)]
        return jnp.concatenate(tiles, 0)

    def face(axis, z, px, py):
        kind = "xyz".index(axis)
        if kind == 2 and not 0 <= z < 2 * planes - 1:
            return None
        return base(kind, z, px, py) * factor_ref[kind, z, px, py]

    face = Lazy(face)
    mass = Lazy(lambda z, px, py: base(3, z, px, py) * factor_ref[3, z, px, py])

    def pair(axis, z, px, py):
        if axis == "x":
            lower = face("x", z, 0, py) if px else shift_x(face("x", z, 1, py), -1)
        elif axis == "y":
            lower = face("y", z, px, 0) if py else shift_y(face("y", z, px, 1), -1)
        else:
            lower = face("z", z - 1, px, py)
        return plus(face(axis, z, px, py), lower)

    pair = Lazy(pair)

    def inverse(z, px, py):
        total = mass(z, px, py)
        for axis, odd in (("x", px), ("y", py), ("z", z % 2)):
            if odd:
                total = total + pair(axis, z, px, py)
        return 1.0 / jnp.where(factor_ref[3, z, px, py] > 0.0, total, 1.0)

    inverse = Lazy(inverse)

    def w_x(i, a):
        return None if not 0 <= i < planes else inverse(2 * i, 1, 0) * face("x", 2 * i, a, 0)

    def w_y(i, b):
        return None if not 0 <= i < planes else inverse(2 * i, 0, 1) * face("y", 2 * i, 0, b)

    def w_z(i, c):
        return times(inverse(2 * i + 1, 0, 0), face("z", 2 * i + c, 0, 0))

    w_x, w_y, w_z = Lazy(w_x), Lazy(w_y), Lazy(w_z)
    w_x_up = Lazy(lambda i, a: shift_y(w_x(i, a), 1))
    w_y_up = Lazy(lambda i, b: shift_x(w_y(i, b), 1))
    w_z_upx = Lazy(lambda i, c: shift_x(w_z(i, c), 1))
    w_z_upy = Lazy(lambda i, c: shift_y(w_z(i, c), 1))

    def w_xy(i, a, b):
        if not 0 <= i < planes:
            return None
        z = 2 * i
        return inverse(z, 1, 1) * (
            face("x", z, a, 1) * (w_y_up(i, b) if a else w_y(i, b)) + face("y", z, 1, b) * (w_x_up(i, a) if b else w_x(i, a))
        )

    def w_xz(i, a, c):
        z = 2 * i + 1
        return times(
            inverse(z, 1, 0),
            plus(times(face("x", z, a, 0), w_z_upx(i, c) if a else w_z(i, c)), times(face("z", 2 * i + c, 1, 0), w_x(i + c, a))),
        )

    def w_yz(i, b, c):
        z = 2 * i + 1
        return times(
            inverse(z, 0, 1),
            plus(times(face("y", z, 0, b), w_z_upy(i, c) if b else w_z(i, c)), times(face("z", 2 * i + c, 0, 1), w_y(i + c, b))),
        )

    w_xy, w_xz, w_yz = Lazy(w_xy), Lazy(w_xz), Lazy(w_yz)
    w_yz_up = Lazy(lambda i, b, c: shift_x(w_yz(i, b, c), 1))
    w_xz_up = Lazy(lambda i, a, c: shift_y(w_xz(i, a, c), 1))

    def w_xyz(i, a, b, c):
        z = 2 * i + 1
        if not 0 <= i < planes or not 0 <= i + c < planes:
            return None
        return inverse(z, 1, 1) * (
            face("x", z, a, 1) * (w_yz_up(i, b, c) if a else w_yz(i, b, c))
            + face("y", z, 1, b) * (w_xz_up(i, a, c) if b else w_xz(i, a, c))
            + face("z", 2 * i + c, 1, 1) * w_xy(i + c, a, b)
        )

    w_xyz = Lazy(w_xyz)

    def weights_of(i, pz, px, py, moved=None):
        plain = {
            (0, 1, 0): lambda c, a, b: w_x(i, a),
            (0, 0, 1): lambda c, a, b: w_y(i, b),
            (1, 0, 0): lambda c, a, b: w_z(i, c),
            (0, 1, 1): lambda c, a, b: w_xy(i, a, b),
            (1, 1, 0): lambda c, a, b: w_xz(i, a, c),
            (1, 0, 1): lambda c, a, b: w_yz(i, b, c),
            (1, 1, 1): lambda c, a, b: w_xyz(i, a, b, c),
        }
        up_x = {
            (0, 0, 1): lambda c, a, b: w_y_up(i, b),
            (1, 0, 0): lambda c, a, b: w_z_upx(i, c),
            (1, 0, 1): lambda c, a, b: w_yz_up(i, b, c),
        }
        up_y = {
            (0, 1, 0): lambda c, a, b: w_x_up(i, a),
            (1, 0, 0): lambda c, a, b: w_z_upy(i, c),
            (1, 1, 0): lambda c, a, b: w_xz_up(i, a, c),
        }
        if (pz, px, py) == (0, 0, 0):
            return {(0, 0, 0): None}
        rule = {"x": up_x, "y": up_y, None: plain}[moved][pz, px, py]
        values = {(c, a, b): rule(c, a, b) for c in range(pz + 1) for a in range(px + 1) for b in range(py + 1)}
        return {sides: value for sides, value in values.items() if value is not None}

    parts = {}

    def keep(i, step, place, value):
        key = (i, *step, *place)
        parts[key] = plus(parts.get(key), value)

    for i in range(planes):
        keep(i, (0, 0, 0), (0, 0), mass(2 * i, 0, 0))
    for i, pz, px, py, axis, side in itertools.product(range(planes), (0, 1), (0, 1), (0, 1), "zxy", (0, 1)):
        parity = {"z": pz, "x": px, "y": py}
        if not parity[axis] or (axis == "z" and i + side >= planes):
            continue
        parity[axis] = 0
        lower = (parity["z"], parity["x"], parity["y"])
        offset = tuple(side if axis == name else 0 for name in "zxy")
        z = 2 * i + pz
        if axis == "z":
            here, joined = weights_of(i + side, *lower), face("z", 2 * i + side, px, py)
        elif axis == "x":
            here, joined = weights_of(i, *lower, "x" if side else None), face("x", z, side, py)
        else:
            here, joined = weights_of(i, *lower, "y" if side else None), face("y", z, px, side)
        there = weights_of(i, pz, px, py)
        drop = {}
        for column, value in there.items():
            own = tuple(at - by for at, by in zip(column, offset))
            drop[column] = -value
            if own in here:
                drop[column] = (1.0 if here[own] is None else here[own]) - value
        for sides, value in here.items():
            row = tuple(at + by for at, by in zip(sides, offset))
            scaled_row = joined if value is None else joined * value
            for column, change in drop.items():
                step = tuple(to - at for to, at in zip(column, row))
                if step >= (0, 0, 0):
                    keep(i + row[0], step, row[1:], scaled_row * change)

    def direct(i, dz, dx, dy):
        low, high = (
            plus(parts.get((i, dz, dx, dy, 0, side)), shift_x(parts.get((i, dz, dx, dy, 1, side)), -1)) for side in (0, 1)
        )
        return plus(low, shift_y(high, -1))

    def coarse(i, dz, dx, dy):
        if not 0 <= i + dz < planes:
            return None
        if (dz, dx, dy) >= (0, 0, 0):
            return direct(i, dz, dx, dy)
        return shift_y(shift_x(coarse(i + dz, -dz, -dx, -dy), dx), dy)

    coarse = Lazy(coarse)

    resid = Lazy(lambda z, px, py: base(4, z, px, py))
    odd_z = range(planes)
    q_xyz = [inverse(2 * i + 1, 1, 1) * resid(2 * i + 1, 1, 1) for i in odd_z] + [None]
    q_xy, q_xz, q_yz, q_x, q_y, q_z, rhs = [], [], [], [], [], [], []

    def side_x(z, py, value):
        return plus(times(face("x", z, 0, py), value), shift_x(times(face("x", z, 1, py), value), -1))

    def side_y(z, px, value):
        return plus(times(face("y", z, px, 0), value), shift_y(times(face("y", z, px, 1), value), -1))

    def side_z(z, px, py, values):
        i = z // 2
        return plus(times(face("z", z, px, py), values[i]), times(face("z", z - 1, px, py), values[i - 1] if i else None))

    for i in range(planes):
        z = 2 * i
        q_xy.append(inverse(z, 1, 1) * plus(resid(z, 1, 1), side_z(z, 1, 1, q_xyz)))
        q_xz.append(inverse(z + 1, 1, 0) * plus(resid(z + 1, 1, 0), side_y(z + 1, 1, q_xyz[i])))
        q_yz.append(inverse(z + 1, 0, 1) * plus(resid(z + 1, 0, 1), side_x(z + 1, 1, q_xyz[i])))
    for i in range(planes):
        z = 2 * i
        q_x.append(inverse(z, 1, 0) * plus(resid(z, 1, 0), side_y(z, 1, q_xy[i]), side_z(z, 1, 0, q_xz)))
        q_y.append(inverse(z, 0, 1) * plus(resid(z, 0, 1), side_x(z, 1, q_xy[i]), side_z(z, 0, 1, q_yz)))
        q_z.append(
            inverse(z + 1, 0, 0) * plus(resid(z + 1, 0, 0), side_x(z + 1, 0, q_xz[i]), side_y(z + 1, 0, q_yz[i]))
        )
    for i in range(planes):
        z = 2 * i
        rhs.append(plus(resid(z, 0, 0), side_x(z, 0, q_x[i]), side_y(z, 0, q_y[i]), side_z(z, 0, 0, q_z)))

    keep_x, keep_y = stencil_ref.shape[2:]
    for i in range(planes):
        for dz in (-1, 0, 1):
            for dx in (-1, 0, 1):
                for dy in (-1, 0, 1):
                    value = coarse(i, dz, dx, dy)
                    number = 9 * (dz + 1) + 3 * (dx + 1) + dy + 1
                    if value is None:
                        stencil_ref[number, i] = jnp.zeros((keep_x, keep_y), F32)
                    else:
                        for odd in range(2):
                            rows = value[HALO * odd : HALO * odd + keep_x // 2, :keep_y]
                            stencil_ref[number, i, pl.ds(odd, keep_x // 2, stride=2), :] = rows

    scaled = []
    for i in range(planes):
        inside = factor_ref[3, 2 * i, 0, 0] > 0.0
        scaled.append(jnp.where(inside, OMEGA / jnp.where(inside, coarse(i, 0, 0, 0), 1.0), 0.0))
    near_row = {}
    for i in range(planes):
        for dz in range(-i, planes - i):
            for dy in (-1, 0, 1):
                near_row[i, dz, 0, dy] = coarse(i, dz, 0, dy)
                for dx in (-1, 1):
                    near_row[i, dz, dx, dy] = shift_x(coarse(i, dz, dx, dy), -dx)
    u = [scaled[i] * rhs[i] for i in range(planes)]
    for _ in range(SWEEPS - 1):
        moved = {(i, dy): shift_y(u[i], dy) if dy else u[i] for i in range(planes) for dy in (-1, 0, 1)}
        new = []
        for i in range(planes):
            sums = {}
            for dx in (-1, 0, 1):
                sums[dx] = tree_sum(
                    [near_row[i, dz, dx, dy] * moved[i + dz, dy] for dz in range(-i, planes - i) for dy in (-1, 0, 1)]
                )
            total = sums[0] + (shift_x(sums[1], 1) + shift_x(sums[-1], -1))
            new.append(u[i] + scaled[i] * (rhs[i] - total))
        u = new
    for i in range(planes):
        for odd in range(2):
            rows = u[i][HALO * odd : HALO * odd + keep_x // 2, :keep_y]
            solution_ref[i, pl.ds(odd, keep_x // 2, stride=2), :] = rows
    stencil_copy = pltpu.make_async_copy(stencil_ref, stencil_hbm, sems.at[0])
    stencil_copy.start()
    solution_copy = pltpu.make_async_copy(solution_ref, solution_hbm, sems.at[1])
    solution_copy.start()
    stencil_copy.wait()
    solution_copy.wait()


def swap(value, axis, first, wrap):
    count = lax.axis_size(axis)
    partner = list(range(count))
    for i in range(first, count if wrap else count - 1, 2):
        partner[i], partner[(i + 1) % count] = (i + 1) % count, i
    return lax.ppermute(value, axis, list(enumerate(partner)))


def swap_x(value, first, step=2):
    nx, ny = lax.axis_size("gx"), lax.axis_size("gy")
    partner = {}
    for x in range(first, nx - 1, step):
        partner[x], partner[x + 1] = x + 1, x
    pairs = []
    for x in range(nx):
        for y in range(ny):
            target = (partner[x], y) if x in partner else (x, y + 1 if y % 2 == 0 else y - 1)
            pairs.append((x * ny + y, target[0] * ny + target[1]))
    return lax.ppermute(value, ("gx", "gy"), pairs)


def on_chip(value):
    return pltpu.with_memory_space_constraint(value, pltpu.VMEM)


def on_device(base_cond, base_mass, fine_residual, point_index, gen_vector, z_offset):
    plane_count, width_x, width_y = base_mass.shape
    nx_total = width_x * lax.axis_size("gx")
    ny_total = width_y * lax.axis_size("gy")
    vmem = pl.BlockSpec(memory_space=pltpu.VMEM)
    hbm = pl.BlockSpec(memory_space=pl.ANY)
    strip = pltpu.VMEM((2, HALO, LANES), F32)
    groups = field_start(5, plane_count)
    raw, near_y, far_y, gen = pl.pallas_call(
        strips_body,
        out_shape=(pltpu.VMEM((groups, HALO, width_y), F32), strip, strip, pltpu.VMEM((1, gen_vector.size), jnp.int32)),
        in_specs=[hbm] * 4,
        out_specs=(vmem,) * 4,
        scratch_shapes=[pltpu.SemaphoreType.DMA((6,))],
        name="strips",
    )(base_cond, base_mass, fine_residual, gen_vector.reshape(1, -1))
    far_y = swap(far_y, "gy", 1, True)
    near_y = swap(near_y, "gy", 0, False)
    own = pl.pallas_call(
        halves_body,
        out_shape=pltpu.VMEM((groups + 3, HALO, LANES), F32),
        in_specs=[vmem],
        out_specs=vmem,
        name="halves",
    )(on_chip(raw))
    own = lax.dynamic_update_slice(own, far_y[:1], (groups + 1, 0, 0))
    own = lax.dynamic_update_slice(own, near_y[:1], (groups, 0, 0))
    own = lax.dynamic_update_slice(own, far_y[1:] + near_y[1:], (groups + 2, 0, 0))
    smem = pl.BlockSpec(memory_space=pltpu.SMEM)
    factors, wide, pick_strip = pl.pallas_call(
        lambda *refs: local_body(nx_total, ny_total, width_x, width_y, *refs),
        out_shape=(
            pltpu.VMEM((4, plane_count, 2, 2, ROWS, LANES), F32),
            pltpu.VMEM((groups, 2, HALO, LANES), F32),
            pltpu.VMEM((4 * HALO, 2 * LANES), BF16),
        ),
        in_specs=[smem, smem, vmem, vmem],
        out_specs=(vmem,) * 3,
        name="local",
    )(point_index, z_offset, on_chip(gen), on_chip(own))
    far = swap_x(own, 1)
    first = swap_x(own, 0, 4)
    last = swap_x(own, 2, 4)
    coarse_block = (plane_count // 2, width_x // 2, width_y // 2)
    return pl.pallas_call(
        main_body,
        out_shape=(jax.ShapeDtypeStruct((27, *coarse_block), F32), jax.ShapeDtypeStruct(coarse_block, F32)),
        in_specs=[vmem] * 6,
        out_specs=(hbm, hbm),
        scratch_shapes=[
            pltpu.VMEM((groups, 2, 2 * ROWS, LANES), F32),
            pltpu.VMEM((27, *coarse_block), F32),
            pltpu.VMEM(coarse_block, F32),
            pltpu.SemaphoreType.DMA((2,)),
        ],
        name="galerkin",
    )(*[on_chip(value) for value in (factors, pick_strip, wide, last, far, first)])


def solution(mesh):
    return jax.shard_map(
        on_device,
        mesh=mesh,
        in_specs=(
            P(None, None, "gx", "gy"),
            P(None, "gx", "gy"),
            P("parts", "gx", "gy"),
            P("parts"),
            P(),
            P(),
        ),
        out_specs=(P(None, "parts", "gx", "gy"), P("parts", "gx", "gy")),
        check_vma=False,
    )
```
